32 devices in a mesh: seq: 8 (over y, x, core), exp: 4 (over z).
Axes of the slice: x: 2, y: 2, z: 4, core: 2. Of those that a mesh axis runs over, the one named last changes fastest.
Arguments:
- layer_input: bfloat16 [4, 4096, 768], P('exp', 'seq'), may hold values from -6 to 6
- token_ids: int32 [4, 4096], P('exp', 'seq'), may hold values from 0 to 8007, as said below
- segment_ids: int32 [4, 4096], P('exp'), may hold values from 0 to 7, never falling along the last dimension, each value on 1 to 1024 neighbouring positions
- hash_table: int32 [8008], replicated, may hold values from 0 to 3, as said below
- first_gain: float32 [768], replicated, may hold values from 0.25 to 1.75
- first_bias: float32 [768], replicated, may hold values from -1.5 to 1.5
- second_gain: float32 [768], replicated, may hold values from 0.25 to 1.75
- second_bias: float32 [768], replicated, may hold values from -1.5 to 1.5
- w_qkv: bfloat16 [768, 2304], replicated, may hold values from -0.21875 to 0.21875
- w_out: bfloat16 [768, 768], replicated, may hold values from -3 to 3
- w_up: bfloat16 [4, 768, 3072], P('exp'), may hold values from -0.21875 to 0.21875
- w_down: bfloat16 [4, 3072, 768], P('exp'), may hold values from -0.109375 to 0.109375
- cotangent: bfloat16 [4, 4096, 768], P('exp', 'seq'), may hold values from -6 to 6
Outputs:
- layer_output: bfloat16 [4, 4096, 768], P('exp', 'seq')
- grad_input: float32 [4, 4096, 768], P('exp', 'seq')
- grad_w_qkv: float32 [768, 2304], replicated
- grad_w_out: float32 [768, 768], replicated
- grad_first_gain: float32 [768], replicated
- grad_first_bias: float32 [768], replicated
- grad_second_gain: float32 [768], replicated
- grad_second_bias: float32 [768], replicated
- grad_w_up: float32 [4, 768, 3072], P('exp')
- grad_w_down: float32 [4, 3072, 768], P('exp')
The draws below stay inside these ranges and needn't reach their ends.
Inputs may be any that keep to these rules, and one draw needn't show every extreme that they name: `token_ids`: token ids range over the vocabulary. Among the 512 positions that one device holds, hash_table sends exactly 256 to one expert, the same expert on all devices that hold the same positions of their sequences, and the other experts' counts differ from one another by at most one. `hash_table`: every expert is named by 2002 token ids. `segment_ids`: numbers never fall along a sequence; each document holds 1 to 1024 neighbouring positions, and one in every sequence holds exactly 1024.
All inputs are finite; a program needn't handle non-finite values.
Results may differ from the reference program's by a relative error of at most 0.017.
Values may be sent and summed in bfloat16 or wider, within the bound.
No kernel may reach another device: no remote copies, remote signals or barrier semaphores. Data moves between devices by JAX's collectives and lax.ppermute only.
A program may use at most 192 MiB of HBM per device.

```python
import math
import jax
import jax.numpy as jnp
import numpy as np
from jax import lax

D = 768
HEADS = 12
HEAD_DIM = 64
FF = 3072
VOCAB = 8008
LOCAL_LEN = 512
DOC_MOST = 1024
EXPERTS = 4
SEQ_LEN = 4096
SEQS = 4
CAP = 256


def shuffled_vocab(key):
    return jax.random.permutation(jax.random.fold_in(key, 101), VOCAB).astype(jnp.int32)


def draw_hash_table(key, part):
    return (shuffled_vocab(key) % EXPERTS).astype(jnp.int32)


def draw_token_ids(key, part):
    shuffled = shuffled_vocab(key)
    inverse = jnp.argsort(shuffled, stable=True).astype(jnp.int32)
    groups = SEQ_LEN // LOCAL_LEN
    favored = jax.random.randint(jax.random.fold_in(key, 202), (groups,), 0, EXPERTS).astype(jnp.int32)
    slots = jnp.arange(LOCAL_LEN, dtype=jnp.int32)
    rest = jnp.maximum(slots - CAP, 0) % (EXPERTS - 1)

    def one_block(index):
        hot = favored[index % groups]
        plan = jnp.where(slots < CAP, hot, (hot + 1 + rest) % EXPERTS)
        block_key = jax.random.fold_in(jax.random.fold_in(key, 303), index)
        placed = plan[jax.random.permutation(jax.random.fold_in(block_key, 1), LOCAL_LEN)]
        bucket = jax.random.randint(jax.random.fold_in(block_key, 2), (LOCAL_LEN,), 0, VOCAB // EXPERTS).astype(jnp.int32)
        return inverse[placed + EXPERTS * bucket]
    blocks = jax.vmap(one_block)(jnp.arange(SEQS * groups, dtype=jnp.int32))
    return blocks.reshape(SEQS, SEQ_LEN).astype(jnp.int32)


def block_scale(stream_key, dims, split, smallest, high):
    gain, own = 1.0, jax.random.fold_in(stream_key, 6)
    for axis_at, parts in split:
        draws = jnp.exp(jax.random.uniform(jax.random.fold_in(own, axis_at), (parts,), jnp.float32, smallest / len(split), high / len(split)))
        gain = gain * jnp.repeat(draws, dims[axis_at] // parts).reshape([-1 if axis == axis_at else 1 for axis in range(len(dims))])
    return gain


def split_up(amount, total, most, lean):
    loads = [(1 << 20) // math.isqrt(rank ** lean) + 1 for rank in range(2, amount + 1)]
    surplus, given = total - most - (amount - 1), [1] * (amount - 1)
    while surplus > 0:
        free = [i for i in range(amount - 1) if given[i] < most]
        whole, remaining = sum([loads[i] for i in free]), surplus
        for i in free:
            addition = min(most - given[i], max(1, remaining * loads[i] // whole), surplus)
            given[i] = given[i] + addition
            surplus = surplus - addition
    return np.array([most] + given)


def ragged_sizes(key, number_of, total, most, slope):
    if number_of == 2:
        one = jax.random.randint(key, (), max(1, total - most), min(most, total - 1) + 1)
        return jnp.stack([one, total - one])
    sizes = jnp.asarray(split_up(number_of, total, most, slope), jnp.int32)
    twos = (number_of - 1) // 2
    source_of, sink = sizes[1:1 + 2 * twos:2], sizes[2:2 + 2 * twos:2]
    room = jnp.minimum(source_of - 1, most - sink)
    passed = jax.random.randint(jax.random.fold_in(key, 1), (twos,), 0, 1 << 20) % (room + 1)
    sizes = sizes.at[1:1 + 2 * twos:2].set(source_of - passed).at[2:2 + 2 * twos:2].set(sink + passed)
    return sizes[jax.random.permutation(jax.random.fold_in(key, 2), number_of)]


def noise(key, extent, width, reach, cuts=(), kind=jnp.bfloat16):
    factor_of = block_scale(key, extent, cuts, -0.22, 0.18) if cuts else 1.0
    values = jax.random.normal(key, extent, jnp.float32) * width * factor_of
    return jnp.minimum(jnp.maximum(values, -reach), reach).astype(kind)


def setup_inputs(seed: int = 0) -> dict:
    arg_keys = jax.random.split(jax.random.key(seed), 14)
    return {
        "layer_input": noise(arg_keys[0], (SEQS, SEQ_LEN, D), 1.0, 6.0, ((0, 4), (1, 8))),
        "token_ids": draw_token_ids(jax.random.fold_in(arg_keys[13], 71), 0),
        "segment_ids": jax.vmap(lambda own: jnp.searchsorted(jnp.cumsum(ragged_sizes(own, 2 * SEQ_LEN // DOC_MOST, SEQ_LEN, DOC_MOST, 0)), jnp.arange(SEQ_LEN), side="right"))(jax.random.split(arg_keys[2], SEQS)).reshape((SEQS, SEQ_LEN)).astype(jnp.int32),
        "hash_table": draw_hash_table(jax.random.fold_in(arg_keys[13], 71), 0),
        "first_gain": jnp.clip(1.0 + 0.15 * jax.random.normal(arg_keys[4], (D,), jnp.float32), 0.25, 1.75),
        "first_bias": noise(arg_keys[5], (D,), 0.3, 1.5, (), jnp.float32),
        "second_gain": jnp.clip(1.0 + 0.15 * jax.random.normal(arg_keys[6], (D,), jnp.float32), 0.25, 1.75),
        "second_bias": noise(arg_keys[7], (D,), 0.3, 1.5, (), jnp.float32),
        "w_qkv": noise(arg_keys[8], (D, 3 * D), D ** -0.5, 0.21875),
        "w_out": noise(arg_keys[9], (D, D), (5 * DOC_MOST ** 0.5 / D), 3.0),
        "w_up": noise(arg_keys[10], (EXPERTS, D, FF), D ** -0.5, 0.21875, ((0, 4),)),
        "w_down": noise(arg_keys[11], (EXPERTS, FF, D), FF ** -0.5, 0.109375, ((0, 4),)),
        "cotangent": noise(arg_keys[12], (SEQS, SEQ_LEN, D), 1.0, 6.0, ((0, 4), (1, 8))),
    }


@jax.custom_vjp
def low(v):
    return lax.optimization_barrier(v.astype(jnp.bfloat16)).astype(jnp.float32)

@jax.custom_vjp
def low_back(v):
    return v

def low_keep(v):
    return (low(v), None)

def low_pass(kept, grad):
    return (grad,)

def back_keep(v):
    return (v, None)

def back_low(kept, grad):
    return (low(grad),)
low.defvjp(low_keep, low_pass)
low_back.defvjp(back_keep, back_low)
EPSILON = 1e-05
NEG_BIG = -1e+30
HIGH = lax.Precision.HIGHEST

def smooth_gate(values):
    return jax.nn.gelu(values, approximate=True)

def norm_rows(values):
    center = values - lax.optimization_barrier(jnp.mean(values, axis=-1, keepdims=True))
    return center * lax.rsqrt(lax.optimization_barrier(jnp.mean(center * center, axis=-1, keepdims=True)) + EPSILON)

def attention(projected, segment_row):
    queries = projected[:, :D].reshape(SEQ_LEN, HEADS, HEAD_DIM)
    key_rows = projected[:, D:2 * D].reshape(SEQ_LEN, HEADS, HEAD_DIM)
    value_rows = projected[:, 2 * D:].reshape(SEQ_LEN, HEADS, HEAD_DIM)
    positions = jnp.arange(SEQ_LEN, dtype=jnp.int32)
    block = min(512, SEQ_LEN)
    scale = HEAD_DIM ** (-0.5)

    def one_block(index):
        first = (index * block).astype(jnp.int32)
        rows = lax.dynamic_slice_in_dim(queries, first, block, 0)
        query_pos = first + jnp.arange(block, dtype=jnp.int32)
        query_seg = lax.dynamic_slice_in_dim(segment_row, first, block, 0)
        allowed = (positions[None, :] <= query_pos[:, None]) & (segment_row[None, :] == query_seg[:, None])
        scores = low_back(jnp.einsum('qhd,khd->hqk', rows, key_rows, precision=HIGH) * scale)
        masked = jnp.where(allowed[None], scores, NEG_BIG)
        top = lax.optimization_barrier(jnp.max(masked, axis=-1, keepdims=True))
        shares = jnp.exp(masked - top)
        soft = shares / lax.optimization_barrier(jnp.sum(shares, axis=-1, keepdims=True))
        weights = low(soft)
        return jnp.einsum('hqk,khd->qhd', weights, value_rows, precision=HIGH).reshape(block, D)
    blocks = lax.map(jax.checkpoint(one_block), jnp.arange(SEQ_LEN // block, dtype=jnp.int32))
    return blocks.reshape(SEQ_LEN, D)

def expert_part(rows, choice_ids, w_up, w_down):
    order = jnp.argsort(choice_ids, stable=True).astype(jnp.int32)
    places = jnp.argsort(order, stable=True).astype(jnp.int32)
    grid = jnp.arange(EXPERTS, dtype=jnp.int32)
    counts = lax.optimization_barrier(jnp.sum((choice_ids[None, :] == grid[:, None]).astype(jnp.int32), axis=1)).astype(jnp.int32)
    starts = (jnp.cumsum(counts) - counts).astype(jnp.int32)
    slots = jnp.arange(CAP, dtype=jnp.int32)
    index = order[jnp.minimum(starts[:, None] + slots[None, :], LOCAL_LEN - 1)]
    filled = slots[None, :] < counts[:, None]
    gathered = jnp.where(filled[:, :, None], rows[index], 0.0)
    pre_act = low_back(jnp.einsum('ecd,edf->ecf', gathered, w_up, precision=HIGH))
    hidden = low(smooth_gate(pre_act))
    result = low_back(low(jnp.einsum('ecf,efd->ecd', hidden, w_down, precision=HIGH)))
    token_slot = (choice_ids * CAP + places - starts[choice_ids]).astype(jnp.int32)
    return result.reshape(EXPERTS * CAP, D)[token_slot]

def layer_sequence(inputs, segment_row, choice_ids, first_gain, first_bias, second_gain, second_bias, w_qkv, w_out, w_up, w_down):
    attn_in = low(norm_rows(inputs) * first_gain + first_bias)
    projected = low_back(low(jnp.dot(attn_in, w_qkv, precision=HIGH)))
    attn_rows = low_back(low(attention(projected, segment_row)))
    resid = inputs + low_back(jnp.dot(attn_rows, w_out, precision=HIGH))
    ffn_in = low_back(low(norm_rows(resid) * second_gain + second_bias))
    groups = SEQ_LEN // LOCAL_LEN
    ffn_rows = jax.vmap(expert_part, in_axes=(0, 0, None, None))(ffn_in.reshape(groups, LOCAL_LEN, D), choice_ids.reshape(groups, LOCAL_LEN), w_up, w_down)
    return resid + ffn_rows.reshape(SEQ_LEN, D)

def reference(layer_input, token_ids, segment_ids, hash_table, first_gain, first_bias, second_gain, second_bias, w_qkv, w_out, w_up, w_down, cotangent):
    choice_ids = hash_table[token_ids].astype(jnp.int32)
    params = tuple((item.astype(jnp.float32) for item in (first_gain, first_bias, second_gain, second_bias, w_qkv, w_out, w_up, w_down)))
    inputs = layer_input.astype(jnp.float32)

    def whole(inputs, *weights):

        def one(state, items):
            row_in, seg_row, id_row = items
            return (state, layer_sequence(row_in, seg_row, id_row, *weights))
        unused, outputs = lax.scan(one, jnp.zeros((), jnp.float32), (inputs, segment_ids, choice_ids))
        return outputs
    result, pullback = jax.vjp(whole, inputs, *params)
    grads = pullback(cotangent.astype(jnp.float32))
    return (result.astype(jnp.bfloat16), grads[0], grads[5], grads[6], grads[1], grads[2], grads[3], grads[4], grads[7], grads[8])
```

```python
import functools
import math

import jax
import jax.numpy as jnp
from jax import lax
from jax.experimental import pallas as pl
from jax.experimental.pallas import tpu as pltpu
from jax.sharding import PartitionSpec as P

HEADS = 12
HEAD_DIM = 64
DOC_MOST = 1024
EPSILON = 1e-05
LOW = -1e30
LOWER = -2e30
LANES = 128
TILE = 256
F32 = jnp.float32
BF16 = jnp.bfloat16
MIB = 1 << 20
COST = 1


def dot(a, b):
    return lax.dot_general(a, b, (((1,), (0,)), ((), ())), preferred_element_type=F32)


def dot_nt(a, b):
    return lax.dot_general(a, b, (((1,), (1,)), ((), ())), preferred_element_type=F32)


def dot_tn(a, b):
    return lax.dot_general(a, b, (((0,), (0,)), ((), ())), preferred_element_type=F32)


def iota(shape, axis):
    return lax.broadcasted_iota(jnp.int32, shape, axis)


def one_hot(ids, width):
    return jnp.where(iota((ids.shape[0], width), 1) == ids, 1.0, 0.0).astype(BF16)


def norm_rows(values):
    center = values - jnp.mean(values, axis=-1, keepdims=True)
    scale = lax.rsqrt(jnp.mean(center * center, axis=-1, keepdims=True) + EPSILON)
    return center * scale, scale


def norm_back(grad, normed, scale):
    inner = jnp.mean(grad * normed, axis=-1, keepdims=True)
    return scale * (grad - jnp.mean(grad, axis=-1, keepdims=True) - normed * inner)


def after(value, *others):
    return lax.optimization_barrier((value, others))[0]


def shape(dims, dtype):
    return jax.ShapeDtypeStruct(dims, dtype)


def call(body, name, out_shape, args, *, grid=(), in_specs=None, out_specs=None, scratch=(),
         scalars=0, aliases=None, flops=0, nbytes=0, special=0, vmem=56):
    outs = out_shape if isinstance(out_shape, (tuple, list)) else [out_shape]
    whole = pl.BlockSpec(memory_space=pltpu.VMEM)
    if in_specs is None:
        in_specs = [whole] * (len(args) - scalars)
    if out_specs is None:
        out_specs = [whole] * len(outs)
        if not isinstance(out_shape, (tuple, list)):
            out_specs = out_specs[0]
    return pl.pallas_call(
        body,
        name=name,
        out_shape=out_shape,
        grid_spec=pltpu.PrefetchScalarGridSpec(
            num_scalar_prefetch=scalars,
            grid=grid,
            in_specs=in_specs,
            out_specs=out_specs,
            scratch_shapes=scratch,
        ),
        input_output_aliases=aliases or {},
        cost_estimate=pl.CostEstimate(flops=COST, bytes_accessed=COST, transcendentals=0),
        compiler_params=pltpu.CompilerParams(vmem_limit_bytes=vmem * MIB),
    )(*args)


def route_body(parts, capacity, place_ref, ids_ref, table_ref, rows_ref, slot_ref, *out_refs):
    ids = ids_ref[...]
    count = ids.shape[0]
    lines = table_ref.shape[0]
    picked = dot(one_hot(ids >> 7, lines), table_ref[...])
    lane = iota((count, LANES), 1)
    choice = jnp.sum(
        jnp.where(lane == (ids & (LANES - 1)), picked, 0.0), axis=1, keepdims=True
    ).astype(jnp.int32)
    mine = lane == choice
    below = jnp.where(iota((count, count), 0) > iota((count, count), 1), 1.0, 0.0).astype(BF16)
    ranks = dot(below, jnp.where(mine, 1.0, 0.0).astype(BF16))
    rank = jnp.sum(jnp.where(mine, ranks, 0.0), axis=1, keepdims=True).astype(jnp.int32)
    slot = (choice ^ place_ref[0]) * capacity + rank
    slot_ref[...] = slot
    rows = rows_ref[...]
    for k in range(parts):
        chosen = one_hot(slot - k * capacity, capacity)
        out_refs[k][...] = dot_tn(chosen, rows).astype(BF16)


def route(place, ids, table, rows, parts, capacity):
    count, width = rows.shape
    outs = [shape((count, 1), jnp.int32)] + [shape((capacity, width), BF16)] * parts
    return call(
        functools.partial(route_body, parts, capacity), "route", outs, (place, ids, table, rows),
        scalars=1, flops=2 * count * parts * capacity * width + 2 * count * count * LANES,
    )


def project_body(skip, core_ref, own_ref, sib_ref, gain_ref, bias_ref, wq_ref, wk_ref, wv_ref, *refs):
    outs = refs[skip:]
    step = pl.program_id(0)

    def work(rows):
        normed, unused = norm_rows(rows.astype(F32))
        a = (normed * gain_ref[...] + bias_ref[...]).astype(BF16)
        outs[0][...] = a
        outs[1][...] = dot(a, wk_ref[...]).astype(BF16)
        outs[2][...] = dot(a, wv_ref[...]).astype(BF16)
        if not skip:
            outs[3][...] = dot(a, wq_ref[...]).astype(BF16)

    half = pl.num_programs(0) // 2
    work(jnp.where(step < half, own_ref[...], sib_ref[...]))


def project(core, own, sib, gain, bias, w_qkv, made):
    count, width = own.shape
    mine = width // 2
    half = count // TILE
    base = 0 if made else 2 * half

    def place(i, c):
        return base + ((i // half) ^ c[0]) * half + i % half

    row = pl.BlockSpec((1, width), lambda i, c: (0, 0))
    in_specs = [
        pl.BlockSpec((TILE, width), lambda i, c: (jnp.minimum(i, half - 1), 0)),
        pl.BlockSpec((TILE, width), lambda i, c: (jnp.maximum(i - half, 0), 0)),
        row,
        row,
    ] + [
        pl.BlockSpec((width, mine), functools.partial(lambda t, i, c: (0, 2 * t + c[0]), t))
        for t in range(3)
    ]
    args = [core, own, sib, gain, bias, w_qkv, w_qkv, w_qkv]
    outs = [shape((4 * count, width), BF16)] + [shape((4 * count, mine), BF16)] * 2
    out_specs = [
        pl.BlockSpec((TILE, width), lambda i, c: (place(i, c), 0)),
        pl.BlockSpec((TILE, mine), lambda i, c: (place(i, c), 0)),
        pl.BlockSpec((TILE, mine), lambda i, c: (place(i, c), 0)),
    ]
    aliases = {}
    if made:
        in_specs += [pl.BlockSpec(memory_space=pl.ANY)] * 3
        aliases = {8: 0, 9: 1, 10: 2}
        args += list(made)
    else:
        outs.append(shape((2 * count, mine), BF16))
        out_specs.append(
            pl.BlockSpec((TILE, mine), lambda i, c: (((i // half) ^ c[0]) * half + i % half, 0))
        )
    return call(
        functools.partial(project_body, 3 if made else 0), "project", outs, args,
        grid=(2 * half,), in_specs=in_specs, out_specs=out_specs, scalars=1, aliases=aliases,
        flops=2 * 2 * count * width * mine * (2 if made else 3),
        nbytes=2 * (2 * count * width * 2 + 3 * width * mine + 6 * count * mine),
    )


def masked_heads(block):
    lane = iota(block.shape, 1)
    zero = jnp.zeros((), block.dtype)
    return [
        jnp.where(lane < HEAD_DIM, block, zero),
        jnp.where(lane < HEAD_DIM, zero, block),
    ]


def flip(block):
    return block.astype(F32).T.astype(block.dtype)


def lanes_of(group):
    return slice(group * LANES, (group + 1) * LANES)


def put_heads(ref, block):
    for g in range(block.shape[1] // LANES):
        for h, part in enumerate(masked_heads(block[:, lanes_of(g)])):
            ref[2 * g + h] = part


def tile_mask(begin, low, high):
    place = begin + iota((TILE, TILE), 0)
    return (place >= low) & (place <= high)


def attend_body(meta_ref, q_ref, k_ref, v_ref, lo_ref, own_ref, sib_ref, all_ref, tall_ref,
                log_ref, vt_ref, heads_ref, acc_ref, rows_ref):
    total, mine = q_ref.shape
    half = total // 2
    heads = mine // HEAD_DIM
    vt_ref[...] = flip(v_ref[...])
    put_heads(heads_ref, q_ref[...] * jnp.asarray(HEAD_DIM**-0.5, BF16))
    core = meta_ref[0]
    log_ref[...] = jnp.zeros_like(log_ref)

    def tile(t, unused):
        at = pl.multiple_of(t * TILE, TILE)
        here = pl.ds(at, TILE)
        low = lo_ref[:, here]
        high = total + at + iota((1, TILE), 1)
        acc_ref[...] = jnp.zeros_like(acc_ref)

        def step(j, state):
            begin = pl.multiple_of(j * TILE, TILE)
            allowed = tile_mask(begin, low, high)
            after = []
            for h in range(heads):
                top, total_h = state[2 * h : 2 * h + 2]
                span = slice(h * HEAD_DIM, (h + 1) * HEAD_DIM)
                keys = k_ref[pl.ds(begin, TILE), lanes_of(h // 2)]
                scores = jnp.where(allowed, dot_nt(keys, heads_ref[h, here, :]), LOWER)
                new_top = jnp.maximum(top, jnp.max(scores, axis=0, keepdims=True))
                shares = jnp.exp(scores - new_top)
                factor = jnp.exp(top - new_top)
                total_h = total_h * factor + jnp.sum(shares, axis=0, keepdims=True)
                values = vt_ref[span, pl.ds(begin, TILE)]
                acc_ref[span, :] = acc_ref[span, :] * factor + dot(values, shares.astype(BF16))
                after += [new_top, total_h]
            return tuple(after)

        first = (jnp.full((1, TILE), LOW, F32), jnp.zeros((1, TILE), F32))
        state = lax.fori_loop(meta_ref[1 + t], total // TILE + t + 1, step, first * heads)
        for h in range(heads):
            top, total_h = state[2 * h : 2 * h + 2]
            span = slice(h * HEAD_DIM, (h + 1) * HEAD_DIM)
            out = acc_ref[span, :] / total_h
            acc_ref[span, :] = out
            tall_ref[span, here] = out
            log_ref[h : h + 1, here] = top + jnp.log(total_h)
        rows_ref[here, :] = acc_ref[...].T
        return unused

    lax.fori_loop(0, total // TILE, tile, 0)
    all_ref[...] = rows_ref[...].astype(BF16)
    own_at = pl.multiple_of(core * half, half)
    sib_at = pl.multiple_of((1 - core) * half, half)
    own_ref[...] = rows_ref[pl.ds(own_at, half), :].astype(BF16)
    sib_ref[...] = rows_ref[pl.ds(sib_at, half), :].astype(BF16)


def attend(meta, q, k, v, low):
    total, mine = q.shape
    heads = mine // HEAD_DIM
    outs = [
        shape((total // 2, mine), BF16),
        shape((total // 2, mine), BF16),
        shape((total, mine), BF16),
        shape((mine, total), F32),
        shape((-(-heads // 8) * 8, total), F32),
    ]
    return call(
        attend_body, "attend", outs, (meta, q, k, v, low), scalars=1,
        scratch=[pltpu.VMEM((mine, 2 * total), BF16), pltpu.VMEM((heads, total, LANES), BF16),
                 pltpu.VMEM((mine, TILE), F32), pltpu.VMEM((total, mine), F32)],
    )


def attend_back_body(sizes, meta_ref, q_ref, k_ref, v_ref, a_ref, own_ref, sib_ref, wo_ref,
                     all_ref, tall_ref, log_ref, lo_ref, gq_ref, gk_ref, gv_ref, *refs):
    piece_refs = refs[:4]
    (rows_ref, heads_ref, grads_ref, delta_ref, kt_ref, gqt_ref, gks_ref, gvs_ref,
     dense_ref) = refs[4:]
    total, mine = q_ref.shape
    width = own_ref.shape[1]
    half = total // 2
    heads = mine // HEAD_DIM
    core = meta_ref[0]
    rows_ref[pl.ds(pl.multiple_of(core * half, half), half), :] = own_ref[...]
    rows_ref[pl.ds(pl.multiple_of((1 - core) * half, half), half), :] = sib_ref[...]
    weights = wo_ref[pl.ds(pl.multiple_of(core * mine, mine), mine), :]
    for t in range(total // TILE):
        here = slice(t * TILE, (t + 1) * TILE)
        grads = dot_nt(rows_ref[here, :], weights).astype(BF16)
        turned = grads.astype(F32).T * tall_ref[:, here]
        for h in range(heads):
            span = slice(h * HEAD_DIM, (h + 1) * HEAD_DIM)
            delta_ref[h : h + 1, here] = jnp.sum(turned[span, :], axis=0, keepdims=True)
        for g in range(mine // LANES):
            for h, part in enumerate(masked_heads(grads[:, lanes_of(g)])):
                grads_ref[2 * g + h, here, :] = part
    put_heads(heads_ref, q_ref[...] * jnp.asarray(HEAD_DIM**-0.5, BF16))
    kt_ref[...] = flip(k_ref[...])
    gks_ref[...] = jnp.zeros_like(gks_ref)
    gvs_ref[...] = jnp.zeros_like(gvs_ref)
    gqt_ref[...] = jnp.zeros_like(gqt_ref)

    def tile(t, unused):
        at = pl.multiple_of(t * TILE, TILE)
        here = pl.ds(at, TILE)
        low = lo_ref[:, here]
        high = total + at + iota((1, TILE), 1)

        def step(j, carry):
            begin = pl.multiple_of(j * TILE, TILE)
            there = pl.ds(begin, TILE)
            allowed = tile_mask(begin, low, high)
            for g in range(heads // 2):
                keys = k_ref[there, lanes_of(g)]
                values = v_ref[there, lanes_of(g)]
                gk = gks_ref[there, lanes_of(g)]
                gv = gvs_ref[there, lanes_of(g)]
                for h in (2 * g, 2 * g + 1):
                    span = slice(h * HEAD_DIM, (h + 1) * HEAD_DIM)
                    queries = heads_ref[h, here, :]
                    grads = grads_ref[h, here, :]
                    scores = jnp.where(allowed, dot_nt(keys, queries), LOWER)
                    soft = jnp.exp(scores - log_ref[h : h + 1, here])
                    grad_soft = dot_nt(values, grads) - delta_ref[h : h + 1, here]
                    grad_scores = (soft * grad_soft).astype(BF16)
                    gv += dot(soft.astype(BF16), grads)
                    gk += dot(grad_scores, queries)
                    gqt_ref[span, here] += dot(kt_ref[span, there], grad_scores)
                gks_ref[there, lanes_of(g)] = gk
                gvs_ref[there, lanes_of(g)] = gv
            return carry

        return lax.fori_loop(meta_ref[1 + t], total // TILE + t + 1, step, unused)

    lax.fori_loop(0, total // TILE, tile, 0)
    gqt = gqt_ref[...] * (HEAD_DIM**-0.5)
    gq_ref[...] = gqt.T.astype(BF16)
    gk_ref[...] = gks_ref[...].astype(BF16)
    gv_ref[...] = gvs_ref[...].astype(BF16)

    cols = mine // LANES
    lines = cols * width

    def put(kind, turned):
        for j in range(cols):
            first = kind * lines + j * width
            dense_ref[first : first + width, :] = turned[lanes_of(j), :].T.astype(BF16)

    put(0, dot(gqt.astype(BF16), a_ref[total:, :]))
    put(1, dot_tn(gk_ref[...], a_ref[...]))
    put(2, dot_tn(gv_ref[...], a_ref[...]))
    grad_out = dot_tn(all_ref[...], rows_ref[...]).astype(BF16)
    for j in range(width // LANES):
        first = 3 * lines + j * mine
        dense_ref[first : first + mine, :] = grad_out[:, lanes_of(j)]
    filled = 3 * lines + mine * (width // LANES)
    count = dense_ref.shape[0]
    if count > filled:
        dense_ref[filled:, :] = jnp.zeros((count - filled, LANES), BF16)
    quarter = count // 4
    for p in range(2):
        side = meta_ref[sizes + p]
        for r, which in enumerate((side, 1 - side)):
            first = pl.multiple_of(2 * p * quarter + which * quarter, 16)
            piece_refs[2 * p + r][...] = dense_ref[pl.ds(first, quarter), :]


def attend_back(meta, q, k, v, a, own, sib, w_out, attn_all, tall, logs, low, count):
    total, mine = q.shape
    width = own.shape[1]
    heads = mine // HEAD_DIM
    outs = [
        shape((total, mine), BF16),
        shape((2 * total, mine), BF16),
        shape((2 * total, mine), BF16),
    ] + [shape((count // 4, LANES), BF16)] * 4
    return call(
        functools.partial(attend_back_body, meta.shape[0] - 2), "attend_back", outs,
        (meta, q, k, v, a, own, sib, w_out, attn_all, tall, logs, low), scalars=1,
        scratch=[pltpu.VMEM((total, width), BF16), pltpu.VMEM((heads, total, LANES), BF16),
                 pltpu.VMEM((heads, total, LANES), BF16), pltpu.VMEM(logs.shape, F32),
                 pltpu.VMEM((mine, 2 * total), BF16), pltpu.VMEM((mine, total), F32),
                 pltpu.VMEM((2 * total, mine), F32), pltpu.VMEM((2 * total, mine), F32),
                 pltpu.VMEM((count, LANES), BF16)],
    )


def lift_body(parts, capacity, core_ref, own_ref, other_ref, w_ref, x_ref, gain_ref, bias_ref,
              slot_ref, resid_ref, *out_refs):
    mine = own_ref.shape[1]
    core = core_ref[0]
    own_w = w_ref[pl.ds(pl.multiple_of(core * mine, mine), mine), :]
    other_w = w_ref[pl.ds(pl.multiple_of((1 - core) * mine, mine), mine), :]
    resid = x_ref[...].astype(F32) + (dot(own_ref[...], own_w) + dot(other_ref[...], other_w))
    resid_ref[...] = resid
    normed, unused = norm_rows(resid)
    rows = (normed * gain_ref[...] + bias_ref[...]).astype(BF16)
    slot = slot_ref[...]
    for k in range(parts):
        chosen = one_hot(slot - k * capacity, capacity)
        out_refs[k][...] = dot_tn(chosen, rows).astype(BF16)


def lift(core, own, other, w_out, x, gain, bias, slot, parts, capacity):
    count, width = x.shape
    outs = [shape((count, width), F32)] + [shape((capacity, width), BF16)] * parts
    return call(
        functools.partial(lift_body, parts, capacity), "lift", outs,
        (core, own, other, w_out, x, gain, bias, slot),
        scalars=1, flops=2 * count * width * (width + parts * capacity),
    )


GATE_A = math.sqrt(2.0 / math.pi)
GATE_B = 0.044715


def expert_body(sub, rows_ref, grad_ref, up_ref, down_ref, hid_ref, pre_ref, back_ref, out_ref,
                back_acc, out_acc):
    step = pl.program_id(0)

    @pl.when(step == 0)
    def _():
        back_acc[...] = jnp.zeros_like(back_acc)
        out_acc[...] = jnp.zeros_like(out_acc)

    back, out = None, None
    for s in range(down_ref.shape[0] // sub):
        part = slice(s * sub, (s + 1) * sub)
        pre = dot(rows_ref[...], up_ref[:, part])
        grad_hidden = dot_nt(grad_ref[...], down_ref[part, :])
        square = pre * pre
        bend = jnp.tanh(GATE_A * (pre + GATE_B * (square * pre)))
        half = 0.5 * (1.0 + bend)
        hid = pre * half
        hid_ref[part, :] = hid.T.astype(BF16)
        slope = half + (0.5 * GATE_A) * pre * (1.0 - bend * bend) * (1.0 + (3.0 * GATE_B) * square)
        grad_pre = (grad_hidden * slope).astype(BF16)
        pre_ref[:, part] = grad_pre
        more = dot_nt(grad_pre, up_ref[:, part])
        back = more if back is None else back + more
        more = dot(hid.astype(BF16), down_ref[part, :])
        out = more if out is None else out + more
    back_acc[...] += back
    out_acc[...] += out

    @pl.when(step == pl.num_programs(0) - 1)
    def _():
        back_ref[...] = back_acc[...].astype(BF16)
        out_ref[...] = out_acc[...].astype(BF16)


def expert(rows, grads, w_up, w_down, block=768, sub=256):
    count, width = rows.shape
    hidden = w_up.shape[1]
    const = pl.BlockSpec((count, width), lambda j: (0, 0))
    return call(
        functools.partial(expert_body, sub), "expert",
        [shape((hidden, count), BF16), shape((count, hidden), BF16), shape((count, width), BF16),
         shape((count, width), BF16)],
        (rows, grads, w_up, w_down), grid=(hidden // block,),
        in_specs=[const, const, pl.BlockSpec((width, block), lambda j: (0, j)),
                  pl.BlockSpec((block, width), lambda j: (j, 0))],
        out_specs=[pl.BlockSpec((block, count), lambda j: (j, 0)),
                   pl.BlockSpec((count, block), lambda j: (0, j)), const, const],
        scratch=[pltpu.VMEM((count, width), F32)] * 2,
    )


def expert_grad_body(parts, *refs):
    rows, grads, hids, pres = (refs[parts * t : parts * (t + 1)] for t in range(4))
    out_ref, turned_ref = refs[4 * parts :]
    count = rows[0].shape[0]
    width = rows[0].shape[1]

    @pl.when(pl.program_id(0) == 0)
    def _():
        for k in range(parts):
            turned_ref[:, k * count : (k + 1) * count] = flip(rows[k][...])

    up, down = None, None
    for k in range(parts):
        more = dot(hids[k][...], grads[k][...])
        down = more if down is None else down + more
        more = dot(turned_ref[:, k * count : (k + 1) * count], pres[k][...])
        up = more if up is None else up + more
    out_ref[:width, :] = up.astype(BF16)
    out_ref[width:, :] = down.astype(BF16)


def expert_grad(rows, grads, hids, pres):
    parts = len(rows)
    count, width = rows[0].shape
    block = width
    hidden = hids[0].shape[0]
    const = pl.BlockSpec((count, width), lambda j: (0, 0))
    col = pl.BlockSpec((count, block), lambda j: (0, j))
    line = pl.BlockSpec((block, count), lambda j: (j, 0))
    return call(
        functools.partial(expert_grad_body, parts), "expert_grad",
        shape((2 * hidden, width), BF16),
        (*rows, *grads, *hids, *pres), grid=(hidden // block,),
        in_specs=[const] * (2 * parts) + [line] * parts + [col] * parts,
        out_specs=pl.BlockSpec((2 * block, width), lambda j: (j, 0)),
        scratch=[pltpu.VMEM((width, parts * count), BF16)],
    )


def widen_body(up_ref, down_ref, up_out, down_out):
    up_out[...] = up_ref[...].astype(F32)
    down_out[...] = down_ref[...].astype(F32)


def widen(grads, pieces=2):
    width = grads.shape[1]
    hidden = grads.shape[0] // 2
    rows = width // pieces
    return call(
        widen_body, "widen", [shape((width, hidden), F32), shape((hidden, width), F32)],
        (grads, grads), grid=(hidden // width, pieces),
        in_specs=[pl.BlockSpec((rows, width), lambda j, r: (2 * j * pieces + r, 0)),
                  pl.BlockSpec((rows, width), lambda j, r: ((2 * j + 1) * pieces + r, 0))],
        out_specs=[pl.BlockSpec((rows, width), lambda j, r: (r, j)),
                   pl.BlockSpec((rows, width), lambda j, r: (j * pieces + r, 0))],
    )


def collect(slot, part_refs):
    total = None
    for k, ref in enumerate(part_refs):
        capacity = ref.shape[0]
        more = dot(one_hot(slot - k * capacity, capacity), ref[...])
        total = more if total is None else total + more
    return total


def lower_body(parts, slot_ref, resid_ref, cot_ref, gain_ref, *refs):
    grads = collect(slot_ref[...], refs[:parts])
    gr_ref, low_ref, gain_out, bias_out = refs[parts:]
    normed, scale = norm_rows(resid_ref[...])
    gain_out[...] = jnp.sum(grads * normed, axis=0, keepdims=True)
    bias_out[...] = jnp.sum(grads, axis=0, keepdims=True)
    gr = cot_ref[...].astype(F32) + norm_back(grads * gain_ref[...], normed, scale)
    gr_ref[...] = gr
    low_ref[...] = gr.astype(BF16)


def lower(slot, resid, cot, gain, back):
    parts = len(back)
    count, width = resid.shape
    outs = [shape((count, width), F32), shape((count, width), BF16),
            shape((1, width), F32), shape((1, width), F32)]
    return call(
        functools.partial(lower_body, parts), "lower", outs, (slot, resid, cot, gain, *back),
        flops=2 * count * width * parts * back[0].shape[0],
    )


def finish_body(slot_ref, resid_ref, *refs):
    refs[-1][...] = (resid_ref[...] + collect(slot_ref[...], refs[:-1])).astype(BF16)


def finish(slot, resid, parts):
    count, width = resid.shape
    return call(
        finish_body, "finish", shape((count, width), BF16), (slot, resid, *parts),
        flops=2 * count * width * len(parts) * parts[0].shape[0],
    )


def project_back_body(half, core_ref, own_ref, sib_ref, hal_ref, has_ref, gq_ref, gk_ref, gv_ref,
                      wq_ref, wk_ref, wv_ref, keep_ref, send_ref, halo_ref, gain_ref, bias_ref):
    step = pl.program_id(0)
    rows = jnp.where(
        step < 2 * half,
        jnp.where(step < half, own_ref[...], sib_ref[...]),
        jnp.where(step < 3 * half, hal_ref[...], has_ref[...]),
    )
    normed, unused = norm_rows(rows.astype(F32))
    here = step < 2 * half
    ga = dot_nt(gk_ref[...], wk_ref[...]) + dot_nt(gv_ref[...], wv_ref[...])
    gq = jnp.where(here, gq_ref[...], jnp.zeros_like(gq_ref))
    ga = ga + dot_nt(gq, wq_ref[...])

    @pl.when(step == 0)
    def _():
        gain_ref[...] = jnp.zeros_like(gain_ref)
        bias_ref[...] = jnp.zeros_like(bias_ref)

    gain_ref[...] += jnp.sum(ga * normed, axis=0, keepdims=True)
    bias_ref[...] += jnp.sum(ga, axis=0, keepdims=True)

    @pl.when(step < half)
    def _():
        keep_ref[...] = ga

    @pl.when((step // half) % 2 == 1)
    def _():
        send_ref[...] = ga.astype(BF16)

    @pl.when(step // half == 2)
    def _():
        halo_ref[...] = ga


def project_back(core, own, sib, hal, has, gq, gk, gv, w_qkv):
    count, width = own.shape
    mine = gq.shape[1]
    half = count // TILE

    def at(t):
        return lambda i, c: (jnp.clip(i - t * half, 0, half - 1), 0)

    def place(i, c):
        return jnp.where(i < 2 * half, 2 * half, 0) + (((i // half) % 2) ^ c[0]) * half + i % half

    def sent(i, c):
        late = half + jnp.clip(i - 3 * half, 0, half - 1)
        return (jnp.where(i < 2 * half, jnp.clip(i - half, 0, half - 1), late), 0)

    row = pl.BlockSpec((1, width), lambda i, c: (0, 0))
    in_specs = [pl.BlockSpec((TILE, width), at(t)) for t in range(4)] + [
        pl.BlockSpec((TILE, mine), lambda i, c: (jnp.maximum(place(i, c) - 2 * half, 0), 0)),
        pl.BlockSpec((TILE, mine), lambda i, c: (place(i, c), 0)),
        pl.BlockSpec((TILE, mine), lambda i, c: (place(i, c), 0)),
    ] + [
        pl.BlockSpec((width, mine), functools.partial(lambda t, i, c: (0, 2 * t + c[0]), t))
        for t in range(3)
    ]
    return call(
        functools.partial(project_back_body, half), "project_back",
        [shape((count, width), F32), shape((2 * count, width), BF16), shape((count, width), F32),
         shape((1, width), F32), shape((1, width), F32)],
        (core, own, sib, hal, has, gq, gk, gv, w_qkv, w_qkv, w_qkv),
        grid=(4 * half,), in_specs=in_specs, scalars=1,
        out_specs=[pl.BlockSpec((TILE, width), at(0)), pl.BlockSpec((TILE, width), sent),
                   pl.BlockSpec((TILE, width), at(2)), row, row],
        flops=20 * count * width * mine,
    )


def close_body(x_ref, gr_ref, keep_ref, near_ref, far_ref, gain_ref, out_ref):
    ga = keep_ref[...] + near_ref[...].astype(F32) + far_ref[...].astype(F32)
    normed, scale = norm_rows(x_ref[...].astype(F32))
    out_ref[...] = gr_ref[...] + norm_back(ga * gain_ref[...], normed, scale)


def close(x, gr, keep, near, far, gain):
    count, width = x.shape
    block = pl.BlockSpec((TILE, width), lambda i: (i, 0))
    return call(
        close_body, "close", shape((count, width), F32), (x, gr, keep, near, far, gain),
        grid=(count // TILE,),
        in_specs=[block] * 5 + [pl.BlockSpec((1, width), lambda i: (0, 0))], out_specs=block,
    )


def swap(block, axis, distance):
    return lax.ppermute(block, axis, [(i, i ^ distance) for i in range(lax.axis_size(axis))])


def shift(block, axis, distance):
    size = lax.axis_size(axis)
    route = [(i, i + distance) for i in range(size) if 0 <= i + distance < size]
    return lax.ppermute(block, axis, route)


def add(a, b):
    return (a.astype(F32) + b.astype(F32)).astype(BF16)


def at_index(block, index):
    return lax.dynamic_index_in_dim(block, index, 0, keepdims=False)


def total_of(pieces, bit_orders, seq_at, exp_at, beside):
    sources = lax.axis_size("exp")
    stages = len(bit_orders[0])
    parts = list(pieces)
    for s in range(stages):
        pairs = []
        for part, bits in zip(parts, bit_orders):
            if s:
                side = (seq_at // bits[s]) % 2
                cut = part.reshape(2, -1, LANES)
                part = (at_index(cut, side), at_index(cut, 1 - side))
            pairs.append(part)
        arrived = beside([swap(p[1], "seq", bits[s]) for p, bits in zip(pairs, bit_orders)])
        parts = [add(p[0], r) for p, r in zip(pairs, arrived)]
    joined = jnp.stack([p.reshape(sources, -1, LANES) for p in parts], axis=1)
    arrived = beside(
        [swap(at_index(joined, exp_at ^ k), "exp", k) for k in range(1, sources)]
    )
    own = sum((g.astype(F32) for g in arrived), at_index(joined, exp_at).astype(F32)).astype(BF16)
    arrived = beside([swap(own, "exp", k) for k in range(1, sources)])
    spread = jnp.stack([own] + arrived)
    spread = spread[jnp.arange(sources, dtype=jnp.int32) ^ exp_at]
    parts = [spread[:, p].reshape(-1, LANES) for p in range(len(bit_orders))]
    for s in reversed(range(stages)):
        arrived = beside([swap(p, "seq", bits[s]) for p, bits in zip(parts, bit_orders)])
        moved = list(zip(parts, arrived))
        if not s:
            return moved
        parts = []
        for (mine, theirs), bits in zip(moved, bit_orders):
            side = (seq_at // bits[s]) % 2
            parts.append(
                jnp.where(
                    side == 0,
                    jnp.concatenate([mine, theirs], axis=0),
                    jnp.concatenate([theirs, mine], axis=0),
                )
            )


def join_body(side_ref, *refs):
    out_ref = refs[4]
    quarter = refs[0].shape[0]
    for p in range(2):
        side = side_ref[p]
        for r, which in enumerate((side, 1 - side)):
            first = pl.multiple_of(2 * p * quarter + which * quarter, 16)
            out_ref[pl.ds(first, quarter), :] = refs[2 * p + r][...]


def join(sides, pieces):
    quarter = pieces[0].shape[0]
    return call(
        join_body, "join", shape((4 * quarter, LANES), BF16), (sides, *pieces), scalars=1
    )


def spread_body(cols, core_ref, own_ref, sib_ref, out_ref):
    first = core_ref[0] == 0
    for kind in range(3):
        for j in range(cols):
            own = own_ref[kind * cols + j].astype(F32)
            sib = sib_ref[kind * cols + j].astype(F32)
            left = 2 * kind * cols + j
            out_ref[:, lanes_of(left)] = jnp.where(first, own, sib)
            out_ref[:, lanes_of(left + cols)] = jnp.where(first, sib, own)


def spread_columns(core, own, sib, width, mine, block=64):
    cols = mine // LANES
    blocks = 3 * cols
    own, sib = (t[: blocks * width].reshape(blocks, width, LANES) for t in (own, sib))
    part = pl.BlockSpec((blocks, block, LANES), lambda i, c: (0, i, 0))
    return call(
        functools.partial(spread_body, cols), "spread_columns",
        shape((width, 3 * width), F32), (core, own, sib), grid=(width // block,), scalars=1,
        in_specs=[part, part],
        out_specs=pl.BlockSpec((block, 3 * width), lambda i, c: (i, 0)),
    )


def spread_rows_body(core_ref, own_ref, sib_ref, out_ref):
    mine = own_ref.shape[1]
    for s, ref in enumerate((own_ref, sib_ref)):
        side = core_ref[0] if s == 0 else 1 - core_ref[0]
        here = pl.ds(pl.multiple_of(side * mine, mine), mine)
        for j in range(ref.shape[0]):
            out_ref[here, lanes_of(j)] = ref[j].astype(F32)


def spread_rows(core, own, sib, width, mine, skip):
    blocks = width // LANES
    own, sib = (
        t[skip : skip + blocks * mine].reshape(blocks, mine, LANES) for t in (own, sib)
    )
    return call(
        spread_rows_body, "spread_rows", shape((width, width), F32), (core, own, sib), scalars=1
    )


def on_device(
    layer_input,
    token_ids,
    segment_ids,
    hash_table,
    first_gain,
    first_bias,
    second_gain,
    second_bias,
    w_qkv,
    w_out,
    w_up,
    w_down,
    cotangent,
):
    x = layer_input[0]
    cot = cotangent[0]
    local_len, width = x.shape
    mine = width // 2
    sources = lax.axis_size("exp")
    ring = lax.axis_size("seq")
    capacity = 2 * local_len // sources
    seq_at = lax.axis_index("seq")
    exp_at = lax.axis_index("exp")
    core = (seq_at % 2).astype(jnp.int32)
    core_arg = core.reshape(1)
    gain_one, bias_one = first_gain[None], first_bias[None]
    gain_two, bias_two = second_gain[None], second_bias[None]
    up, down = w_up[0], w_down[0]

    hal = shift(x, "seq", 2)
    sib = swap(x, "seq", 1)

    pair_len = 2 * local_len
    segment_row = segment_ids[0]
    pair_at = (seq_at // 2) * pair_len
    docs = 2 * ring * local_len // DOC_MOST
    grid = jnp.arange(docs, dtype=jnp.int32)[:, None]
    starts = jnp.sum((segment_row[None, :] < grid).astype(jnp.int32), axis=1, keepdims=True)
    here = lax.dynamic_slice_in_dim(segment_row, pair_at, pair_len, 0)[None, :]
    low = jnp.sum(jnp.where(here == grid, starts, 0), axis=0, keepdims=True) - (pair_at - pair_len)
    meta = jnp.concatenate([core_arg, low[0, ::TILE] // TILE])

    lines = -(-hash_table.shape[0] // (8 * LANES)) * 8
    table = jnp.pad(hash_table, (0, lines * LANES - hash_table.shape[0])).astype(BF16)
    slot, *grad_out = route(
        exp_at.astype(jnp.int32).reshape(1), token_ids[0][:, None],
        table.reshape(lines, LANES), cot, sources, capacity,
    )
    grad_in = [grad_out[0]] + [swap(grad_out[k], "exp", k) for k in range(1, sources)]

    *made, q = project(core_arg, x, after(sib, slot), gain_one, bias_one, w_qkv, None)
    hal = after(hal, q)
    has = swap(hal, "seq", 1)
    a, k, v = project(core_arg, hal, has, gain_one, bias_one, w_qkv, made)
    attn_own, attn_give, attn_all, attn_tall, logs = attend(meta, q, k, v, low)
    attn_other = swap(attn_give, "seq", 1)
    resid, *rows_out = lift(
        core_arg, attn_own, after(attn_other, grad_in), w_out, x, gain_two, bias_two, slot, sources, capacity
    )
    rows_in = [rows_out[0]] + [swap(rows_out[k], "exp", k) for k in range(1, sources)]
    hids, pres, backs, outs = [], [], [], []
    for k_at in range(sources):
        hid, pre, back, out = expert(rows_in[k_at], grad_in[k_at], up, down)
        hids.append(hid)
        pres.append(pre)
        backs.append(back if k_at == 0 else swap(back, "exp", k_at))
        outs.append(out)
        if k_at + 1 < sources:
            rows_in[k_at + 1] = after(rows_in[k_at + 1], back)
    grad_experts = expert_grad(rows_in, grad_in, hids, pres)
    backs, grad_experts = lax.optimization_barrier((backs, grad_experts))
    part_experts = lax.psum_scatter(grad_experts, "seq", scatter_dimension=0, tiled=True)

    gr, gattn, gain_two_grad, bias_two_grad = lower(slot, resid, cot, gain_two, backs)
    *outs, gattn = lax.optimization_barrier((*outs, gattn))
    returned = [outs[0]] + [swap(outs[k], "exp", k) for k in range(1, sources)]
    gattn_sib = swap(gattn, "seq", 1)
    bits = [1 << b for b in range(1, ring.bit_length() - 1)]
    orders = [bits, bits[::-1]]
    sides = jnp.stack([(seq_at // o[0]) % 2 for o in orders]).astype(jnp.int32)
    filled = 3 * width * mine // LANES + mine * width // LANES
    unit = ring * sources * 16
    gq, gk, gv, *pieces = attend_back(
        jnp.concatenate([meta, sides]), q, k, v, a, gattn, gattn_sib, w_out, attn_all, attn_tall,
        logs, low, filled + -filled % unit,
    )
    keep, give, halo, gain_one_grad, bias_one_grad = project_back(
        core_arg, x, sib, hal, has, gq, gk, gv, w_qkv
    )
    near = swap(give, "seq", 1)
    small = jnp.concatenate([gain_one_grad, bias_one_grad, gain_two_grad, bias_two_grad], axis=0)
    hops = [("seq", 1 << b) for b in range(ring.bit_length() - 1)]
    hops += [("exp", 1 << b) for b in range(sources.bit_length() - 1)]
    done = {"step": 0, "small": small, "experts": part_experts, "returned": returned}

    def beside(arrived):
        step = done["step"]
        done["step"] = step + 1
        if step == 0:
            return lax.optimization_barrier((arrived, give))[0]
        hop = hops[step - 1 : step]
        sent = [swap(done["small"], *h) for h in hop]
        if step == 1:
            tied = (near,)
        elif step == len(bits):
            tied = (part_experts,)
        elif step == len(bits) + 1:
            done["output"] = finish(slot, resid, done["returned"])
            tied = (done["output"],)
        elif step == len(bits) + 2:
            done["far"] = shift(add(halo, done["near"][local_len:]), "seq", -2)
            done["input"] = close(x, gr, keep, done["near"][:local_len], done["far"], gain_one)
            tied = (done["input"],)
        else:
            tied = ()
        arrived, sent, tied = lax.optimization_barrier((arrived, sent, tied))
        if step == 1:
            done["near"] = tied[0]
        if step == len(bits):
            done["experts"] = tied[0]
        elif step == len(bits) + 1:
            done["output"] = tied[0]
        elif step == len(bits) + 2:
            done["input"] = tied[0]
        for s in sent:
            done["small"] = done["small"] + s
        return arrived

    pieces, done["returned"] = lax.optimization_barrier((pieces, returned))
    quarters = total_of(
        [(pieces[0], pieces[1]), (pieces[2], pieces[3])], orders, seq_at, exp_at, beside
    )
    small = done["small"]
    for hop in hops[done["step"] - 1 :]:
        small = small + swap(small, *hop)
    all_experts = lax.all_gather(done["experts"], "seq", axis=0, tiled=True)
    own_sum = join(sides, [quarters[0][0], quarters[0][1], quarters[1][0], quarters[1][1]])
    sib_sum = swap(own_sum, "seq", 1)
    grad_w_qkv = spread_columns(core_arg, own_sum, sib_sum, width, mine)
    grad_w_out = spread_rows(core_arg, own_sum, sib_sum, width, mine, 3 * width * mine // LANES)

    grad_w_up, grad_w_down = widen(all_experts)
    return (
        done["output"][None],
        done["input"][None],
        grad_w_qkv,
        grad_w_out,
        small[0],
        small[1],
        small[2],
        small[3],
        grad_w_up[None],
        grad_w_down[None],
    )


def solution(mesh):
    in_specs = (
        P("exp", "seq", None),
        P("exp", "seq"),
        P("exp", None),
        P(),
        P(),
        P(),
        P(),
        P(),
        P(),
        P(),
        P("exp", None, None),
        P("exp", None, None),
        P("exp", "seq", None),
    )
    out_specs = (
        P("exp", "seq", None),
        P("exp", "seq", None),
        P(),
        P(),
        P(),
        P(),
        P(),
        P(),
        P("exp", None, None),
        P("exp", None, None),
    )
    return jax.shard_map(
        on_device, mesh=mesh, in_specs=in_specs, out_specs=out_specs, check_vma=False
    )
```

```python
import functools
import math

import jax
import jax.numpy as jnp
from jax import lax
from jax.experimental import pallas as pl
from jax.experimental.pallas import tpu as pltpu
from jax.sharding import PartitionSpec as P

HEADS = 12
HEAD_DIM = 64
DOC_MOST = 1024
EPSILON = 1e-05
LOW = -1e30
LOWER = -2e30
LANES = 128
TILE = 256
F32 = jnp.float32
BF16 = jnp.bfloat16
MIB = 1 << 20
COST = 1


def dot(a, b):
    return lax.dot_general(a, b, (((1,), (0,)), ((), ())), preferred_element_type=F32)


def dot_nt(a, b):
    return lax.dot_general(a, b, (((1,), (1,)), ((), ())), preferred_element_type=F32)


def dot_tn(a, b):
    return lax.dot_general(a, b, (((0,), (0,)), ((), ())), preferred_element_type=F32)


def iota(shape, axis):
    return lax.broadcasted_iota(jnp.int32, shape, axis)


def one_hot(ids, width):
    return jnp.where(iota((ids.shape[0], width), 1) == ids, 1.0, 0.0).astype(BF16)


def norm_rows(values):
    center = values - jnp.mean(values, axis=-1, keepdims=True)
    scale = lax.rsqrt(jnp.mean(center * center, axis=-1, keepdims=True) + EPSILON)
    return center * scale, scale


def norm_back(grad, normed, scale):
    inner = jnp.mean(grad * normed, axis=-1, keepdims=True)
    return scale * (grad - jnp.mean(grad, axis=-1, keepdims=True) - normed * inner)


def after(value, *others):
    return lax.optimization_barrier((value, others))[0]


def shape(dims, dtype):
    return jax.ShapeDtypeStruct(dims, dtype)


def call(body, name, out_shape, args, *, grid=(), in_specs=None, out_specs=None, scratch=(),
         scalars=0, aliases=None, flops=0, nbytes=0, special=0, vmem=56):
    outs = out_shape if isinstance(out_shape, (tuple, list)) else [out_shape]
    whole = pl.BlockSpec(memory_space=pltpu.VMEM)
    if in_specs is None:
        in_specs = [whole] * (len(args) - scalars)
    if out_specs is None:
        out_specs = [whole] * len(outs)
        if not isinstance(out_shape, (tuple, list)):
            out_specs = out_specs[0]
    return pl.pallas_call(
        body,
        name=name,
        out_shape=out_shape,
        grid_spec=pltpu.PrefetchScalarGridSpec(
            num_scalar_prefetch=scalars,
            grid=grid,
            in_specs=in_specs,
            out_specs=out_specs,
            scratch_shapes=scratch,
        ),
        input_output_aliases=aliases or {},
        cost_estimate=pl.CostEstimate(flops=COST, bytes_accessed=COST, transcendentals=0),
        compiler_params=pltpu.CompilerParams(vmem_limit_bytes=vmem * MIB),
    )(*args)


def route_body(parts, capacity, place_ref, ids_ref, table_ref, rows_ref, slot_ref, *out_refs):
    ids = ids_ref[...]
    count = ids.shape[0]
    lines = table_ref.shape[0]
    picked = dot(one_hot(ids >> 7, lines), table_ref[...])
    lane = iota((count, LANES), 1)
    choice = jnp.sum(
        jnp.where(lane == (ids & (LANES - 1)), picked, 0.0), axis=1, keepdims=True
    ).astype(jnp.int32)
    mine = lane == choice
    below = jnp.where(iota((count, count), 0) > iota((count, count), 1), 1.0, 0.0).astype(BF16)
    ranks = dot(below, jnp.where(mine, 1.0, 0.0).astype(BF16))
    rank = jnp.sum(jnp.where(mine, ranks, 0.0), axis=1, keepdims=True).astype(jnp.int32)
    slot = (choice ^ place_ref[0]) * capacity + rank
    slot_ref[...] = slot
    rows = rows_ref[...]
    for k in range(parts):
        chosen = one_hot(slot - k * capacity, capacity)
        out_refs[k][...] = dot_tn(chosen, rows).astype(BF16)


def route(place, ids, table, rows, parts, capacity):
    count, width = rows.shape
    outs = [shape((count, 1), jnp.int32)] + [shape((capacity, width), BF16)] * parts
    return call(
        functools.partial(route_body, parts, capacity), "route", outs, (place, ids, table, rows),
        scalars=1, flops=2 * count * parts * capacity * width + 2 * count * count * LANES,
    )


def project_body(skip, core_ref, own_ref, sib_ref, norm_ref, wq_ref, wk_ref, wv_ref, *refs):
    outs = refs[skip:-1]
    held_ref = refs[-1]
    step = pl.program_id(0)
    half = (pl.num_programs(0) - 1) // 2
    before = held_ref[(step + 1) % 2]
    outs[1][...] = dot(before, wk_ref[...]).astype(BF16)
    outs[2][...] = dot(before, wv_ref[...]).astype(BF16)
    if not skip:
        outs[3][...] = dot(before, wq_ref[...]).astype(BF16)
    rows = jnp.where(step < half, own_ref[...], sib_ref[...])
    normed, unused = norm_rows(rows.astype(F32))
    a = (normed * norm_ref[0:1, :] + norm_ref[1:2, :]).astype(BF16)
    held_ref[step % 2] = a
    outs[0][...] = a


def project(core, own, sib, norms, w_qkv, made):
    count, width = own.shape
    mine = width // 2
    half = count // TILE
    base = 0 if made else 2 * half

    def place(i, c):
        return ((i // half) ^ c[0]) * half + i % half

    def now(i, c):
        return (base + place(jnp.minimum(i, 2 * half - 1), c), 0)

    def then(i, c):
        return (base + place(jnp.maximum(i - 1, 0), c), 0)

    in_specs = [
        pl.BlockSpec((TILE, width), lambda i, c: (jnp.minimum(i, half - 1), 0)),
        pl.BlockSpec((TILE, width), lambda i, c: (jnp.clip(i - half, 0, half - 1), 0)),
        pl.BlockSpec(norms.shape, lambda i, c: (0, 0)),
    ] + [
        pl.BlockSpec((width, mine), functools.partial(lambda t, i, c: (0, 2 * t + c[0]), t))
        for t in range(3)
    ]
    args = [core, own, sib, norms, w_qkv, w_qkv, w_qkv]
    outs = [shape((4 * count, width), BF16)] + [shape((4 * count, mine), BF16)] * 2
    out_specs = [
        pl.BlockSpec((TILE, width), now),
        pl.BlockSpec((TILE, mine), then),
        pl.BlockSpec((TILE, mine), then),
    ]
    aliases = {}
    if made:
        in_specs += [pl.BlockSpec(memory_space=pl.ANY)] * 3
        aliases = {7: 0, 8: 1, 9: 2}
        args += list(made)
    else:
        outs.append(shape((2 * count, mine), BF16))
        out_specs.append(
            pl.BlockSpec((TILE, mine), lambda i, c: (place(jnp.maximum(i - 1, 0), c), 0))
        )
    return call(
        functools.partial(project_body, 3 if made else 0), "project", outs, args,
        grid=(2 * half + 1,), in_specs=in_specs, out_specs=out_specs, scalars=1, aliases=aliases,
        scratch=[pltpu.VMEM((2, TILE, width), BF16)],
    )


def masked_heads(block):
    lane = iota(block.shape, 1)
    zero = jnp.zeros((), block.dtype)
    return [
        jnp.where(lane < HEAD_DIM, block, zero),
        jnp.where(lane < HEAD_DIM, zero, block),
    ]


def flip(block):
    return block.astype(F32).T.astype(block.dtype)


def lanes_of(group):
    return slice(group * LANES, (group + 1) * LANES)


def put_heads(ref, block):
    for g in range(block.shape[1] // LANES):
        for h, part in enumerate(masked_heads(block[:, lanes_of(g)])):
            ref[2 * g + h] = part


def tile_mask(begin, low, high):
    place = begin + iota((TILE, TILE), 0)
    return (place >= low) & (place <= high)


def attend_body(meta_ref, q_ref, k_ref, v_ref, lo_ref, own_ref, sib_ref, all_ref, tall_ref,
                log_ref, heads_ref, acc_ref, rows_ref):
    total, mine = q_ref.shape
    half = total // 2
    heads = range(mine // HEAD_DIM)
    put_heads(heads_ref, q_ref[...] * jnp.asarray(HEAD_DIM**-0.5, BF16))
    core = meta_ref[0]

    def tile(t, unused):
        at = pl.multiple_of(t * TILE, TILE)
        here = pl.ds(at, TILE)
        low = lo_ref[here, :]
        high = total + at + iota((TILE, 1), 0)
        acc_ref[...] = jnp.zeros_like(acc_ref)

        def step(j, state):
            begin = pl.multiple_of(j * TILE, TILE)
            there = pl.ds(begin, TILE)
            place = begin + iota((TILE, TILE), 1)
            allowed = (place >= low) & (place <= high)
            scores = [
                jnp.where(
                    allowed, dot_nt(heads_ref[h, here, :], k_ref[there, lanes_of(h // 2)]), LOWER
                )
                for h in heads
            ]
            tops = [
                jnp.maximum(state[2 * h], jnp.max(scores[h], axis=1, keepdims=True)) for h in heads
            ]
            shares = [jnp.exp(scores[h] - tops[h]) for h in heads]
            factors = [jnp.exp(state[2 * h] - tops[h]) for h in heads]
            sums = [
                state[2 * h + 1] * factors[h] + jnp.sum(shares[h], axis=1, keepdims=True)
                for h in heads
            ]
            more = [dot(shares[h].astype(BF16), v_ref[there, lanes_of(h // 2)]) for h in heads]
            for h in heads:
                acc_ref[h] = acc_ref[h] * factors[h] + more[h]
            return tuple(x for h in heads for x in (tops[h], sums[h]))

        first = (jnp.full((TILE, 1), LOW, F32), jnp.zeros((TILE, 1), F32))
        state = lax.fori_loop(
            meta_ref[1 + t], total // TILE + t + 1, step, first * len(heads)
        )
        lane = iota((TILE, LANES), 1)
        logs = jnp.zeros((TILE, LANES), F32)
        for h in heads:
            logs = jnp.where(lane == h, state[2 * h] + jnp.log(state[2 * h + 1]), logs)
        log_ref[:, here] = logs.T[: log_ref.shape[0], :]
        for g in range(mine // LANES):
            left = acc_ref[2 * g] / state[4 * g + 1]
            right = acc_ref[2 * g + 1] / state[4 * g + 3]
            out = jnp.where(lane < HEAD_DIM, left, right)
            rows_ref[here, lanes_of(g)] = out
            tall_ref[lanes_of(g), here] = out.T
        return unused

    lax.fori_loop(0, total // TILE, tile, 0)
    all_ref[...] = rows_ref[...].astype(BF16)
    own_at = pl.multiple_of(core * half, half)
    sib_at = pl.multiple_of((1 - core) * half, half)
    own_ref[...] = rows_ref[pl.ds(own_at, half), :].astype(BF16)
    sib_ref[...] = rows_ref[pl.ds(sib_at, half), :].astype(BF16)


def attend(meta, q, k, v, low):
    total, mine = q.shape
    heads = mine // HEAD_DIM
    outs = [
        shape((total // 2, mine), BF16),
        shape((total // 2, mine), BF16),
        shape((total, mine), BF16),
        shape((mine, total), F32),
        shape((-(-heads // 8) * 8, total), F32),
    ]
    return call(
        attend_body, "attend", outs, (meta, q, k, v, low), scalars=1,
        scratch=[pltpu.VMEM((heads, total, LANES), BF16), pltpu.VMEM((heads, TILE, LANES), F32),
                 pltpu.VMEM((total, mine), F32)],
    )


def attend_back_body(meta_ref, q_ref, k_ref, v_ref, own_ref, sib_ref, wo_ref, tall_ref, log_ref,
                     lo_ref, gq_ref, gk_ref, gv_ref, rows_ref, heads_ref, grads_ref, delta_ref,
                     kt_ref, gqt_ref, gks_ref, gvs_ref):
    total, mine = q_ref.shape
    width = own_ref.shape[1]
    half = total // 2
    heads = mine // HEAD_DIM
    core = meta_ref[0]
    rows_ref[pl.ds(pl.multiple_of(core * half, half), half), :] = own_ref[...]
    rows_ref[pl.ds(pl.multiple_of((1 - core) * half, half), half), :] = sib_ref[...]
    weights = wo_ref[pl.ds(pl.multiple_of(core * mine, mine), mine), :]
    for t in range(total // TILE):
        here = slice(t * TILE, (t + 1) * TILE)
        grads = dot_nt(rows_ref[here, :], weights).astype(BF16)
        turned = grads.astype(F32).T * tall_ref[:, here]
        for h in range(heads):
            span = slice(h * HEAD_DIM, (h + 1) * HEAD_DIM)
            delta_ref[h : h + 1, here] = jnp.sum(turned[span, :], axis=0, keepdims=True)
        for g in range(mine // LANES):
            for h, part in enumerate(masked_heads(grads[:, lanes_of(g)])):
                grads_ref[2 * g + h, here, :] = part
    put_heads(heads_ref, q_ref[...] * jnp.asarray(HEAD_DIM**-0.5, BF16))
    kt_ref[...] = flip(k_ref[...])
    gks_ref[...] = jnp.zeros_like(gks_ref)
    gvs_ref[...] = jnp.zeros_like(gvs_ref)
    gqt_ref[...] = jnp.zeros_like(gqt_ref)

    def tile(t, unused):
        at = pl.multiple_of(t * TILE, TILE)
        here = pl.ds(at, TILE)
        low = lo_ref[:, here]
        high = total + at + iota((1, TILE), 1)

        logs = [log_ref[h : h + 1, here] for h in range(heads)]
        deltas = [delta_ref[h : h + 1, here] for h in range(heads)]

        def step(j, carry):
            begin = pl.multiple_of(j * TILE, TILE)
            there = pl.ds(begin, TILE)
            allowed = tile_mask(begin, low, high)
            every = range(heads)
            queries = [heads_ref[h, here, :] for h in every]
            grads = [grads_ref[h, here, :] for h in every]
            scores = [dot_nt(k_ref[there, lanes_of(h // 2)], queries[h]) for h in every]
            grad_soft = [dot_nt(v_ref[there, lanes_of(h // 2)], grads[h]) for h in every]
            soft = [jnp.exp(jnp.where(allowed, scores[h], LOWER) - logs[h]) for h in every]
            grad_scores = [(soft[h] * (grad_soft[h] - deltas[h])).astype(BF16) for h in every]
            soft = [s.astype(BF16) for s in soft]
            gv = [dot(soft[h], grads[h]) for h in every]
            gk = [dot(grad_scores[h], queries[h]) for h in every]
            gq = [
                dot(kt_ref[h * HEAD_DIM : (h + 1) * HEAD_DIM, there], grad_scores[h])
                for h in every
            ]
            for g in range(heads // 2):
                gvs_ref[there, lanes_of(g)] += gv[2 * g] + gv[2 * g + 1]
                gks_ref[there, lanes_of(g)] += gk[2 * g] + gk[2 * g + 1]
            for h in every:
                gqt_ref[h * HEAD_DIM : (h + 1) * HEAD_DIM, here] += gq[h]
            return carry

        return lax.fori_loop(meta_ref[1 + t], total // TILE + t + 1, step, unused)

    lax.fori_loop(0, total // TILE, tile, 0)
    gqt = gqt_ref[...] * (HEAD_DIM**-0.5)
    gq_ref[...] = gqt.T.astype(BF16)
    gk_ref[...] = gks_ref[...].astype(BF16)
    gv_ref[...] = gvs_ref[...].astype(BF16)


def attend_back(meta, q, k, v, own, sib, w_out, tall, logs, low):
    total, mine = q.shape
    width = own.shape[1]
    heads = mine // HEAD_DIM
    outs = [
        shape((total, mine), BF16),
        shape((2 * total, mine), BF16),
        shape((2 * total, mine), BF16),
    ]
    return call(
        attend_back_body, "attend_back", outs,
        (meta, q, k, v, own, sib, w_out, tall, logs, low), scalars=1,
        scratch=[pltpu.VMEM((total, width), BF16), pltpu.VMEM((heads, total, LANES), BF16),
                 pltpu.VMEM((heads, total, LANES), BF16), pltpu.VMEM(logs.shape, F32),
                 pltpu.VMEM((mine, 2 * total), BF16), pltpu.VMEM((mine, total), F32),
                 pltpu.VMEM((2 * total, mine), F32), pltpu.VMEM((2 * total, mine), F32)],
    )


def dense_body(subs, sub, chip_ref, a_ref, gq_ref, gk_ref, gv_ref, all_ref, own_ref, sib_ref, *refs):
    piece_refs, dense_ref = refs[:4], refs[4]
    total, mine = gq_ref.shape
    half, width = own_ref.shape
    lines = width // subs
    quarter = subs * sub

    def put(kind, turned):
        for j in range(mine // LANES):
            block = turned[lanes_of(j), :].T.astype(BF16)
            for at in range(subs):
                first = kind * quarter + at * sub + j * lines
                dense_ref[first : first + lines, :] = block[at * lines : (at + 1) * lines, :]

    put(0, dot_tn(gq_ref[...], a_ref[total:, :]))
    put(1, dot_tn(gk_ref[...], a_ref[...]))
    put(2, dot_tn(gv_ref[...], a_ref[...]))
    core = chip_ref[0]
    own_at = pl.ds(pl.multiple_of(core * half, half), half)
    sib_at = pl.ds(pl.multiple_of((1 - core) * half, half), half)
    put(3, dot_tn(all_ref[own_at, :], own_ref[...]) + dot_tn(all_ref[sib_at, :], sib_ref[...]))
    spare = sub - mine // LANES * lines
    if spare:
        for at in range(4 * subs):
            dense_ref[(at + 1) * sub - spare : (at + 1) * sub, :] = jnp.zeros((spare, LANES), BF16)
    for p in range(2):
        side = chip_ref[1 + p]
        for r, which in enumerate((side, 1 - side)):
            for at in range(subs):
                from_at = pl.multiple_of((2 * p + which) * quarter + at * sub, 16)
                to_at = pl.multiple_of((at ^ chip_ref[3 + p]) * sub, 16)
                piece_refs[2 * p + r][pl.ds(to_at, sub), :] = dense_ref[pl.ds(from_at, sub), :]


def dense_pieces(chip, a, gq, gk, gv, attn_all, own, sib, subs, sub):
    return call(
        functools.partial(dense_body, subs, sub), "dense",
        [shape((subs * sub, LANES), BF16)] * 4,
        (chip, a, gq, gk, gv, attn_all, own, sib), scalars=1,
        scratch=[pltpu.VMEM((4 * subs * sub, LANES), BF16)],
    )


def lift_body(parts, capacity, core_ref, own_ref, other_ref, w_ref, x_ref, norm_ref, slot_ref,
              resid_ref, *out_refs):
    mine = own_ref.shape[1]
    core = core_ref[0]
    own_w = w_ref[pl.ds(pl.multiple_of(core * mine, mine), mine), :]
    other_w = w_ref[pl.ds(pl.multiple_of((1 - core) * mine, mine), mine), :]
    resid = x_ref[...].astype(F32) + (dot(own_ref[...], own_w) + dot(other_ref[...], other_w))
    resid_ref[...] = resid
    normed, unused = norm_rows(resid)
    rows = (normed * norm_ref[2:3, :] + norm_ref[3:4, :]).astype(BF16)
    slot = slot_ref[...]
    for k in range(parts):
        chosen = one_hot(slot - k * capacity, capacity)
        out_refs[k][...] = dot_tn(chosen, rows).astype(BF16)


def lift(core, own, other, w_out, x, norms, slot, parts, capacity):
    count, width = x.shape
    outs = [shape((count, width), F32)] + [shape((capacity, width), BF16)] * parts
    return call(
        functools.partial(lift_body, parts, capacity), "lift", outs,
        (core, own, other, w_out, x, norms, slot),
        scalars=1, flops=2 * count * width * (width + parts * capacity),
    )


GATE_A = math.sqrt(2.0 / math.pi)
GATE_B = 0.044715


def expert_body(sub, rows_ref, grad_ref, up_ref, down_ref, tall_ref, pre_ref, back_ref, out_ref,
                turned_ref, back_acc, out_acc):
    step = pl.program_id(0)

    @pl.when(step == 0)
    def _():
        back_acc[...] = jnp.zeros_like(back_acc)
        out_acc[...] = jnp.zeros_like(out_acc)
        turned_ref[...] = flip(rows_ref[...])

    parts = [slice(s * sub, (s + 1) * sub) for s in range(down_ref.shape[0] // sub)]
    pres = [dot(rows_ref[...], up_ref[:, part]) for part in parts]
    grads = [dot_nt(grad_ref[...], down_ref[part, :]) for part in parts]
    hids, slopes = [], []
    for pre in pres:
        square = pre * pre
        bend = jnp.tanh(GATE_A * (pre + GATE_B * (square * pre)))
        half = 0.5 + 0.5 * bend
        hids.append(pre * half)
        slopes.append(
            half + (pre * (1.0 - bend * bend)) * (0.5 * GATE_A + (1.5 * GATE_A * GATE_B) * square)
        )
    low = jnp.concatenate([(g * s).astype(BF16) for g, s in zip(grads, slopes)], axis=1)
    back_acc[...] += dot_nt(low, up_ref[...])
    out_acc[...] += dot(jnp.concatenate([h.astype(BF16) for h in hids], axis=1), down_ref[...])
    pre_ref[...] = low
    for part, hid in zip(parts, hids):
        tall_ref[part, :] = hid.T.astype(BF16)

    @pl.when(step == pl.num_programs(0) - 1)
    def _():
        back_ref[...] = back_acc[...].astype(BF16)
        out_ref[...] = out_acc[...].astype(BF16)


def expert(rows, grads, w_up, w_down, sub=256):
    count, width = rows.shape
    hidden = w_up.shape[1]
    block = width
    const = pl.BlockSpec((count, width), lambda j: (0, 0))
    return call(
        functools.partial(expert_body, sub), "expert",
        [shape((hidden, count), BF16), shape((count, hidden), BF16), shape((count, width), BF16),
         shape((count, width), BF16), shape((width, count), BF16)],
        (rows, grads, w_up, w_down), grid=(hidden // block,),
        in_specs=[const, const, pl.BlockSpec((width, block), lambda j: (0, j)),
                  pl.BlockSpec((block, width), lambda j: (j, 0))],
        out_specs=[pl.BlockSpec((block, count), lambda j: (j, 0)),
                   pl.BlockSpec((count, block), lambda j: (0, j)), const, const,
                   pl.BlockSpec((width, count), lambda j: (0, 0))],
        scratch=[pltpu.VMEM((count, width), F32)] * 2,
    )


def expert_grad_body(parts, subs, chip_ref, *refs):
    turned, grads, talls, pres = (refs[parts * t : parts * (t + 1)] for t in range(4))
    give_ref, keep_ref = refs[4 * parts :]
    width = give_ref.shape[1]
    lines = width // subs
    step = pl.program_id(0)
    half = pl.num_programs(0) // 2

    def product(left, right):
        out = None
        for a, b in zip(left, right):
            more = dot(a[...], b[...])
            out = more if out is None else out + more
        return out.astype(BF16)

    up, down = product(turned, pres), product(talls, grads)
    side, mask = chip_ref[1 + step % half], chip_ref[3 + step % half]

    def put(out_ref):
        for value, stays in ((up, side == 0), (down, side == 1)):
            base = jnp.where(stays, width, 0)
            for at in range(subs):
                first = pl.multiple_of(base + (at ^ mask) * lines, 16)
                out_ref[pl.ds(first, lines), :] = value[at * lines : (at + 1) * lines, :]

    @pl.when(step < half)
    def _():
        put(give_ref)

    @pl.when(step >= half)
    def _():
        put(keep_ref)


def expert_grad(chip, turned, grads, talls, pres, subs):
    parts = len(grads)
    count, width = grads[0].shape
    blocks = talls[0].shape[0] // width
    half = blocks // 2

    def column(i, m):
        return jnp.where(i < half, (1 - m[0]) * half, m[0] * half - half) + i

    const = lambda dims: pl.BlockSpec(dims, lambda i, m: (0, 0))
    return call(
        functools.partial(expert_grad_body, parts, subs), "expert_grad",
        [shape((2 * half * width, width), BF16)] * 2,
        (chip, *turned, *grads, *talls, *pres), grid=(blocks,), scalars=1,
        in_specs=[const((width, count))] * parts + [const((count, width))] * parts
        + [pl.BlockSpec((width, count), lambda i, m: (column(i, m), 0))] * parts
        + [pl.BlockSpec((count, width), lambda i, m: (0, column(i, m)))] * parts,
        out_specs=[pl.BlockSpec((2 * width, width), lambda i, m: (jnp.minimum(i, half - 1), 0)),
                   pl.BlockSpec((2 * width, width), lambda i, m: (jnp.maximum(i - half, 0), 0))],
    )


def widen_body(up_ref, down_ref, up_out, down_out):
    up_out[...] = up_ref[...].astype(F32)
    down_out[...] = down_ref[...].astype(F32)


def widen(got, orders, hidden):
    ring, unused, lines, width = got.shape
    subs = width // lines

    def source(kind, j, r):
        core, p = j // 2, j % 2
        device = 0
        for bits in orders:
            here = core + kind * bits[0]
            for at, bit in enumerate(bits[1:]):
                here = here + ((r >> (len(bits) - 2 - at)) & 1) * bit
            device = device + jnp.where(p == orders.index(bits), here, 0)
        return device, p, 0, 0

    block = lambda kind: pl.BlockSpec((None, None, lines, width), functools.partial(source, kind))
    return call(
        widen_body, "widen", [shape((width, hidden), F32), shape((hidden, width), F32)],
        (got, got), grid=(hidden // width, subs), in_specs=[block(0), block(1)],
        out_specs=[pl.BlockSpec((lines, width), lambda j, r: (r, j)),
                   pl.BlockSpec((lines, width), lambda j, r: (j * subs + r, 0))],
    )


def collect(slot, part_refs):
    total = None
    for k, ref in enumerate(part_refs):
        capacity = ref.shape[0]
        more = dot(one_hot(slot - k * capacity, capacity), ref[...])
        total = more if total is None else total + more
    return total


def lower_body(parts, slot_ref, resid_ref, cot_ref, norm_ref, *refs):
    grads = collect(slot_ref[...], refs[:parts])
    gr_ref, low_ref, gain_out, bias_out = refs[parts:]
    normed, scale = norm_rows(resid_ref[...])
    gain_out[...] = jnp.sum(grads * normed, axis=0, keepdims=True)
    bias_out[...] = jnp.sum(grads, axis=0, keepdims=True)
    gr = cot_ref[...].astype(F32) + norm_back(grads * norm_ref[2:3, :], normed, scale)
    gr_ref[...] = gr
    low_ref[...] = gr.astype(BF16)


def lower(slot, resid, cot, norms, back):
    parts = len(back)
    count, width = resid.shape
    outs = [shape((count, width), F32), shape((count, width), BF16),
            shape((1, width), F32), shape((1, width), F32)]
    return call(
        functools.partial(lower_body, parts), "lower", outs, (slot, resid, cot, norms, *back),
        flops=2 * count * width * parts * back[0].shape[0],
    )


def finish_body(slot_ref, resid_ref, *refs):
    refs[-1][...] = (resid_ref[...] + collect(slot_ref[...], refs[:-1])).astype(BF16)


def finish(slot, resid, parts):
    return call(finish_body, "finish", shape(resid.shape, BF16), (slot, resid, *parts))


def project_back_body(half, core_ref, own_ref, sib_ref, hal_ref, has_ref, gq_ref, gk_ref, gv_ref,
                      wq_ref, wk_ref, wv_ref, keep_ref, send_ref, halo_ref, gain_ref, bias_ref):
    step = pl.program_id(0)
    rows = jnp.where(
        step < 2 * half,
        jnp.where(step < half, own_ref[...], sib_ref[...]),
        jnp.where(step < 3 * half, hal_ref[...], has_ref[...]),
    )
    normed, unused = norm_rows(rows.astype(F32))
    here = step < 2 * half
    ga = dot_nt(gk_ref[...], wk_ref[...]) + dot_nt(gv_ref[...], wv_ref[...])
    gq = jnp.where(here, gq_ref[...], jnp.zeros_like(gq_ref))
    ga = ga + dot_nt(gq, wq_ref[...])

    @pl.when(step == 0)
    def _():
        gain_ref[...] = jnp.zeros_like(gain_ref)
        bias_ref[...] = jnp.zeros_like(bias_ref)

    gain_ref[...] += jnp.sum(ga * normed, axis=0, keepdims=True)
    bias_ref[...] += jnp.sum(ga, axis=0, keepdims=True)

    @pl.when(step < half)
    def _():
        keep_ref[...] = ga

    @pl.when((step // half) % 2 == 1)
    def _():
        send_ref[...] = ga.astype(BF16)

    @pl.when(step // half == 2)
    def _():
        halo_ref[...] = ga


def project_back(core, own, sib, hal, has, gq, gk, gv, w_qkv):
    count, width = own.shape
    mine = gq.shape[1]
    half = count // TILE

    def at(t):
        return lambda i, c: (jnp.clip(i - t * half, 0, half - 1), 0)

    def place(i, c):
        return jnp.where(i < 2 * half, 2 * half, 0) + (((i // half) % 2) ^ c[0]) * half + i % half

    def sent(i, c):
        late = half + jnp.clip(i - 3 * half, 0, half - 1)
        return (jnp.where(i < 2 * half, jnp.clip(i - half, 0, half - 1), late), 0)

    row = pl.BlockSpec((1, width), lambda i, c: (0, 0))
    in_specs = [pl.BlockSpec((TILE, width), at(t)) for t in range(4)] + [
        pl.BlockSpec((TILE, mine), lambda i, c: (jnp.maximum(place(i, c) - 2 * half, 0), 0)),
        pl.BlockSpec((TILE, mine), lambda i, c: (place(i, c), 0)),
        pl.BlockSpec((TILE, mine), lambda i, c: (place(i, c), 0)),
    ] + [
        pl.BlockSpec((width, mine), functools.partial(lambda t, i, c: (0, 2 * t + c[0]), t))
        for t in range(3)
    ]
    return call(
        functools.partial(project_back_body, half), "project_back",
        [shape((count, width), F32), shape((2 * count, width), BF16), shape((count, width), F32),
         shape((1, width), F32), shape((1, width), F32)],
        (core, own, sib, hal, has, gq, gk, gv, w_qkv, w_qkv, w_qkv),
        grid=(4 * half,), in_specs=in_specs, scalars=1,
        out_specs=[pl.BlockSpec((TILE, width), at(0)), pl.BlockSpec((TILE, width), sent),
                   pl.BlockSpec((TILE, width), at(2)), row, row],
        flops=20 * count * width * mine,
    )


def close_body(x_ref, gr_ref, keep_ref, near_ref, far_ref, norm_ref, out_ref):
    ga = keep_ref[...] + near_ref[...].astype(F32) + far_ref[...].astype(F32)
    normed, scale = norm_rows(x_ref[...].astype(F32))
    out_ref[...] = gr_ref[...] + norm_back(ga * norm_ref[0:1, :], normed, scale)


def close(x, gr, keep, near, far, norms):
    count, width = x.shape
    block = pl.BlockSpec((TILE, width), lambda i: (i, 0))
    return call(
        close_body, "close", shape((count, width), F32), (x, gr, keep, near, far, norms),
        grid=(count // TILE,),
        in_specs=[block] * 5 + [pl.BlockSpec(norms.shape, lambda i: (0, 0))], out_specs=block,
    )


def swap(block, axis, distance):
    return lax.ppermute(block, axis, [(i, i ^ distance) for i in range(lax.axis_size(axis))])


def trade(block, axis):
    return lax.all_to_all(block, axis, split_axis=0, concat_axis=0, tiled=True)


def shift(block, axis, distance):
    size = lax.axis_size(axis)
    route = [(i, i + distance) for i in range(size) if 0 <= i + distance < size]
    return lax.ppermute(block, axis, route)


def total(terms):
    return sum(t.astype(F32) for t in terms).astype(BF16)


def add(a, b):
    return total([a, b])


def at_index(block, index):
    return lax.dynamic_index_in_dim(block, index, 0, keepdims=False)


def scatter_steps(pieces, orders):
    pairs = list(pieces)
    for s in range(len(orders[0])):
        arrived = yield [(goes, "seq", bits[s]) for (stays, goes), bits in zip(pairs, orders)]
        terms = [stays + [got] for (stays, goes), got in zip(pairs, arrived)]
        if s + 1 < len(orders[0]):
            half = terms[0][0].shape[0] // 2
            pairs = [
                ([total([t[half:] for t in terms_p])], total([t[:half] for t in terms_p]))
                for terms_p in terms
            ]
    return [total(terms_p) for terms_p in terms]


def gather_steps(parts, orders):
    parts = list(parts)
    for s in reversed(range(1, len(orders[0]))):
        arrived = yield [(part, "seq", bits[s]) for part, bits in zip(parts, orders)]
        parts = [jnp.concatenate([got, part], axis=0) for got, part in zip(arrived, parts)]
    return parts


def dense_steps(pieces, orders):
    sources = lax.axis_size("exp")
    parts = yield from scatter_steps(pieces, orders)
    joined = jnp.stack([p.reshape(sources, -1, LANES) for p in parts], axis=1)
    (got,) = yield [(joined, "exp", 0)]
    own = jnp.sum(got.astype(F32), axis=0).astype(BF16)
    (got,) = yield [(jnp.broadcast_to(own, (sources, *own.shape)), "exp", 0)]
    parts = [got[:, p].reshape(-1, LANES) for p in range(len(orders))]
    return (yield from gather_steps(parts, orders))


def one_step(sends):
    return (yield sends)


def across(parts, orders):
    return Stream(one_step([(part, "seq", bits[0]) for part, bits in zip(parts, orders)]))


def beside(parts):
    return Stream(one_step([(part, "seq", 1) for part in parts]))


def small_steps(value, hops):
    for hop in hops:
        (got,) = yield [(value, *hop)]
        value = value + got
    return value


class Stream:
    def __init__(self, steps):
        self.steps = steps
        self.result = None
        self.sent = []
        self.go(None)

    def go(self, arrived):
        try:
            sends = self.steps.send(arrived)
        except StopIteration as stop:
            self.sent, self.raw, self.result = [], [], stop.value
        else:
            self.raw = [send[0] for send in sends]
            self.sent = [swap(*send) if send[2] else trade(*send[:2]) for send in sends]


def meet(streams, others=()):
    streams = [stream for stream in streams if stream.sent]
    arrived, others = lax.optimization_barrier(([stream.sent for stream in streams], others))
    before = []
    for stream, got in zip(streams, arrived):
        stream.go(after(got, before) if before else got)
        before = before + stream.raw
    return others


def spread_columns_body(cols, chip_ref, *refs):
    out_ref = refs[-1]
    first = chip_ref[0] == 0
    own, sib = refs[:4], refs[4:8]
    picks = [
        (0, chip_ref[1] == 0, 0, 1),
        (1, chip_ref[1] == 1, 0, 1),
        (2, chip_ref[2] == 0, 2, 3),
    ]
    for kind, mine, here, there in picks:
        for j in range(cols):
            a, b = (jnp.where(mine, t[here][0, j], t[there][0, j]).astype(F32) for t in (own, sib))
            left = 2 * kind * cols + j
            out_ref[:, lanes_of(left)] = jnp.where(first, a, b)
            out_ref[:, lanes_of(left + cols)] = jnp.where(first, b, a)


def spread_rows_body(chip_ref, *refs):
    out_ref = refs[-1]
    own = pl.program_id(0) == chip_ref[0]
    mine = chip_ref[2] == 1
    subs, cols, lines, unused = refs[0].shape
    for at in range(subs):
        from_at = at ^ chip_ref[4]
        for j in range(cols):
            a, b = (
                jnp.where(mine, refs[t][from_at, j], refs[t + 1][from_at, j]) for t in (0, 2)
            )
            out_ref[lanes_of(j), at * lines : (at + 1) * lines] = (
                jnp.where(own, a, b).astype(F32).T
            )


def spread(chip, own, sib, width, mine, subs):
    cols = mine // LANES
    lines = width // subs
    block = math.gcd(lines, 192)

    def view(t):
        return t.reshape(subs, -1, LANES)[:, : cols * lines].reshape(subs, cols, lines, LANES)

    def part(p):
        def index(i, m):
            return ((i * block // lines) ^ m[3 + p], 0, i % (lines // block), 0)

        return pl.BlockSpec((1, cols, block, LANES), index)

    parts = [[view(t) for pair in side for t in pair] for side in (own, sib)]
    grad_qkv = call(
        functools.partial(spread_columns_body, cols), "spread_columns",
        shape((width, 3 * width), F32), (chip, *parts[0], *parts[1]), grid=(width // block,),
        scalars=1, in_specs=[part(0), part(0), part(1), part(1)] * 2,
        out_specs=pl.BlockSpec((block, 3 * width), lambda i, m: (i, 0)),
    )
    whole = pl.BlockSpec((subs, cols, lines, LANES), lambda i, m: (0, 0, 0, 0))
    grad_out = call(
        spread_rows_body, "spread_rows", shape((width, width), F32),
        (chip, *parts[0][2:], *parts[1][2:]), grid=(2,), scalars=1, in_specs=[whole] * 4,
        out_specs=pl.BlockSpec((mine, width), lambda i, m: (i, 0)),
    )
    return grad_qkv, grad_out


def on_device(
    layer_input,
    token_ids,
    segment_ids,
    hash_table,
    first_gain,
    first_bias,
    second_gain,
    second_bias,
    w_qkv,
    w_out,
    w_up,
    w_down,
    cotangent,
):
    x = layer_input[0]
    cot = cotangent[0]
    local_len, width = x.shape
    mine = width // 2
    sources = lax.axis_size("exp")
    ring = lax.axis_size("seq")
    capacity = 2 * local_len // sources
    seq_at = lax.axis_index("seq")
    exp_at = lax.axis_index("exp")
    core = (seq_at % 2).astype(jnp.int32)
    core_arg = core.reshape(1)
    norms = jnp.stack([first_gain, first_bias, second_gain, second_bias])
    up, down = w_up[0], w_down[0]

    hal = shift(x, "seq", 2)
    sib = swap(x, "seq", 1)

    pair_len = 2 * local_len
    segment_row = segment_ids[0]
    pair_at = (seq_at // 2) * pair_len
    docs = 2 * ring * local_len // DOC_MOST
    grid = jnp.arange(docs, dtype=jnp.int32)[:, None]
    starts = jnp.sum((segment_row[None, :] < grid).astype(jnp.int32), axis=1, keepdims=True)
    here = lax.dynamic_slice_in_dim(segment_row, pair_at, pair_len, 0)[None, :]
    low = jnp.sum(jnp.where(here == grid, starts, 0), axis=0, keepdims=True) - (pair_at - pair_len)
    meta = jnp.concatenate([core_arg, low[0, ::TILE] // TILE])

    lines = -(-hash_table.shape[0] // (8 * LANES)) * 8
    table = jnp.pad(hash_table, (0, lines * LANES - hash_table.shape[0])).astype(BF16)
    place = exp_at.astype(jnp.int32).reshape(1)
    slot, *grad_out = route(
        place, token_ids[0][:, None], table.reshape(lines, LANES), cot, sources, capacity
    )
    grad_in = [grad_out[0]] + [swap(grad_out[k], "exp", k) for k in range(1, sources)]

    *made, q = project(core_arg, x, after(sib, slot), norms, w_qkv, None)
    hal = after(hal, q)
    has = swap(hal, "seq", 1)
    a, k, v = project(core_arg, hal, has, norms, w_qkv, made)
    attn_own, attn_give, attn_all, attn_tall, logs = attend(meta, q, k, v, low.reshape(-1, 1))
    attn_other = swap(attn_give, "seq", 1)
    resid, *rows_out = lift(
        core_arg, attn_own, after(attn_other, grad_in), w_out, x, norms, slot, sources, capacity
    )
    rows_in = [rows_out[0]] + [swap(rows_out[k], "exp", k) for k in range(1, sources)]
    talls, pres, backs, outs, turned = [], [], [], [], []
    for k_at in range(sources):
        tall, pre, back, out, turn = expert(rows_in[k_at], grad_in[k_at], up, down)
        talls.append(tall)
        pres.append(pre)
        outs.append(out)
        turned.append(turn)
        backs.append(back if k_at == 0 else swap(back, "exp", k_at))
        if k_at + 1 < sources:
            rows_in[k_at + 1] = after(rows_in[k_at + 1], back)
    bits = [1 << b for b in range(1, ring.bit_length() - 1)]
    orders = [bits, bits[::-1]]
    sides = [(seq_at // o[0]) % 2 for o in orders]
    subs = ring // 4
    masks = [
        sum((1 - (seq_at // bit) % 2) << (len(o) - 2 - at) for at, bit in enumerate(o[1:]))
        for o in orders
    ]
    chip = jnp.stack([core, *sides, *masks]).astype(jnp.int32)

    turned, backs[:-2] = lax.optimization_barrier((turned, backs[:-2]))
    given, kept = expert_grad(chip, turned, grad_in, talls, pres, subs)
    given, backs[-2] = lax.optimization_barrier((given, backs[-2]))
    given, backs[-1] = lax.optimization_barrier((given, backs[-1]))
    got = swap(given, "seq", 1)
    gr, gattn, gain_two_grad, bias_two_grad = lower(slot, resid, cot, norms, backs)
    got, kept = (t.reshape(2, 2, width, width) for t in (after(got, gattn), kept))
    goes = [add(kept[p, 0], got[p, 0]) for p in range(2)]
    stays = [[kept[p, 1], got[p, 1]] for p in range(2)]
    experts = Stream(scatter_steps(list(zip(stays, goes)), orders))
    outs = after(outs, goes)
    returned = [outs[0]] + [swap(outs[k], "exp", k) for k in range(1, sources)]
    gattn_sib = swap(gattn, "seq", 1)
    unit = sources * 16
    sub = -(-(mine // LANES * width // subs) // unit) * unit
    gq, gk, gv = attend_back(
        meta, q, k, v, gattn, after(gattn_sib, goes), w_out, attn_tall, logs, low
    )
    pieces = dense_pieces(chip, a, gq, gk, gv, attn_all, gattn, gattn_sib, subs, sub)
    pieces, returned = lax.optimization_barrier((pieces, returned))
    dense = Stream(
        dense_steps([([pieces[0]], pieces[1]), ([pieces[2]], pieces[3])], orders)
    )
    (gq,) = meet([experts], (after(gq, pieces),))
    keep, give, halo, gain_one_grad, bias_one_grad = project_back(
        core_arg, x, sib, hal, has, gq, gk, gv, w_qkv
    )
    small = jnp.concatenate([gain_one_grad, bias_one_grad, gain_two_grad, bias_two_grad], axis=0)
    (give,) = meet([dense, experts], (give,))
    for rest in range(len(bits) - 2):
        meet([experts])
    gathered = lax.all_gather(jnp.stack(experts.result), "seq")
    near = swap(give, "seq", 1)
    hops = [("seq", 1 << b) for b in range(ring.bit_length() - 1)]
    hops += [("exp", 1 << b) for b in range(sources.bit_length() - 1)]
    small = Stream(small_steps(small, hops))
    (near,) = meet([dense, small], (near,))
    far = shift(add(halo, near[local_len:]), "seq", -2)
    for rest in range(len(bits) - 2):
        meet([dense, small])
    layer_output = finish(slot, resid, returned)
    (layer_output,) = meet([dense, small], (layer_output,))
    while dense.result is None:
        meet([dense, small])
    own_dense = dense.result
    dense_chip, dense_core = across(own_dense, orders), beside(own_dense)
    grad_w_up, grad_w_down = meet(
        [dense_chip, dense_core, small], widen(gathered, orders, down.shape[0])
    )
    dense_both = beside(dense_chip.result)
    meet([dense_both, small])
    while small.sent:
        meet([small])
    grad_w_qkv, grad_w_out = spread(
        chip, list(zip(own_dense, dense_chip.result)),
        list(zip(dense_core.result, dense_both.result)), width, mine, subs,
    )
    grad_input = close(x, gr, keep, near[:local_len], after(far, grad_w_qkv), norms)
    small = small.result
    return (
        layer_output[None],
        grad_input[None],
        grad_w_qkv,
        grad_w_out,
        small[0],
        small[1],
        small[2],
        small[3],
        grad_w_up[None],
        grad_w_down[None],
    )


def solution(mesh):
    in_specs = (
        P("exp", "seq", None),
        P("exp", "seq"),
        P("exp", None),
        P(),
        P(),
        P(),
        P(),
        P(),
        P(),
        P(),
        P("exp", None, None),
        P("exp", None, None),
        P("exp", "seq", None),
    )
    out_specs = (
        P("exp", "seq", None),
        P("exp", "seq", None),
        P(),
        P(),
        P(),
        P(),
        P(),
        P(),
        P("exp", None, None),
        P("exp", None, None),
    )
    return jax.shard_map(
        on_device, mesh=mesh, in_specs=in_specs, out_specs=out_specs, check_vma=False
    )
```

```python
import functools
import math

import jax
import jax.numpy as jnp
from jax import lax
from jax.experimental import pallas as pl
from jax.experimental.pallas import tpu as pltpu
from jax.sharding import PartitionSpec as P

HEADS = 12
HEAD_DIM = 64
DOC_MOST = 1024
EPSILON = 1e-05
LOW = -1e30
LOWER = -2e30
LANES = 128
TILE = 256
F32 = jnp.float32
BF16 = jnp.bfloat16
MIB = 1 << 20
COST = 1


def dot(a, b):
    return lax.dot_general(a, b, (((1,), (0,)), ((), ())), preferred_element_type=F32)


def dot_nt(a, b):
    return lax.dot_general(a, b, (((1,), (1,)), ((), ())), preferred_element_type=F32)


def dot_tn(a, b):
    return lax.dot_general(a, b, (((0,), (0,)), ((), ())), preferred_element_type=F32)


def iota(shape, axis):
    return lax.broadcasted_iota(jnp.int32, shape, axis)


def one_hot(ids, width):
    return jnp.where(iota((ids.shape[0], width), 1) == ids, 1.0, 0.0).astype(BF16)


def norm_rows(values):
    center = values - jnp.mean(values, axis=-1, keepdims=True)
    scale = lax.rsqrt(jnp.mean(center * center, axis=-1, keepdims=True) + EPSILON)
    return center * scale, scale


def norm_back(grad, normed, scale):
    inner = jnp.mean(grad * normed, axis=-1, keepdims=True)
    return scale * (grad - jnp.mean(grad, axis=-1, keepdims=True) - normed * inner)


def after(value, *others):
    return lax.optimization_barrier((value, others))[0]


def shape(dims, dtype):
    return jax.ShapeDtypeStruct(dims, dtype)


def call(body, name, out_shape, args, *, grid=(), in_specs=None, out_specs=None, scratch=(),
         scalars=0, aliases=None, flops=0, nbytes=0, special=0, vmem=56):
    outs = out_shape if isinstance(out_shape, (tuple, list)) else [out_shape]
    whole = pl.BlockSpec(memory_space=pltpu.VMEM)
    if in_specs is None:
        in_specs = [whole] * (len(args) - scalars)
    if out_specs is None:
        out_specs = [whole] * len(outs)
        if not isinstance(out_shape, (tuple, list)):
            out_specs = out_specs[0]
    return pl.pallas_call(
        body,
        name=name,
        out_shape=out_shape,
        grid_spec=pltpu.PrefetchScalarGridSpec(
            num_scalar_prefetch=scalars,
            grid=grid,
            in_specs=in_specs,
            out_specs=out_specs,
            scratch_shapes=scratch,
        ),
        input_output_aliases=aliases or {},
        cost_estimate=pl.CostEstimate(flops=COST, bytes_accessed=COST, transcendentals=0),
        compiler_params=pltpu.CompilerParams(vmem_limit_bytes=vmem * MIB),
    )(*args)


def column(row):
    return jnp.broadcast_to(row.astype(F32), (8, row.shape[1])).T[:, :1].astype(jnp.int32)


def route_body(parts, capacity, docs, at_ref, ids_ref, table_ref, rows_ref, segment_ref, slot_ref,
               low_ref, tall_ref, meta_ref, *out_refs):
    ids = column(ids_ref[...])
    count = ids.shape[0]
    lines = table_ref.shape[0]
    picked = dot(one_hot(ids >> 7, lines), table_ref[...].astype(F32).astype(BF16))
    lane = iota((count, LANES), 1)
    choice = jnp.sum(
        jnp.where(lane == (ids & (LANES - 1)), picked, 0.0), axis=1, keepdims=True
    ).astype(jnp.int32)
    mine = lane == choice
    below = jnp.where(iota((count, count), 0) > iota((count, count), 1), 1.0, 0.0).astype(BF16)
    ranks = dot(below, jnp.where(mine, 1.0, 0.0).astype(BF16))
    rank = jnp.sum(jnp.where(mine, ranks, 0.0), axis=1, keepdims=True).astype(jnp.int32)
    slot = (choice ^ at_ref[0]) * capacity + rank
    slot_ref[...] = slot
    rows = rows_ref[...]
    for k in range(parts):
        chosen = one_hot(slot - k * capacity, capacity)
        out_refs[k][...] = dot_tn(chosen, rows).astype(BF16)

    pair_len = low_ref.shape[1]
    pair_at = pl.multiple_of(at_ref[2] * pair_len, pair_len)
    segments = segment_ref[...]
    here = segment_ref[:, pl.ds(pair_at, pair_len)]
    low = jnp.zeros((1, pair_len), F32)
    for d in range(docs):
        start = jnp.sum(jnp.where(segments < d, 1.0, 0.0), axis=1, keepdims=True)
        low = low + jnp.where(here == d, start, 0.0)
    low = low.astype(jnp.int32) - (pair_at - pair_len)
    low_ref[...] = low
    tall_ref[...] = column(low)
    place = iota((1, LANES), 1)
    meta = jnp.where(place == 0, at_ref[1], 0)
    for t in range(pair_len // TILE):
        meta = jnp.where(place == 1 + t, low[:, t * TILE : t * TILE + 1] >> 8, meta)
    meta_ref[...] = meta


def route(at, ids, table, rows, segments, parts, capacity, docs):
    count, width = rows.shape
    pair_len = 2 * count
    outs = [shape((count, 1), jnp.int32), shape((1, pair_len), jnp.int32),
            shape((pair_len, 1), jnp.int32), shape((1, LANES), jnp.int32)]
    outs += [shape((capacity, width), BF16)] * parts
    return call(
        functools.partial(route_body, parts, capacity, docs), "route", outs,
        (at, ids, table, rows, segments), scalars=1,
    )


def vector(ref, at):
    lines = ref.shape[0] // 4
    return jnp.concatenate([ref[at * lines + j : at * lines + j + 1, :] for j in range(lines)], axis=1)


def project_body(skip, core_ref, own_ref, sib_ref, norm_ref, wq_ref, wk_ref, wv_ref, *refs):
    outs = refs[skip:-1]
    held_ref = refs[-1]
    step = pl.program_id(0)
    half = (pl.num_programs(0) - 1) // 2
    before = held_ref[(step + 1) % 2]
    outs[1][...] = dot(before, wk_ref[...]).astype(BF16)
    outs[2][...] = dot(before, wv_ref[...]).astype(BF16)
    if not skip:
        outs[3][...] = dot(before, wq_ref[...]).astype(BF16)
    rows = jnp.where(step < half, own_ref[...], sib_ref[...])
    normed, unused = norm_rows(rows.astype(F32))
    a = (normed * vector(norm_ref, 0) + vector(norm_ref, 1)).astype(BF16)
    held_ref[step % 2] = a
    outs[0][...] = a


def project(core, own, sib, norms, w_qkv, made):
    count, width = own.shape
    mine = width // 2
    half = count // TILE
    base = 0 if made else 2 * half

    def place(i, c):
        return ((i // half) ^ c[0]) * half + i % half

    def now(i, c):
        return (base + place(jnp.minimum(i, 2 * half - 1), c), 0)

    def then(i, c):
        return (base + place(jnp.maximum(i - 1, 0), c), 0)

    in_specs = [
        pl.BlockSpec((TILE, width), lambda i, c: (jnp.minimum(i, half - 1), 0)),
        pl.BlockSpec((TILE, width), lambda i, c: (jnp.clip(i - half, 0, half - 1), 0)),
        pl.BlockSpec(norms.shape, lambda i, c: (0, 0)),
    ] + [
        pl.BlockSpec((width, mine), functools.partial(lambda t, i, c: (0, 2 * t + c[0]), t))
        for t in range(3)
    ]
    args = [core, own, sib, norms, w_qkv, w_qkv, w_qkv]
    outs = [shape((4 * count, width), BF16)] + [shape((4 * count, mine), BF16)] * 2
    out_specs = [
        pl.BlockSpec((TILE, width), now),
        pl.BlockSpec((TILE, mine), then),
        pl.BlockSpec((TILE, mine), then),
    ]
    aliases = {}
    if made:
        in_specs += [pl.BlockSpec(memory_space=pl.ANY)] * 3
        aliases = {7: 0, 8: 1, 9: 2}
        args += list(made)
    else:
        outs.append(shape((2 * count, mine), BF16))
        out_specs.append(
            pl.BlockSpec((TILE, mine), lambda i, c: (place(jnp.maximum(i - 1, 0), c), 0))
        )
    return call(
        functools.partial(project_body, 3 if made else 0), "project", outs, args,
        grid=(2 * half + 1,), in_specs=in_specs, out_specs=out_specs, scalars=1, aliases=aliases,
        scratch=[pltpu.VMEM((2, TILE, width), BF16)],
    )


def masked_heads(block):
    lane = iota(block.shape, 1)
    zero = jnp.zeros((), block.dtype)
    return [
        jnp.where(lane < HEAD_DIM, block, zero),
        jnp.where(lane < HEAD_DIM, zero, block),
    ]


def flip(block):
    return block.astype(F32).T.astype(block.dtype)


def lanes_of(group):
    return slice(group * LANES, (group + 1) * LANES)


def put_heads(ref, block):
    for g in range(block.shape[1] // LANES):
        for h, part in enumerate(masked_heads(block[:, lanes_of(g)])):
            ref[2 * g + h] = part


def tile_mask(begin, low, high):
    place = begin + iota((TILE, TILE), 0)
    return (place >= low) & (place <= high)


def attend_body(meta_ref, q_ref, k_ref, v_ref, lo_ref, own_ref, sib_ref, all_ref, tall_ref,
                log_ref, heads_ref, acc_ref, rows_ref):
    total, mine = q_ref.shape
    half = total // 2
    heads = range(mine // HEAD_DIM)
    put_heads(heads_ref, q_ref[...] * jnp.asarray(HEAD_DIM**-0.5, BF16))
    core = meta_ref[0, 0]

    def tile(t, unused):
        at = pl.multiple_of(t * TILE, TILE)
        here = pl.ds(at, TILE)
        low = lo_ref[here, :]
        high = total + at + iota((TILE, 1), 0)
        acc_ref[...] = jnp.zeros_like(acc_ref)

        def step(j, state):
            begin = pl.multiple_of(j * TILE, TILE)
            there = pl.ds(begin, TILE)
            place = begin + iota((TILE, TILE), 1)
            allowed = (place >= low) & (place <= high)
            scores = [
                jnp.where(
                    allowed, dot_nt(heads_ref[h, here, :], k_ref[there, lanes_of(h // 2)]), LOWER
                )
                for h in heads
            ]
            tops = [
                jnp.maximum(state[2 * h], jnp.max(scores[h], axis=1, keepdims=True)) for h in heads
            ]
            shares = [jnp.exp(scores[h] - tops[h]) for h in heads]
            factors = [jnp.exp(state[2 * h] - tops[h]) for h in heads]
            sums = [
                state[2 * h + 1] * factors[h] + jnp.sum(shares[h], axis=1, keepdims=True)
                for h in heads
            ]
            more = [dot(shares[h].astype(BF16), v_ref[there, lanes_of(h // 2)]) for h in heads]
            for h in heads:
                acc_ref[h] = acc_ref[h] * factors[h] + more[h]
            return tuple(x for h in heads for x in (tops[h], sums[h]))

        first = (jnp.full((TILE, 1), LOW, F32), jnp.zeros((TILE, 1), F32))
        state = lax.fori_loop(
            meta_ref[0, 1 + t], total // TILE + t + 1, step, first * len(heads)
        )
        lane = iota((TILE, LANES), 1)
        logs = jnp.zeros((TILE, LANES), F32)
        for h in heads:
            logs = jnp.where(lane == h, state[2 * h] + jnp.log(state[2 * h + 1]), logs)
        log_ref[:, here] = logs.T[: log_ref.shape[0], :]
        for g in range(mine // LANES):
            left = acc_ref[2 * g] / state[4 * g + 1]
            right = acc_ref[2 * g + 1] / state[4 * g + 3]
            out = jnp.where(lane < HEAD_DIM, left, right)
            rows_ref[here, lanes_of(g)] = out
            tall_ref[lanes_of(g), here] = out.T
        return unused

    lax.fori_loop(0, total // TILE, tile, 0)
    all_ref[...] = rows_ref[...].astype(BF16)
    own_at = pl.multiple_of(core * half, half)
    sib_at = pl.multiple_of((1 - core) * half, half)
    own_ref[...] = rows_ref[pl.ds(own_at, half), :].astype(BF16)
    sib_ref[...] = rows_ref[pl.ds(sib_at, half), :].astype(BF16)


def attend(meta, q, k, v, low):
    total, mine = q.shape
    heads = mine // HEAD_DIM
    outs = [
        shape((total // 2, mine), BF16),
        shape((total // 2, mine), BF16),
        shape((total, mine), BF16),
        shape((mine, total), F32),
        shape((-(-heads // 8) * 8, total), F32),
    ]
    return call(
        attend_body, "attend", outs, (meta, q, k, v, low), scalars=1,
        scratch=[pltpu.VMEM((heads, total, LANES), BF16), pltpu.VMEM((heads, TILE, LANES), F32),
                 pltpu.VMEM((total, mine), F32)],
    )


def fetch(pairs, sems):
    copies = [pltpu.make_async_copy(a, b, sems.at[i]) for i, (a, b) in enumerate(pairs)]
    for copy in copies:
        copy.start()
    return [copy.wait for copy in copies]


def both_rows(core, own, sib, rows_ref):
    half = own.shape[0]
    return [
        (own, rows_ref.at[pl.ds(pl.multiple_of(core * half, half), half), :]),
        (sib, rows_ref.at[pl.ds(pl.multiple_of((1 - core) * half, half), half), :]),
    ]


def attend_back_body(meta_ref, q_hbm, k_hbm, v_hbm, own_hbm, sib_hbm, wo_hbm, tall_hbm, log_ref,
                     lo_ref, gq_ref, gk_ref, gv_ref, rows_ref, heads_ref, grads_ref, delta_ref,
                     kt_ref, gqt_ref, gks_ref, gvs_ref, q_ref, k_ref, v_ref, wo_ref, tall_ref,
                     sems):
    total, mine = q_ref.shape
    heads = mine // HEAD_DIM
    core = meta_ref[0, 0]
    mine_at = pl.ds(pl.multiple_of(core * mine, mine), mine)
    waits = fetch(
        both_rows(core, own_hbm, sib_hbm, rows_ref)
        + [(wo_hbm.at[mine_at, :], wo_ref), (tall_hbm, tall_ref), (q_hbm, q_ref), (k_hbm, k_ref),
           (v_hbm, v_ref)],
        sems,
    )
    gks_ref[...] = jnp.zeros_like(gks_ref)
    gvs_ref[...] = jnp.zeros_like(gvs_ref)
    gqt_ref[...] = jnp.zeros_like(gqt_ref)
    for wait in waits[:4]:
        wait()
    weights = wo_ref[...]
    for t in range(total // TILE):
        here = slice(t * TILE, (t + 1) * TILE)
        grads = dot_nt(rows_ref[here, :], weights).astype(BF16)
        turned = grads.astype(F32).T * tall_ref[:, here]
        for h in range(heads):
            span = slice(h * HEAD_DIM, (h + 1) * HEAD_DIM)
            delta_ref[h : h + 1, here] = jnp.sum(turned[span, :], axis=0, keepdims=True)
        for g in range(mine // LANES):
            for h, part in enumerate(masked_heads(grads[:, lanes_of(g)])):
                grads_ref[2 * g + h, here, :] = part
    waits[4]()
    put_heads(heads_ref, q_ref[...] * jnp.asarray(HEAD_DIM**-0.5, BF16))
    waits[5]()
    kt_ref[...] = flip(k_ref[...])
    waits[6]()

    def tile(t, unused):
        at = pl.multiple_of(t * TILE, TILE)
        here = pl.ds(at, TILE)
        low = lo_ref[:, here]
        high = total + at + iota((1, TILE), 1)

        logs = [log_ref[h : h + 1, here] for h in range(heads)]
        deltas = [delta_ref[h : h + 1, here] for h in range(heads)]

        def step(j, carry):
            begin = pl.multiple_of(j * TILE, TILE)
            there = pl.ds(begin, TILE)
            allowed = tile_mask(begin, low, high)
            every = range(heads)
            queries = [heads_ref[h, here, :] for h in every]
            grads = [grads_ref[h, here, :] for h in every]
            scores = [dot_nt(k_ref[there, lanes_of(h // 2)], queries[h]) for h in every]
            grad_soft = [dot_nt(v_ref[there, lanes_of(h // 2)], grads[h]) for h in every]
            soft = [jnp.exp(jnp.where(allowed, scores[h], LOWER) - logs[h]) for h in every]
            grad_scores = [(soft[h] * (grad_soft[h] - deltas[h])).astype(BF16) for h in every]
            soft = [s.astype(BF16) for s in soft]
            gv = [dot(soft[h], grads[h]) for h in every]
            gk = [dot(grad_scores[h], queries[h]) for h in every]
            gq = [
                dot(kt_ref[h * HEAD_DIM : (h + 1) * HEAD_DIM, there], grad_scores[h])
                for h in every
            ]
            for g in range(heads // 2):
                gvs_ref[there, lanes_of(g)] += gv[2 * g] + gv[2 * g + 1]
                gks_ref[there, lanes_of(g)] += gk[2 * g] + gk[2 * g + 1]
            for h in every:
                gqt_ref[h * HEAD_DIM : (h + 1) * HEAD_DIM, here] += gq[h]
            return carry

        return lax.fori_loop(meta_ref[0, 1 + t], total // TILE + t + 1, step, unused)

    lax.fori_loop(0, total // TILE, tile, 0)
    gqt = gqt_ref[...] * (HEAD_DIM**-0.5)
    gq_ref[...] = gqt.T.astype(BF16)
    gk_ref[...] = gks_ref[...].astype(BF16)
    gv_ref[...] = gvs_ref[...].astype(BF16)


def attend_back(meta, q, k, v, own, sib, w_out, tall, logs, low):
    total, mine = q.shape
    width = own.shape[1]
    heads = mine // HEAD_DIM
    outs = [
        shape((total, mine), BF16),
        shape((2 * total, mine), BF16),
        shape((2 * total, mine), BF16),
    ]
    return call(
        attend_back_body, "attend_back", outs,
        (meta, q, k, v, own, sib, w_out, tall, logs, low), scalars=1,
        in_specs=[pl.BlockSpec(memory_space=pl.ANY)] * 7 + [pl.BlockSpec(memory_space=pltpu.VMEM)] * 2,
        scratch=[pltpu.VMEM((total, width), BF16), pltpu.VMEM((heads, total, LANES), BF16),
                 pltpu.VMEM((heads, total, LANES), BF16), pltpu.VMEM(logs.shape, F32),
                 pltpu.VMEM((mine, 2 * total), BF16), pltpu.VMEM((mine, total), F32),
                 pltpu.VMEM((2 * total, mine), F32), pltpu.VMEM((2 * total, mine), F32),
                 pltpu.VMEM(q.shape, BF16), pltpu.VMEM(k.shape, BF16), pltpu.VMEM(v.shape, BF16),
                 pltpu.VMEM((mine, width), BF16), pltpu.VMEM(tall.shape, F32),
                 pltpu.SemaphoreType.DMA((7,))],
    )


def dense_body(subs, sub, chip_ref, a_hbm, gq_hbm, gk_hbm, gv_hbm, all_hbm, own_hbm, sib_hbm,
               *refs):
    piece_refs = refs[:4]
    dense_ref, a_ref, gq_ref, gk_ref, gv_ref, all_ref, rows_ref, sems = refs[4:]
    total, mine = gq_ref.shape
    width = rows_ref.shape[1]
    lines = width // subs
    quarter = subs * sub
    waits = fetch(
        both_rows(chip_ref[0], own_hbm, sib_hbm, rows_ref)
        + [(all_hbm, all_ref), (gq_hbm, gq_ref), (a_hbm, a_ref), (gk_hbm, gk_ref), (gv_hbm, gv_ref)],
        sems,
    )

    def put(kind, turned):
        for j in range(mine // LANES):
            block = turned[lanes_of(j), :].T.astype(BF16)
            for at in range(subs):
                first = kind * quarter + at * sub + j * lines
                dense_ref[first : first + lines, :] = block[at * lines : (at + 1) * lines, :]

    for wait in waits[:3]:
        wait()
    put(3, dot_tn(all_ref[...], rows_ref[...]))
    waits[3]()
    waits[4]()
    put(0, dot_tn(gq_ref[...], a_ref[total:, :]))
    waits[5]()
    put(1, dot_tn(gk_ref[...], a_ref[...]))
    waits[6]()
    put(2, dot_tn(gv_ref[...], a_ref[...]))
    spare = sub - mine // LANES * lines
    if spare:
        for at in range(4 * subs):
            dense_ref[(at + 1) * sub - spare : (at + 1) * sub, :] = jnp.zeros((spare, LANES), BF16)
    for p in range(2):
        side = chip_ref[1 + p]
        for r, which in enumerate((side, 1 - side)):
            for at in range(subs):
                from_at = pl.multiple_of((2 * p + which) * quarter + at * sub, 16)
                to_at = pl.multiple_of((at ^ chip_ref[3 + p]) * sub, 16)
                piece_refs[2 * p + r][pl.ds(to_at, sub), :] = dense_ref[pl.ds(from_at, sub), :]


def dense_pieces(chip, a, gq, gk, gv, attn_all, own, sib, subs, sub):
    return call(
        functools.partial(dense_body, subs, sub), "dense",
        [shape((subs * sub, LANES), BF16)] * 4,
        (chip, a, gq, gk, gv, attn_all, own, sib), scalars=1,
        in_specs=[pl.BlockSpec(memory_space=pl.ANY)] * 7,
        scratch=[pltpu.VMEM((4 * subs * sub, LANES), BF16), pltpu.VMEM(a.shape, BF16),
                 pltpu.VMEM(gq.shape, BF16), pltpu.VMEM(gk.shape, BF16),
                 pltpu.VMEM(gv.shape, BF16), pltpu.VMEM(attn_all.shape, BF16),
                 pltpu.VMEM((2 * own.shape[0], own.shape[1]), BF16),
                 pltpu.SemaphoreType.DMA((7,))],
    )


def lift_body(parts, capacity, core_ref, own_ref, other_ref, w_ref, x_ref, norm_ref, slot_ref,
              resid_ref, *out_refs):
    mine = own_ref.shape[1]
    core = core_ref[0]
    own_w = w_ref[pl.ds(pl.multiple_of(core * mine, mine), mine), :]
    other_w = w_ref[pl.ds(pl.multiple_of((1 - core) * mine, mine), mine), :]
    resid = x_ref[...].astype(F32) + (dot(own_ref[...], own_w) + dot(other_ref[...], other_w))
    resid_ref[...] = resid
    normed, unused = norm_rows(resid)
    rows = (normed * vector(norm_ref, 2) + vector(norm_ref, 3)).astype(BF16)
    slot = slot_ref[...]
    for k in range(parts):
        chosen = one_hot(slot - k * capacity, capacity)
        out_refs[k][...] = dot_tn(chosen, rows).astype(BF16)


def lift(core, own, other, w_out, x, norms, slot, parts, capacity):
    count, width = x.shape
    outs = [shape((count, width), F32)] + [shape((capacity, width), BF16)] * parts
    return call(
        functools.partial(lift_body, parts, capacity), "lift", outs,
        (core, own, other, w_out, x, norms, slot),
        scalars=1, flops=2 * count * width * (width + parts * capacity),
    )


GATE_A = math.sqrt(2.0 / math.pi)
GATE_B = 0.044715


def expert_body(sub, rows_ref, grad_ref, up_ref, down_ref, tall_ref, pre_ref, back_ref, out_ref,
                turned_ref, back_acc, out_acc):
    step = pl.program_id(0)

    @pl.when(step == 0)
    def _():
        back_acc[...] = jnp.zeros_like(back_acc)
        out_acc[...] = jnp.zeros_like(out_acc)
        turned_ref[...] = flip(rows_ref[...])

    parts = [slice(s * sub, (s + 1) * sub) for s in range(down_ref.shape[0] // sub)]
    pres = [dot(rows_ref[...], up_ref[:, part]) for part in parts]
    grads = [dot_nt(grad_ref[...], down_ref[part, :]) for part in parts]
    hids, slopes = [], []
    for pre in pres:
        square = pre * pre
        bend = jnp.tanh(GATE_A * (pre + GATE_B * (square * pre)))
        half = 0.5 + 0.5 * bend
        hids.append(pre * half)
        slopes.append(
            half + (pre * (1.0 - bend * bend)) * (0.5 * GATE_A + (1.5 * GATE_A * GATE_B) * square)
        )
    low = jnp.concatenate([(g * s).astype(BF16) for g, s in zip(grads, slopes)], axis=1)
    back_acc[...] += dot_nt(low, up_ref[...])
    out_acc[...] += dot(jnp.concatenate([h.astype(BF16) for h in hids], axis=1), down_ref[...])
    pre_ref[...] = low
    for part, hid in zip(parts, hids):
        tall_ref[part, :] = hid.T.astype(BF16)

    @pl.when(step == pl.num_programs(0) - 1)
    def _():
        back_ref[...] = back_acc[...].astype(BF16)
        out_ref[...] = out_acc[...].astype(BF16)


def expert(rows, grads, w_up, w_down, sub=256):
    count, width = rows.shape
    hidden = w_up.shape[1]
    block = width
    const = pl.BlockSpec((count, width), lambda j: (0, 0))
    return call(
        functools.partial(expert_body, sub), "expert",
        [shape((hidden, count), BF16), shape((count, hidden), BF16), shape((count, width), BF16),
         shape((count, width), BF16), shape((width, count), BF16)],
        (rows, grads, w_up, w_down), grid=(hidden // block,),
        in_specs=[const, const, pl.BlockSpec((width, block), lambda j: (0, j)),
                  pl.BlockSpec((block, width), lambda j: (j, 0))],
        out_specs=[pl.BlockSpec((block, count), lambda j: (j, 0)),
                   pl.BlockSpec((count, block), lambda j: (0, j)), const, const,
                   pl.BlockSpec((width, count), lambda j: (0, 0))],
        scratch=[pltpu.VMEM((count, width), F32)] * 2,
    )


def expert_grad_body(parts, subs, chip_ref, *refs):
    turned, grads, talls, pres = (refs[parts * t : parts * (t + 1)] for t in range(4))
    *outs, held_ref, sems = refs[4 * parts :]
    width = held_ref.shape[2]
    lines = width // subs
    step = pl.program_id(0)
    steps = len(outs)
    slot = step % 2

    def copy(t, at):
        return pltpu.make_async_copy(held_ref.at[at], outs[t], sems.at[at])

    @pl.when(step >= 2)
    def _():
        copy(0, slot).wait()

    def product(left, right):
        out = None
        for a, b in zip(left, right):
            more = dot(a[...], b[...])
            out = more if out is None else out + more
        return out.astype(BF16)

    half = steps // 2
    side, mask = chip_ref[1 + step % half], chip_ref[3 + step % half]
    pairs = ((product(turned, pres), side == 0), (product(talls, grads), side == 1))
    for value, stays in pairs:
        base = jnp.where(stays, width, 0)
        for at in range(subs):
            first = pl.multiple_of(base + (at ^ mask) * lines, 16)
            held_ref[slot, pl.ds(first, lines), :] = value[at * lines : (at + 1) * lines, :]

    for t in range(steps):

        @pl.when(step == t)
        def _(t=t):
            copy(t, t % 2).start()

    @pl.when(step == steps - 1)
    def _():
        copy(0, 0).wait()
        copy(0, 1).wait()


def expert_grad(chip, turned, grads, talls, pres, subs):
    parts = len(grads)
    count, width = grads[0].shape
    blocks = talls[0].shape[0] // width
    half = blocks // 2

    def column(i, m):
        return jnp.where(i < half, (1 - m[0]) * half, m[0] * half - half) + i

    const = lambda dims: pl.BlockSpec(dims, lambda i, m: (0, 0))
    return call(
        functools.partial(expert_grad_body, parts, subs), "expert_grad",
        [shape((2 * width, width), BF16)] * blocks,
        (chip, *turned, *grads, *talls, *pres), grid=(blocks,), scalars=1,
        in_specs=[const((width, count))] * parts + [const((count, width))] * parts
        + [pl.BlockSpec((width, count), lambda i, m: (column(i, m), 0))] * parts
        + [pl.BlockSpec((count, width), lambda i, m: (0, column(i, m)))] * parts,
        out_specs=[pl.BlockSpec(memory_space=pl.ANY)] * blocks,
        scratch=[pltpu.VMEM((2, 2 * width, width), BF16), pltpu.SemaphoreType.DMA((2,))],
    )


def widen_body(skip, meta_ref, *refs):
    pairs, (up_out, down_out) = refs[:4], refs[4 + skip :]
    second = pl.program_id(0) >= pl.num_programs(0) // 2
    first = meta_ref[1 + pl.program_id(0) // (pl.num_programs(0) // 2)] == 0
    mine = jnp.where(second, pairs[2][...], pairs[0][...])
    theirs = jnp.where(second, pairs[3][...], pairs[1][...])
    up_out[...] = jnp.where(first, mine, theirs).astype(F32)
    down_out[...] = jnp.where(first, theirs, mine).astype(F32)


def widen(core, sides, masks, mine, theirs, made, hidden, subs):
    width = mine[0].shape[1]
    rows = width // subs
    meta = jnp.stack([core, *sides, *masks]).astype(jnp.int32)

    def index(p):
        def at(i, m):
            here = jnp.clip(i - p * subs, 0, subs - 1)
            return (here ^ m[3 + p], 0)

        return at

    blocks = [pl.BlockSpec((rows, width), index(p)) for p in (0, 0, 1, 1)]
    column = lambda i, m: 2 * m[0] + i // subs
    return call(
        functools.partial(widen_body, len(made)), "widen",
        [shape((width, hidden), F32), shape((hidden, width), F32)],
        (meta, mine[0], theirs[0], mine[1], theirs[1], *made), grid=(2 * subs,), scalars=1,
        in_specs=blocks + [pl.BlockSpec(memory_space=pl.ANY)] * len(made),
        out_specs=[pl.BlockSpec((rows, width), lambda i, m: (i % subs, column(i, m))),
                   pl.BlockSpec((rows, width), lambda i, m: (column(i, m) * subs + i % subs, 0))],
        aliases={5: 0, 6: 1} if made else None,
    )


def collect(slot, part_refs):
    total = None
    for k, ref in enumerate(part_refs):
        capacity = ref.shape[0]
        more = dot(one_hot(slot - k * capacity, capacity), ref[...])
        total = more if total is None else total + more
    return total


def lower_body(parts, slot_ref, resid_ref, cot_ref, norm_ref, *refs):
    grads = collect(slot_ref[...], refs[:parts])
    gr_ref, low_ref, gain_out, bias_out = refs[parts:]
    normed, scale = norm_rows(resid_ref[...])
    gain_out[...] = jnp.sum(grads * normed, axis=0, keepdims=True)
    bias_out[...] = jnp.sum(grads, axis=0, keepdims=True)
    gr = cot_ref[...].astype(F32) + norm_back(grads * vector(norm_ref, 2), normed, scale)
    gr_ref[...] = gr
    low_ref[...] = gr.astype(BF16)


def lower(slot, resid, cot, norms, back):
    parts = len(back)
    count, width = resid.shape
    outs = [shape((count, width), F32), shape((count, width), BF16),
            shape((1, width), F32), shape((1, width), F32)]
    return call(
        functools.partial(lower_body, parts), "lower", outs, (slot, resid, cot, norms, *back),
        flops=2 * count * width * parts * back[0].shape[0],
    )


def finish_body(slot_ref, resid_ref, *refs):
    refs[-1][...] = (resid_ref[...] + collect(slot_ref[...], refs[:-1])).astype(BF16)


def finish(slot, resid, parts):
    return call(finish_body, "finish", shape(resid.shape, BF16), (slot, resid, *parts))


def project_back_body(half, core_ref, own_ref, sib_ref, hal_ref, has_ref, gq_ref, gk_ref, gv_ref,
                      wq_ref, wk_ref, wv_ref, keep_ref, send_ref, halo_ref, gain_ref, bias_ref):
    step = pl.program_id(0)
    rows = jnp.where(
        step < 2 * half,
        jnp.where(step < half, own_ref[...], sib_ref[...]),
        jnp.where(step < 3 * half, hal_ref[...], has_ref[...]),
    )
    normed, unused = norm_rows(rows.astype(F32))
    here = step < 2 * half
    ga = dot_nt(gk_ref[...], wk_ref[...]) + dot_nt(gv_ref[...], wv_ref[...])
    gq = jnp.where(here, gq_ref[...], jnp.zeros_like(gq_ref))
    ga = ga + dot_nt(gq, wq_ref[...])

    @pl.when(step == 0)
    def _():
        gain_ref[...] = jnp.zeros_like(gain_ref)
        bias_ref[...] = jnp.zeros_like(bias_ref)

    gain_ref[...] += jnp.sum(ga * normed, axis=0, keepdims=True)
    bias_ref[...] += jnp.sum(ga, axis=0, keepdims=True)

    @pl.when(step < half)
    def _():
        keep_ref[...] = ga

    @pl.when((step // half) % 2 == 1)
    def _():
        send_ref[...] = ga.astype(BF16)

    @pl.when(step // half == 2)
    def _():
        halo_ref[...] = ga


def project_back(core, own, sib, hal, has, gq, gk, gv, w_qkv):
    count, width = own.shape
    mine = gq.shape[1]
    half = count // TILE

    def at(t):
        return lambda i, c: (jnp.clip(i - t * half, 0, half - 1), 0)

    def place(i, c):
        return jnp.where(i < 2 * half, 2 * half, 0) + (((i // half) % 2) ^ c[0]) * half + i % half

    def sent(i, c):
        late = half + jnp.clip(i - 3 * half, 0, half - 1)
        return (jnp.where(i < 2 * half, jnp.clip(i - half, 0, half - 1), late), 0)

    row = pl.BlockSpec((1, width), lambda i, c: (0, 0))
    in_specs = [pl.BlockSpec((TILE, width), at(t)) for t in range(4)] + [
        pl.BlockSpec((TILE, mine), lambda i, c: (jnp.maximum(place(i, c) - 2 * half, 0), 0)),
        pl.BlockSpec((TILE, mine), lambda i, c: (place(i, c), 0)),
        pl.BlockSpec((TILE, mine), lambda i, c: (place(i, c), 0)),
    ] + [
        pl.BlockSpec((width, mine), functools.partial(lambda t, i, c: (0, 2 * t + c[0]), t))
        for t in range(3)
    ]
    return call(
        functools.partial(project_back_body, half), "project_back",
        [shape((count, width), F32), shape((2 * count, width), BF16), shape((count, width), F32),
         shape((1, width), F32), shape((1, width), F32)],
        (core, own, sib, hal, has, gq, gk, gv, w_qkv, w_qkv, w_qkv),
        grid=(4 * half,), in_specs=in_specs, scalars=1,
        out_specs=[pl.BlockSpec((TILE, width), at(0)), pl.BlockSpec((TILE, width), sent),
                   pl.BlockSpec((TILE, width), at(2)), row, row],
        flops=20 * count * width * mine,
    )


def close_body(x_ref, gr_ref, keep_ref, near_ref, far_ref, norm_ref, out_ref):
    ga = keep_ref[...] + near_ref[...].astype(F32) + far_ref[...].astype(F32)
    normed, scale = norm_rows(x_ref[...].astype(F32))
    out_ref[...] = gr_ref[...] + norm_back(ga * vector(norm_ref, 0), normed, scale)


def close(x, gr, keep, near, far, norms):
    count, width = x.shape
    block = pl.BlockSpec((TILE, width), lambda i: (i, 0))
    return call(
        close_body, "close", shape((count, width), F32), (x, gr, keep, near, far, norms),
        grid=(count // TILE,),
        in_specs=[block] * 5 + [pl.BlockSpec(norms.shape, lambda i: (0, 0))], out_specs=block,
    )


def swap(block, axis, distance):
    return lax.ppermute(block, axis, [(i, i ^ distance) for i in range(lax.axis_size(axis))])


def trade(block, axis):
    return lax.all_to_all(block, axis, split_axis=0, concat_axis=0, tiled=True)


def shift(block, axis, distance):
    size = lax.axis_size(axis)
    route = [(i, i + distance) for i in range(size) if 0 <= i + distance < size]
    return lax.ppermute(block, axis, route)


def total(terms):
    return sum(t.astype(F32) for t in terms).astype(BF16)


def add(a, b):
    return total([a, b])


def at_index(block, index):
    return lax.dynamic_index_in_dim(block, index, 0, keepdims=False)


def scatter_steps(pieces, orders):
    pairs = list(pieces)
    for s in range(len(orders[0])):
        arrived = yield [(goes, "seq", bits[s]) for (stays, goes), bits in zip(pairs, orders)]
        terms = [stays + [got] for (stays, goes), got in zip(pairs, arrived)]
        if s + 1 < len(orders[0]):
            half = terms[0][0].shape[0] // 2
            pairs = [
                ([total([t[half:] for t in terms_p])], total([t[:half] for t in terms_p]))
                for terms_p in terms
            ]
    return [total(terms_p) for terms_p in terms]


def gather_steps(parts, orders):
    parts = list(parts)
    for s in reversed(range(1, len(orders[0]))):
        arrived = yield [(part, "seq", bits[s]) for part, bits in zip(parts, orders)]
        parts = [jnp.concatenate([got, part], axis=0) for got, part in zip(arrived, parts)]
    return parts


def dense_steps(pieces, orders):
    sources = lax.axis_size("exp")
    parts = yield from scatter_steps(pieces, orders)
    joined = jnp.stack([p.reshape(sources, -1, LANES) for p in parts], axis=1)
    (got,) = yield [(joined, "exp", 0)]
    own = jnp.sum(got.astype(F32), axis=0).astype(BF16)
    (got,) = yield [(jnp.broadcast_to(own, (sources, *own.shape)), "exp", 0)]
    parts = [got[:, p].reshape(-1, LANES) for p in range(len(orders))]
    return (yield from gather_steps(parts, orders))


def expert_steps(pieces, orders):
    parts = yield from scatter_steps(pieces, orders)
    return (yield from gather_steps(parts, orders))


def one_step(sends):
    return (yield sends)


def across(parts, orders):
    return Stream(one_step([(part, "seq", bits[0]) for part, bits in zip(parts, orders)]))


def beside(parts):
    return Stream(one_step([(part, "seq", 1) for part in parts]))


def small_steps(value, hops):
    for hop in hops:
        (got,) = yield [(value, *hop)]
        value = value + got
    return value


class Stream:
    def __init__(self, steps):
        self.steps = steps
        self.result = None
        self.sent = []
        self.go(None)

    def go(self, arrived):
        try:
            sends = self.steps.send(arrived)
        except StopIteration as stop:
            self.sent, self.raw, self.result = [], [], stop.value
        else:
            self.raw = [send[0] for send in sends]
            self.sent = [swap(*send) if send[2] else trade(*send[:2]) for send in sends]


def meet(streams, others=()):
    streams = [stream for stream in streams if stream.sent]
    arrived, others = lax.optimization_barrier(([stream.sent for stream in streams], others))
    before = []
    for stream, got in zip(streams, arrived):
        stream.go(after(got, before) if before else got)
        before = before + stream.raw
    return others


def spread_columns_body(cols, chip_ref, *refs):
    out_ref = refs[-1]
    first = chip_ref[0] == 0
    own, sib = refs[:4], refs[4:8]
    picks = [
        (0, chip_ref[1] == 0, 0, 1),
        (1, chip_ref[1] == 1, 0, 1),
        (2, chip_ref[2] == 0, 2, 3),
    ]
    for kind, mine, here, there in picks:
        for j in range(cols):
            a, b = (jnp.where(mine, t[here][0, j], t[there][0, j]).astype(F32) for t in (own, sib))
            left = 2 * kind * cols + j
            out_ref[:, lanes_of(left)] = jnp.where(first, a, b)
            out_ref[:, lanes_of(left + cols)] = jnp.where(first, b, a)


def spread_rows_body(chip_ref, *refs):
    out_ref = refs[-1]
    own = pl.program_id(0) == chip_ref[0]
    mine = chip_ref[2] == 1
    subs, cols, lines, unused = refs[0].shape
    for at in range(subs):
        from_at = at ^ chip_ref[4]
        for j in range(cols):
            a, b = (
                jnp.where(mine, refs[t][from_at, j], refs[t + 1][from_at, j]) for t in (0, 2)
            )
            out_ref[lanes_of(j), at * lines : (at + 1) * lines] = (
                jnp.where(own, a, b).astype(F32).T
            )


def spread(chip, own, sib, width, mine, subs):
    cols = mine // LANES
    lines = width // subs
    block = math.gcd(lines, 192)

    def view(t):
        return t.reshape(subs, -1, LANES)[:, : cols * lines].reshape(subs, cols, lines, LANES)

    def part(p):
        def index(i, m):
            return ((i * block // lines) ^ m[3 + p], 0, i % (lines // block), 0)

        return pl.BlockSpec((1, cols, block, LANES), index)

    parts = [[view(t) for pair in side for t in pair] for side in (own, sib)]
    grad_qkv = call(
        functools.partial(spread_columns_body, cols), "spread_columns",
        shape((width, 3 * width), F32), (chip, *parts[0], *parts[1]), grid=(width // block,),
        scalars=1, in_specs=[part(0), part(0), part(1), part(1)] * 2,
        out_specs=pl.BlockSpec((block, 3 * width), lambda i, m: (i, 0)),
    )
    whole = pl.BlockSpec((subs, cols, lines, LANES), lambda i, m: (0, 0, 0, 0))
    grad_out = call(
        spread_rows_body, "spread_rows", shape((width, width), F32),
        (chip, *parts[0][2:], *parts[1][2:]), grid=(2,), scalars=1, in_specs=[whole] * 4,
        out_specs=pl.BlockSpec((mine, width), lambda i, m: (i, 0)),
    )
    return grad_qkv, grad_out


def on_device(
    layer_input,
    token_ids,
    segment_ids,
    hash_table,
    first_gain,
    first_bias,
    second_gain,
    second_bias,
    w_qkv,
    w_out,
    w_up,
    w_down,
    cotangent,
):
    x = layer_input[0]
    cot = cotangent[0]
    local_len, width = x.shape
    mine = width // 2
    sources = lax.axis_size("exp")
    ring = lax.axis_size("seq")
    capacity = 2 * local_len // sources
    seq_at = lax.axis_index("seq")
    exp_at = lax.axis_index("exp")
    core = (seq_at % 2).astype(jnp.int32)
    core_arg = core.reshape(1)
    norms = jnp.concatenate([first_gain, first_bias, second_gain, second_bias])
    norms = norms.reshape(-1, LANES)
    up, down = w_up[0], w_down[0]

    hal = shift(x, "seq", 2)
    sib = swap(x, "seq", 1)

    place = exp_at.astype(jnp.int32).reshape(1)
    at = jnp.stack([exp_at, core, seq_at // 2]).astype(jnp.int32)
    lines = -(-hash_table.shape[0] // (8 * LANES)) * 8
    table = jnp.pad(hash_table, (0, lines * LANES - hash_table.shape[0])).reshape(lines, LANES)
    docs = 2 * ring * local_len // DOC_MOST
    slot, low, low_tall, meta, *grad_out = route(
        at, token_ids, table, cot, segment_ids, sources, capacity, docs
    )
    grad_in = [grad_out[0]] + [swap(grad_out[k], "exp", k) for k in range(1, sources)]

    *made, q = project(core_arg, x, after(sib, slot), norms, w_qkv, None)
    hal = after(hal, q)
    has = swap(hal, "seq", 1)
    a, k, v = project(core_arg, hal, has, norms, w_qkv, made)
    attn_own, attn_give, attn_all, attn_tall, logs = attend(meta, q, k, v, low_tall)
    attn_other = swap(attn_give, "seq", 1)
    resid, *rows_out = lift(
        core_arg, attn_own, after(attn_other, grad_in), w_out, x, norms, slot, sources, capacity
    )
    rows_in = [rows_out[0]] + [swap(rows_out[k], "exp", k) for k in range(1, sources)]
    talls, pres, backs, outs, turned = [], [], [], [], []
    for k_at in range(sources):
        tall, pre, back, out, turn = expert(rows_in[k_at], grad_in[k_at], up, down)
        talls.append(tall)
        pres.append(pre)
        outs.append(out)
        turned.append(turn)
        backs.append(back if k_at == 0 else swap(back, "exp", k_at))
        if k_at + 1 < sources:
            rows_in[k_at + 1] = after(rows_in[k_at + 1], back)
    bits = [1 << b for b in range(1, ring.bit_length() - 1)]
    orders = [bits, bits[::-1]]
    sides = [(seq_at // o[0]) % 2 for o in orders]
    subs = ring // 4
    masks = [
        sum((1 - (seq_at // bit) % 2) << (len(o) - 2 - at) for at, bit in enumerate(o[1:]))
        for o in orders
    ]
    chip = jnp.stack([core, *sides, *masks]).astype(jnp.int32)

    turned, backs[:-2] = lax.optimization_barrier((turned, backs[:-2]))
    blocks = expert_grad(chip, turned, grad_in, talls, pres, subs)
    given, kept = blocks[:2], blocks[2:]
    given, backs[-2] = lax.optimization_barrier((given, backs[-2]))
    given, backs[-1] = lax.optimization_barrier((given, backs[-1]))
    got = [swap(t, "seq", 1) for t in given]
    gr, gattn, gain_two_grad, bias_two_grad = lower(slot, resid, cot, norms, backs)
    got = after(got, gattn)
    goes = [add(kept[p][:width], got[p][:width]) for p in range(2)]
    stays = [[kept[p][width:], got[p][width:]] for p in range(2)]
    experts = Stream(expert_steps(list(zip(stays, goes)), orders))
    outs = after(outs, goes)
    returned = [outs[0]] + [swap(outs[k], "exp", k) for k in range(1, sources)]
    gattn_sib = swap(gattn, "seq", 1)
    unit = sources * 16
    sub = -(-(mine // LANES * width // subs) // unit) * unit
    gq, gk, gv = attend_back(
        meta, q, k, v, gattn, after(gattn_sib, goes), w_out, attn_tall, logs, low
    )
    pieces = dense_pieces(chip, a, gq, gk, gv, attn_all, gattn, gattn_sib, subs, sub)
    pieces, returned = lax.optimization_barrier((pieces, returned))
    dense = Stream(
        dense_steps([([pieces[0]], pieces[1]), ([pieces[2]], pieces[3])], orders)
    )
    (gq,) = meet([experts], (after(gq, pieces),))
    keep, give, halo, gain_one_grad, bias_one_grad = project_back(
        core_arg, x, sib, hal, has, gq, gk, gv, w_qkv
    )
    small = jnp.concatenate([gain_one_grad, bias_one_grad, gain_two_grad, bias_two_grad], axis=0)
    (give,) = meet([dense, experts], (give,))
    near = swap(give, "seq", 1)
    (near,) = meet([dense], (near,))
    for rest in range(len(bits) - 2):
        meet([dense, experts])
    far = shift(add(halo, near[local_len:]), "seq", -2)
    hops = [("seq", bit) for bit in bits + [1]]
    hops += [("exp", 1 << b) for b in range(sources.bit_length() - 1)]
    small = Stream(small_steps(small, hops))
    layer_output = finish(slot, resid, returned)
    (layer_output,) = meet([dense, experts, small], (layer_output,))
    for rest in range(len(bits) - 2):
        meet([experts])
    own_parts = experts.result
    other_chip = across(own_parts, orders)
    other_core = beside(after(own_parts, layer_output))
    meet([dense, other_chip, other_core, small])
    other_both = beside(other_chip.result)
    hidden = down.shape[0]
    made = widen(core, sides, masks, own_parts, other_chip.result, (), hidden, subs)
    while dense.result is None:
        made = meet([dense, other_both, small], made)
    own_dense = dense.result
    dense_chip, dense_core = across(own_dense, orders), beside(own_dense)
    made = widen(
        1 - core, sides, masks, other_core.result, other_both.result, made, hidden, subs
    )
    grad_w_up, grad_w_down = meet([dense_chip, dense_core, small], made)
    dense_both = beside(dense_chip.result)
    meet([dense_both, small])
    while small.sent:
        small.go(small.sent)
    grad_w_qkv, grad_w_out = spread(
        chip, list(zip(own_dense, dense_chip.result)),
        list(zip(dense_core.result, dense_both.result)), width, mine, subs,
    )
    grad_input = close(x, gr, keep, near, after(far, grad_w_qkv), norms)
    small = small.result
    return (
        layer_output[None],
        grad_input[None],
        grad_w_qkv,
        grad_w_out,
        small[0],
        small[1],
        small[2],
        small[3],
        grad_w_up[None],
        grad_w_down[None],
    )


def solution(mesh):
    in_specs = (
        P("exp", "seq", None),
        P("exp", "seq"),
        P("exp", None),
        P(),
        P(),
        P(),
        P(),
        P(),
        P(),
        P(),
        P("exp", None, None),
        P("exp", None, None),
        P("exp", "seq", None),
    )
    out_specs = (
        P("exp", "seq", None),
        P("exp", "seq", None),
        P(),
        P(),
        P(),
        P(),
        P(),
        P(),
        P("exp", None, None),
        P("exp", None, None),
    )
    return jax.shard_map(
        on_device, mesh=mesh, in_specs=in_specs, out_specs=out_specs, check_vma=False
    )
```

```python
import functools
import math

import jax
import jax.numpy as jnp
from jax import lax
from jax.experimental import pallas as pl
from jax.experimental.pallas import tpu as pltpu
from jax.sharding import PartitionSpec as P

HEADS = 12
HEAD_DIM = 64
DOC_MOST = 1024
EPSILON = 1e-05
LOW = -1e30
LOWER = -2e30
LANES = 128
TILE = 256
F32 = jnp.float32
BF16 = jnp.bfloat16
MIB = 1 << 20
COST = 1


def dot(a, b):
    return lax.dot_general(a, b, (((1,), (0,)), ((), ())), preferred_element_type=F32)


def dot_nt(a, b):
    return lax.dot_general(a, b, (((1,), (1,)), ((), ())), preferred_element_type=F32)


def dot_tn(a, b):
    return lax.dot_general(a, b, (((0,), (0,)), ((), ())), preferred_element_type=F32)


def iota(shape, axis):
    return lax.broadcasted_iota(jnp.int32, shape, axis)


def one_hot(ids, width):
    return jnp.where(iota((ids.shape[0], width), 1) == ids, 1.0, 0.0).astype(BF16)


def norm_rows(values):
    center = values - jnp.mean(values, axis=-1, keepdims=True)
    scale = lax.rsqrt(jnp.mean(center * center, axis=-1, keepdims=True) + EPSILON)
    return center * scale, scale


def norm_back(grad, normed, scale):
    inner = jnp.mean(grad * normed, axis=-1, keepdims=True)
    return scale * (grad - jnp.mean(grad, axis=-1, keepdims=True) - normed * inner)


def after(value, *others):
    return lax.optimization_barrier((value, others))[0]


def shape(dims, dtype):
    return jax.ShapeDtypeStruct(dims, dtype)


def call(body, name, out_shape, args, *, grid=(), in_specs=None, out_specs=None, scratch=(),
         scalars=0, aliases=None, flops=0, nbytes=0, special=0, vmem=56):
    outs = out_shape if isinstance(out_shape, (tuple, list)) else [out_shape]
    whole = pl.BlockSpec(memory_space=pltpu.VMEM)
    if in_specs is None:
        in_specs = [whole] * (len(args) - scalars)
    if out_specs is None:
        out_specs = [whole] * len(outs)
        if not isinstance(out_shape, (tuple, list)):
            out_specs = out_specs[0]
    return pl.pallas_call(
        body,
        name=name,
        out_shape=out_shape,
        grid_spec=pltpu.PrefetchScalarGridSpec(
            num_scalar_prefetch=scalars,
            grid=grid,
            in_specs=in_specs,
            out_specs=out_specs,
            scratch_shapes=scratch,
        ),
        input_output_aliases=aliases or {},
        cost_estimate=pl.CostEstimate(flops=COST, bytes_accessed=COST, transcendentals=0),
        compiler_params=pltpu.CompilerParams(vmem_limit_bytes=vmem * MIB),
    )(*args)


def column(row):
    return jnp.broadcast_to(row.astype(F32), (8, row.shape[1])).T[:, :1].astype(jnp.int32)


def route_body(parts, capacity, docs, at_ref, ids_ref, table_ref, rows_ref, segment_ref, slot_ref,
               low_ref, tall_ref, meta_ref, *out_refs):
    ids = column(ids_ref[...])
    count = ids.shape[0]
    lines = table_ref.shape[0]
    picked = dot(one_hot(ids >> 7, lines), table_ref[...].astype(F32).astype(BF16))
    lane = iota((count, LANES), 1)
    choice = jnp.sum(
        jnp.where(lane == (ids & (LANES - 1)), picked, 0.0), axis=1, keepdims=True
    ).astype(jnp.int32)
    mine = lane == choice
    below = jnp.where(iota((count, count), 0) > iota((count, count), 1), 1.0, 0.0).astype(BF16)
    ranks = dot(below, jnp.where(mine, 1.0, 0.0).astype(BF16))
    rank = jnp.sum(jnp.where(mine, ranks, 0.0), axis=1, keepdims=True).astype(jnp.int32)
    slot = (choice ^ at_ref[0]) * capacity + rank
    slot_ref[...] = slot
    rows = rows_ref[...]
    for k in range(parts):
        chosen = one_hot(slot - k * capacity, capacity)
        out_refs[k][...] = dot_tn(chosen, rows).astype(BF16)

    pair_len = low_ref.shape[1]
    pair_at = pl.multiple_of(at_ref[2] * pair_len, pair_len)
    segments = segment_ref[...]
    here = segment_ref[:, pl.ds(pair_at, pair_len)]
    low = jnp.zeros((1, pair_len), F32)
    for d in range(docs):
        start = jnp.sum(jnp.where(segments < d, 1.0, 0.0), axis=1, keepdims=True)
        low = low + jnp.where(here == d, start, 0.0)
    low = low.astype(jnp.int32) - (pair_at - pair_len)
    low_ref[...] = low
    tall_ref[...] = column(low)
    place = iota((1, LANES), 1)
    meta = jnp.where(place == 0, at_ref[1], 0)
    for t in range(pair_len // TILE):
        meta = jnp.where(place == 1 + t, low[:, t * TILE : t * TILE + 1] >> 8, meta)
    meta_ref[...] = meta


def route(at, ids, table, rows, segments, parts, capacity, docs):
    count, width = rows.shape
    pair_len = 2 * count
    outs = [shape((count, 1), jnp.int32), shape((1, pair_len), jnp.int32),
            shape((pair_len, 1), jnp.int32), shape((1, LANES), jnp.int32)]
    outs += [shape((capacity, width), BF16)] * parts
    return call(
        functools.partial(route_body, parts, capacity, docs), "route", outs,
        (at, ids, table, rows, segments), scalars=1,
    )


def vector(ref, at):
    lines = ref.shape[0] // 4
    return jnp.concatenate([ref[at * lines + j : at * lines + j + 1, :] for j in range(lines)], axis=1)


def project_body(skip, core_ref, own_ref, sib_ref, norm_ref, wq_ref, wk_ref, wv_ref, *refs):
    outs = refs[skip:-1]
    held_ref = refs[-1]
    step = pl.program_id(0)
    half = (pl.num_programs(0) - 1) // 2
    before = held_ref[(step + 1) % 2]
    outs[1][...] = dot(before, wk_ref[...]).astype(BF16)
    outs[2][...] = dot(before, wv_ref[...]).astype(BF16)
    if not skip:
        outs[3][...] = dot(before, wq_ref[...]).astype(BF16)
    rows = jnp.where(step < half, own_ref[...], sib_ref[...])
    normed, unused = norm_rows(rows.astype(F32))
    a = (normed * vector(norm_ref, 0) + vector(norm_ref, 1)).astype(BF16)
    held_ref[step % 2] = a
    outs[0][...] = a


def project(core, own, sib, norms, w_qkv, made):
    count, width = own.shape
    mine = width // 2
    half = count // TILE
    base = 0 if made else 2 * half

    def place(i, c):
        return ((i // half) ^ c[0]) * half + i % half

    def now(i, c):
        return (base + place(jnp.minimum(i, 2 * half - 1), c), 0)

    def then(i, c):
        return (base + place(jnp.maximum(i - 1, 0), c), 0)

    in_specs = [
        pl.BlockSpec((TILE, width), lambda i, c: (jnp.minimum(i, half - 1), 0)),
        pl.BlockSpec((TILE, width), lambda i, c: (jnp.clip(i - half, 0, half - 1), 0)),
        pl.BlockSpec(norms.shape, lambda i, c: (0, 0)),
    ] + [
        pl.BlockSpec((width, mine), functools.partial(lambda t, i, c: (0, 2 * t + c[0]), t))
        for t in range(3)
    ]
    args = [core, own, sib, norms, w_qkv, w_qkv, w_qkv]
    outs = [shape((4 * count, width), BF16)] + [shape((4 * count, mine), BF16)] * 2
    out_specs = [
        pl.BlockSpec((TILE, width), now),
        pl.BlockSpec((TILE, mine), then),
        pl.BlockSpec((TILE, mine), then),
    ]
    aliases = {}
    if made:
        in_specs += [pl.BlockSpec(memory_space=pl.ANY)] * 3
        aliases = {7: 0, 8: 1, 9: 2}
        args += list(made)
    else:
        outs.append(shape((2 * count, mine), BF16))
        out_specs.append(
            pl.BlockSpec((TILE, mine), lambda i, c: (place(jnp.maximum(i - 1, 0), c), 0))
        )
    return call(
        functools.partial(project_body, 3 if made else 0), "project", outs, args,
        grid=(2 * half + 1,), in_specs=in_specs, out_specs=out_specs, scalars=1, aliases=aliases,
        scratch=[pltpu.VMEM((2, TILE, width), BF16)],
    )


def masked_heads(block):
    lane = iota(block.shape, 1)
    zero = jnp.zeros((), block.dtype)
    return [
        jnp.where(lane < HEAD_DIM, block, zero),
        jnp.where(lane < HEAD_DIM, zero, block),
    ]


def flip(block):
    return block.astype(F32).T.astype(block.dtype)


def lanes_of(group):
    return slice(group * LANES, (group + 1) * LANES)


def put_heads(heads_ref, q_ref):
    def some(t, unused):
        here = pl.ds(pl.multiple_of(t * TILE, TILE), TILE)
        block = q_ref[here, :] * jnp.asarray(HEAD_DIM**-0.5, BF16)
        for g in range(q_ref.shape[1] // LANES):
            for h, part in enumerate(masked_heads(block[:, lanes_of(g)])):
                heads_ref[2 * g + h, here, :] = part
        return unused

    lax.fori_loop(0, q_ref.shape[0] // TILE, some, 0)


def tile_mask(begin, low, high):
    place = begin + iota((TILE, TILE), 0)
    return (place >= low) & (place <= high)


def attend_body(meta_ref, q_ref, k_ref, v_ref, lo_ref, own_ref, sib_ref, all_ref, tall_ref,
                log_ref, heads_ref, acc_ref, rows_ref):
    total, mine = q_ref.shape
    half = total // 2
    heads = range(mine // HEAD_DIM)
    put_heads(heads_ref, q_ref)
    core = meta_ref[0, 0]

    def tile(t, unused):
        at = pl.multiple_of(t * TILE, TILE)
        here = pl.ds(at, TILE)
        low = lo_ref[here, :]
        high = total + at + iota((TILE, 1), 0)
        acc_ref[...] = jnp.zeros_like(acc_ref)

        def step(j, state):
            begin = pl.multiple_of(j * TILE, TILE)
            there = pl.ds(begin, TILE)
            place = begin + iota((TILE, TILE), 1)
            allowed = (place >= low) & (place <= high)
            scores = [
                jnp.where(
                    allowed, dot_nt(heads_ref[h, here, :], k_ref[there, lanes_of(h // 2)]), LOWER
                )
                for h in heads
            ]
            tops = [
                jnp.maximum(state[2 * h], jnp.max(scores[h], axis=1, keepdims=True)) for h in heads
            ]
            shares = [jnp.exp(scores[h] - tops[h]) for h in heads]
            factors = [jnp.exp(state[2 * h] - tops[h]) for h in heads]
            sums = [
                state[2 * h + 1] * factors[h] + jnp.sum(shares[h], axis=1, keepdims=True)
                for h in heads
            ]
            more = [dot(shares[h].astype(BF16), v_ref[there, lanes_of(h // 2)]) for h in heads]
            for h in heads:
                acc_ref[h] = acc_ref[h] * factors[h] + more[h]
            return tuple(x for h in heads for x in (tops[h], sums[h]))

        first = (jnp.full((TILE, 1), LOW, F32), jnp.zeros((TILE, 1), F32))
        state = lax.fori_loop(
            meta_ref[0, 1 + t], total // TILE + t + 1, step, first * len(heads)
        )
        lane = iota((TILE, LANES), 1)
        logs = jnp.zeros((TILE, LANES), F32)
        for h in heads:
            logs = jnp.where(lane == h, state[2 * h] + jnp.log(state[2 * h + 1]), logs)
        log_ref[:, here] = logs.T[: log_ref.shape[0], :]
        for g in range(mine // LANES):
            left = acc_ref[2 * g] / state[4 * g + 1]
            right = acc_ref[2 * g + 1] / state[4 * g + 3]
            out = jnp.where(lane < HEAD_DIM, left, right)
            rows_ref[here, lanes_of(g)] = out
            tall_ref[lanes_of(g), here] = out.T
        return unused

    lax.fori_loop(0, total // TILE, tile, 0)

    def some(t, unused):
        at = pl.multiple_of(t * TILE, TILE)
        here = pl.ds(at, TILE)
        own_at = pl.ds(pl.multiple_of(core * half + at, TILE), TILE)
        sib_at = pl.ds(pl.multiple_of((1 - core) * half + at, TILE), TILE)
        all_ref[own_at, :] = rows_ref[own_at, :].astype(BF16)
        all_ref[sib_at, :] = rows_ref[sib_at, :].astype(BF16)
        own_ref[here, :] = rows_ref[own_at, :].astype(BF16)
        sib_ref[here, :] = rows_ref[sib_at, :].astype(BF16)
        return unused

    lax.fori_loop(0, half // TILE, some, 0)


def attend(meta, q, k, v, low):
    total, mine = q.shape
    heads = mine // HEAD_DIM
    outs = [
        shape((total // 2, mine), BF16),
        shape((total // 2, mine), BF16),
        shape((total, mine), BF16),
        shape((mine, total), F32),
        shape((-(-heads // 8) * 8, total), F32),
    ]
    return call(
        attend_body, "attend", outs, (meta, q, k, v, low), scalars=1,
        scratch=[pltpu.VMEM((heads, total, LANES), BF16), pltpu.VMEM((heads, TILE, LANES), F32),
                 pltpu.VMEM((total, mine), F32)],
    )


def fetch(pairs, sems):
    copies = [pltpu.make_async_copy(a, b, sems.at[i]) for i, (a, b) in enumerate(pairs)]
    for copy in copies:
        copy.start()
    return [copy.wait for copy in copies]


def both_rows(core, own, sib, rows_ref):
    half = own.shape[0]
    return [
        (own, rows_ref.at[pl.ds(pl.multiple_of(core * half, half), half), :]),
        (sib, rows_ref.at[pl.ds(pl.multiple_of((1 - core) * half, half), half), :]),
    ]


def attend_back_body(meta_ref, q_hbm, k_hbm, v_hbm, own_hbm, sib_hbm, wo_hbm, tall_hbm, log_ref,
                     lo_ref, gq_ref, gk_ref, gv_ref, rows_ref, heads_ref, grads_ref, delta_ref,
                     kt_ref, gqt_ref, gks_ref, gvs_ref, q_ref, k_ref, v_ref, wo_ref, tall_ref,
                     sems):
    total, mine = q_ref.shape
    heads = mine // HEAD_DIM
    core = meta_ref[0, 0]
    mine_at = pl.ds(pl.multiple_of(core * mine, mine), mine)
    waits = fetch(
        both_rows(core, own_hbm, sib_hbm, rows_ref)
        + [(wo_hbm.at[mine_at, :], wo_ref), (tall_hbm, tall_ref), (q_hbm, q_ref), (k_hbm, k_ref),
           (v_hbm, v_ref)],
        sems,
    )

    def clear(t, unused):
        here = pl.ds(pl.multiple_of(t * TILE, TILE), TILE)
        gks_ref[here, :] = jnp.zeros((TILE, mine), F32)
        gvs_ref[here, :] = jnp.zeros((TILE, mine), F32)
        return unused

    lax.fori_loop(0, 2 * total // TILE, clear, 0)
    gqt_ref[...] = jnp.zeros_like(gqt_ref)
    for wait in waits[:4]:
        wait()
    weights = wo_ref[...]

    def begin(t, unused):
        here = pl.ds(pl.multiple_of(t * TILE, TILE), TILE)
        grads = dot_nt(rows_ref[here, :], weights).astype(BF16)
        turned = grads.astype(F32).T * tall_ref[:, here]
        for h in range(heads):
            span = slice(h * HEAD_DIM, (h + 1) * HEAD_DIM)
            delta_ref[h : h + 1, here] = jnp.sum(turned[span, :], axis=0, keepdims=True)
        for g in range(mine // LANES):
            for h, part in enumerate(masked_heads(grads[:, lanes_of(g)])):
                grads_ref[2 * g + h, here, :] = part
        return unused

    lax.fori_loop(0, total // TILE, begin, 0)
    waits[4]()
    put_heads(heads_ref, q_ref)
    waits[5]()

    def turn(t, unused):
        here = pl.ds(pl.multiple_of(t * TILE, TILE), TILE)
        kt_ref[:, here] = flip(k_ref[here, :])
        return unused

    lax.fori_loop(0, 2 * total // TILE, turn, 0)
    waits[6]()

    def tile(t, unused):
        at = pl.multiple_of(t * TILE, TILE)
        here = pl.ds(at, TILE)
        low = lo_ref[:, here]
        high = total + at + iota((1, TILE), 1)

        logs = [log_ref[h : h + 1, here] for h in range(heads)]
        deltas = [delta_ref[h : h + 1, here] for h in range(heads)]

        def step(j, carry):
            begin = pl.multiple_of(j * TILE, TILE)
            there = pl.ds(begin, TILE)
            allowed = tile_mask(begin, low, high)
            every = range(heads)
            queries = [heads_ref[h, here, :] for h in every]
            grads = [grads_ref[h, here, :] for h in every]
            scores = [dot_nt(k_ref[there, lanes_of(h // 2)], queries[h]) for h in every]
            grad_soft = [dot_nt(v_ref[there, lanes_of(h // 2)], grads[h]) for h in every]
            soft = [jnp.exp(jnp.where(allowed, scores[h], LOWER) - logs[h]) for h in every]
            grad_scores = [(soft[h] * (grad_soft[h] - deltas[h])).astype(BF16) for h in every]
            soft = [s.astype(BF16) for s in soft]
            gv = [dot(soft[h], grads[h]) for h in every]
            gk = [dot(grad_scores[h], queries[h]) for h in every]
            gq = [
                dot(kt_ref[h * HEAD_DIM : (h + 1) * HEAD_DIM, there], grad_scores[h])
                for h in every
            ]
            for g in range(heads // 2):
                gvs_ref[there, lanes_of(g)] += gv[2 * g] + gv[2 * g + 1]
                gks_ref[there, lanes_of(g)] += gk[2 * g] + gk[2 * g + 1]
            for h in every:
                gqt_ref[h * HEAD_DIM : (h + 1) * HEAD_DIM, here] += gq[h]
            return carry

        return lax.fori_loop(meta_ref[0, 1 + t], total // TILE + t + 1, step, unused)

    lax.fori_loop(0, total // TILE, tile, 0)

    def finish_queries(t, unused):
        here = pl.ds(pl.multiple_of(t * TILE, TILE), TILE)
        gq_ref[here, :] = (gqt_ref[:, here].T * (HEAD_DIM**-0.5)).astype(BF16)
        return unused

    def finish_keys(t, unused):
        here = pl.ds(pl.multiple_of(t * TILE, TILE), TILE)
        gk_ref[here, :] = gks_ref[here, :].astype(BF16)
        gv_ref[here, :] = gvs_ref[here, :].astype(BF16)
        return unused

    lax.fori_loop(0, total // TILE, finish_queries, 0)
    lax.fori_loop(0, 2 * total // TILE, finish_keys, 0)


def attend_back(meta, q, k, v, own, sib, w_out, tall, logs, low):
    total, mine = q.shape
    width = own.shape[1]
    heads = mine // HEAD_DIM
    outs = [
        shape((total, mine), BF16),
        shape((2 * total, mine), BF16),
        shape((2 * total, mine), BF16),
    ]
    return call(
        attend_back_body, "attend_back", outs,
        (meta, q, k, v, own, sib, w_out, tall, logs, low), scalars=1,
        in_specs=[pl.BlockSpec(memory_space=pl.ANY)] * 7 + [pl.BlockSpec(memory_space=pltpu.VMEM)] * 2,
        scratch=[pltpu.VMEM((total, width), BF16), pltpu.VMEM((heads, total, LANES), BF16),
                 pltpu.VMEM((heads, total, LANES), BF16), pltpu.VMEM(logs.shape, F32),
                 pltpu.VMEM((mine, 2 * total), BF16), pltpu.VMEM((mine, total), F32),
                 pltpu.VMEM((2 * total, mine), F32), pltpu.VMEM((2 * total, mine), F32),
                 pltpu.VMEM(q.shape, BF16), pltpu.VMEM(k.shape, BF16), pltpu.VMEM(v.shape, BF16),
                 pltpu.VMEM((mine, width), BF16), pltpu.VMEM(tall.shape, F32),
                 pltpu.SemaphoreType.DMA((7,))],
    )


def dense_body(subs, sub, chip_ref, a_hbm, gq_hbm, gk_hbm, gv_hbm, all_hbm, own_hbm, sib_hbm,
               *refs):
    piece_refs = refs[:4]
    dense_ref, rows_ref, short_ref, long_ref, sems = refs[4:]
    unused, total, mine = short_ref.shape
    half = total // 2
    width = rows_ref.shape[1]
    lines = width // subs
    quarter = subs * sub
    core = chip_ref[0]
    own_at = pl.multiple_of(2 * total + core * half, half)
    sib_at = pl.multiple_of(2 * total + (1 - core) * half, half)
    waits = fetch(
        [(own_hbm, rows_ref.at[pl.ds(own_at, half), :]),
         (sib_hbm, rows_ref.at[pl.ds(sib_at, half), :]),
         (a_hbm, rows_ref.at[pl.ds(0, 2 * total), :]),
         (gq_hbm, short_ref.at[0]), (all_hbm, short_ref.at[1]),
         (gk_hbm, long_ref.at[0]), (gv_hbm, long_ref.at[1])],
        sems,
    )

    def put(kind, turned):
        for j in range(mine // LANES):
            block = turned[lanes_of(j), :].T.astype(BF16)
            for at in range(subs):
                first = pl.multiple_of(kind * quarter + at * sub + j * lines, 16)
                dense_ref[pl.ds(first, lines), :] = block[at * lines : (at + 1) * lines, :]

    def short(i, unused):
        rows = rows_ref[pl.ds(pl.multiple_of((1 + i) * total, total), total), :]
        put(3 * i, dot_tn(short_ref[i], rows))
        return unused

    def long(i, unused):
        put(1 + i, dot_tn(long_ref[i], rows_ref[: 2 * total, :]))
        return unused

    for wait in waits[:5]:
        wait()
    lax.fori_loop(0, 2, short, 0)
    waits[5]()
    waits[6]()
    lax.fori_loop(0, 2, long, 0)
    spare = sub - mine // LANES * lines
    if spare:
        for at in range(4 * subs):
            dense_ref[(at + 1) * sub - spare : (at + 1) * sub, :] = jnp.zeros((spare, LANES), BF16)
    for p in range(2):
        side = chip_ref[1 + p]
        for r, which in enumerate((side, 1 - side)):
            for at in range(subs):
                from_at = pl.multiple_of((2 * p + which) * quarter + at * sub, 16)
                to_at = pl.multiple_of((at ^ chip_ref[3 + p]) * sub, 16)
                piece_refs[2 * p + r][pl.ds(to_at, sub), :] = dense_ref[pl.ds(from_at, sub), :]


def dense_pieces(chip, a, gq, gk, gv, attn_all, own, sib, subs, sub):
    return call(
        functools.partial(dense_body, subs, sub), "dense",
        [shape((subs * sub, LANES), BF16)] * 4,
        (chip, a, gq, gk, gv, attn_all, own, sib), scalars=1,
        in_specs=[pl.BlockSpec(memory_space=pl.ANY)] * 7,
        scratch=[pltpu.VMEM((4 * subs * sub, LANES), BF16),
                 pltpu.VMEM((3 * gq.shape[0], a.shape[1]), BF16),
                 pltpu.VMEM((2, *gq.shape), BF16), pltpu.VMEM((2, *gk.shape), BF16),
                 pltpu.SemaphoreType.DMA((7,))],
    )


def lift_body(parts, capacity, core_ref, own_ref, other_ref, w_ref, x_ref, norm_ref, slot_ref,
              resid_ref, *out_refs):
    mine = own_ref.shape[1]
    core = core_ref[0]
    own_at = pl.ds(pl.multiple_of(core * mine, mine), mine)
    other_at = pl.ds(pl.multiple_of((1 - core) * mine, mine), mine)
    *out_refs, rows_ref = out_refs

    def some(t, unused):
        here = pl.ds(pl.multiple_of(t * TILE, TILE), TILE)
        more = dot(own_ref[here, :], w_ref[own_at, :]) + dot(other_ref[here, :], w_ref[other_at, :])
        resid = x_ref[here, :].astype(F32) + more
        resid_ref[here, :] = resid
        normed, scale = norm_rows(resid)
        rows_ref[here, :] = (normed * vector(norm_ref, 2) + vector(norm_ref, 3)).astype(BF16)
        return unused

    lax.fori_loop(0, own_ref.shape[0] // TILE, some, 0)
    slot = slot_ref[...]
    for k in range(parts):
        chosen = one_hot(slot - k * capacity, capacity)
        out_refs[k][...] = dot_tn(chosen, rows_ref[...]).astype(BF16)


def lift(core, own, other, w_out, x, norms, slot, parts, capacity):
    count, width = x.shape
    outs = [shape((count, width), F32)] + [shape((capacity, width), BF16)] * parts
    return call(
        functools.partial(lift_body, parts, capacity), "lift", outs,
        (core, own, other, w_out, x, norms, slot), scratch=[pltpu.VMEM((count, width), BF16)],
        scalars=1, flops=2 * count * width * (width + parts * capacity),
    )


GATE_A = math.sqrt(2.0 / math.pi)
GATE_B = 0.044715


def expert_body(sub, rows_ref, grad_ref, up_ref, down_ref, tall_ref, pre_ref, back_ref, out_ref,
                turned_ref, back_acc, out_acc):
    step = pl.program_id(0)

    @pl.when(step == 0)
    def _():
        back_acc[...] = jnp.zeros_like(back_acc)
        out_acc[...] = jnp.zeros_like(out_acc)
        turned_ref[...] = flip(rows_ref[...])

    parts = [slice(s * sub, (s + 1) * sub) for s in range(down_ref.shape[0] // sub)]
    pres = [dot(rows_ref[...], up_ref[:, part]) for part in parts]
    grads = [dot_nt(grad_ref[...], down_ref[part, :]) for part in parts]
    hids, slopes = [], []
    for pre in pres:
        square = pre * pre
        bend = jnp.tanh(GATE_A * (pre + GATE_B * (square * pre)))
        half = 0.5 + 0.5 * bend
        hids.append(pre * half)
        slopes.append(
            half + (pre * (1.0 - bend * bend)) * (0.5 * GATE_A + (1.5 * GATE_A * GATE_B) * square)
        )
    low = jnp.concatenate([(g * s).astype(BF16) for g, s in zip(grads, slopes)], axis=1)
    back_acc[...] += dot_nt(low, up_ref[...])
    out_acc[...] += dot(jnp.concatenate([h.astype(BF16) for h in hids], axis=1), down_ref[...])
    pre_ref[...] = low
    for part, hid in zip(parts, hids):
        tall_ref[part, :] = hid.T.astype(BF16)

    @pl.when(step == pl.num_programs(0) - 1)
    def _():
        back_ref[...] = back_acc[...].astype(BF16)
        out_ref[...] = out_acc[...].astype(BF16)


def expert(rows, grads, w_up, w_down, sub=256):
    count, width = rows.shape
    hidden = w_up.shape[1]
    block = width
    const = pl.BlockSpec((count, width), lambda j: (0, 0))
    return call(
        functools.partial(expert_body, sub), "expert",
        [shape((hidden, count), BF16), shape((count, hidden), BF16), shape((count, width), BF16),
         shape((count, width), BF16), shape((width, count), BF16)],
        (rows, grads, w_up, w_down), grid=(hidden // block,),
        in_specs=[const, const, pl.BlockSpec((width, block), lambda j: (0, j)),
                  pl.BlockSpec((block, width), lambda j: (j, 0))],
        out_specs=[pl.BlockSpec((block, count), lambda j: (j, 0)),
                   pl.BlockSpec((count, block), lambda j: (0, j)), const, const,
                   pl.BlockSpec((width, count), lambda j: (0, 0))],
        scratch=[pltpu.VMEM((count, width), F32)] * 2,
    )


def expert_grad_body(parts, subs, chip_ref, *refs):
    turned, grads, talls, pres = (refs[parts * t : parts * (t + 1)] for t in range(4))
    *outs, held_ref, sems = refs[4 * parts :]
    width = held_ref.shape[2]
    lines = width // subs
    step = pl.program_id(0)
    steps = len(outs)
    slot = step % 2

    def copy(t, at):
        return pltpu.make_async_copy(held_ref.at[at], outs[t], sems.at[at])

    @pl.when(step >= 2)
    def _():
        copy(0, slot).wait()

    def product(left, right):
        out = None
        for a, b in zip(left, right):
            more = dot(a[...], b[...])
            out = more if out is None else out + more
        return out.astype(BF16)

    half = steps // 2
    side, mask = chip_ref[1 + step % half], chip_ref[3 + step % half]
    pairs = ((product(turned, pres), side == 0), (product(talls, grads), side == 1))
    for value, stays in pairs:
        base = jnp.where(stays, width, 0)
        for at in range(subs):
            first = pl.multiple_of(base + (at ^ mask) * lines, 16)
            held_ref[slot, pl.ds(first, lines), :] = value[at * lines : (at + 1) * lines, :]

    for t in range(steps):

        @pl.when(step == t)
        def _(t=t):
            copy(t, t % 2).start()

    @pl.when(step == steps - 1)
    def _():
        copy(0, 0).wait()
        copy(0, 1).wait()


def expert_grad(chip, turned, grads, talls, pres, subs):
    parts = len(grads)
    count, width = grads[0].shape
    blocks = talls[0].shape[0] // width
    half = blocks // 2

    def column(i, m):
        return jnp.where(i < half, (1 - m[0]) * half, m[0] * half - half) + i

    const = lambda dims: pl.BlockSpec(dims, lambda i, m: (0, 0))
    return call(
        functools.partial(expert_grad_body, parts, subs), "expert_grad",
        [shape((2 * width, width), BF16)] * blocks,
        (chip, *turned, *grads, *talls, *pres), grid=(blocks,), scalars=1,
        in_specs=[const((width, count))] * parts + [const((count, width))] * parts
        + [pl.BlockSpec((width, count), lambda i, m: (column(i, m), 0))] * parts
        + [pl.BlockSpec((count, width), lambda i, m: (0, column(i, m)))] * parts,
        out_specs=[pl.BlockSpec(memory_space=pl.ANY)] * blocks,
        scratch=[pltpu.VMEM((2, 2 * width, width), BF16), pltpu.SemaphoreType.DMA((2,))],
    )


def widen_body(skip, meta_ref, *refs):
    pairs, (up_out, down_out) = refs[:4], refs[4 + skip :]
    second = pl.program_id(0) >= pl.num_programs(0) // 2
    first = meta_ref[1 + pl.program_id(0) // (pl.num_programs(0) // 2)] == 0
    mine = jnp.where(second, pairs[2][...], pairs[0][...])
    theirs = jnp.where(second, pairs[3][...], pairs[1][...])
    up_out[...] = jnp.where(first, mine, theirs).astype(F32)
    down_out[...] = jnp.where(first, theirs, mine).astype(F32)


def widen(core, sides, masks, mine, theirs, made, hidden, subs):
    width = mine[0].shape[1]
    rows = width // subs
    meta = jnp.stack([core, *sides, *masks]).astype(jnp.int32)

    def index(p):
        def at(i, m):
            here = jnp.clip(i - p * subs, 0, subs - 1)
            return (here ^ m[3 + p], 0)

        return at

    blocks = [pl.BlockSpec((rows, width), index(p)) for p in (0, 0, 1, 1)]
    column = lambda i, m: 2 * m[0] + i // subs
    return call(
        functools.partial(widen_body, len(made)), "widen",
        [shape((width, hidden), F32), shape((hidden, width), F32)],
        (meta, mine[0], theirs[0], mine[1], theirs[1], *made), grid=(2 * subs,), scalars=1,
        in_specs=blocks + [pl.BlockSpec(memory_space=pl.ANY)] * len(made),
        out_specs=[pl.BlockSpec((rows, width), lambda i, m: (i % subs, column(i, m))),
                   pl.BlockSpec((rows, width), lambda i, m: (column(i, m) * subs + i % subs, 0))],
        aliases={5: 0, 6: 1} if made else None,
    )


def collect(slot, part_refs):
    total = None
    for k, ref in enumerate(part_refs):
        capacity = ref.shape[0]
        more = dot(one_hot(slot - k * capacity, capacity), ref[...])
        total = more if total is None else total + more
    return total


def lower_body(parts, slot_ref, resid_ref, cot_ref, norm_ref, *refs):
    grads = collect(slot_ref[...], refs[:parts])
    gr_ref, low_ref, gain_out, bias_out = refs[parts:]
    normed, scale = norm_rows(resid_ref[...])

    @pl.when(pl.program_id(0) == 0)
    def _():
        gain_out[...] = jnp.zeros_like(gain_out)
        bias_out[...] = jnp.zeros_like(bias_out)

    gain_out[...] += jnp.sum(grads * normed, axis=0, keepdims=True)
    bias_out[...] += jnp.sum(grads, axis=0, keepdims=True)
    gr = cot_ref[...].astype(F32) + norm_back(grads * vector(norm_ref, 2), normed, scale)
    gr_ref[...] = gr
    low_ref[...] = gr.astype(BF16)


def row_specs(dims, *whole):
    return [pl.BlockSpec((TILE, d), lambda i: (i, 0)) for d in dims] + [
        pl.BlockSpec(w.shape, lambda i: (0, 0)) for w in whole
    ]


def lower(slot, resid, cot, norms, back):
    parts = len(back)
    count, width = resid.shape
    outs = [shape((count, width), F32), shape((count, width), BF16),
            shape((1, width), F32), shape((1, width), F32)]
    return call(
        functools.partial(lower_body, parts), "lower", outs, (slot, resid, cot, norms, *back),
        grid=(count // TILE,), in_specs=row_specs((1, width, width), norms, *back),
        out_specs=row_specs((width, width), outs[2], outs[3]),
    )


def finish_body(slot_ref, resid_ref, *refs):
    refs[-1][...] = (resid_ref[...] + collect(slot_ref[...], refs[:-1])).astype(BF16)


def finish(slot, resid, parts):
    count, width = resid.shape
    return call(
        finish_body, "finish", shape(resid.shape, BF16), (slot, resid, *parts),
        grid=(count // TILE,), in_specs=row_specs((1, width), *parts),
        out_specs=row_specs((width,))[0],
    )


def project_back_body(half, core_ref, own_ref, sib_ref, hal_ref, has_ref, gq_ref, gk_ref, gv_ref,
                      wq_ref, wk_ref, wv_ref, keep_ref, send_ref, halo_ref, gain_ref, bias_ref):
    step = pl.program_id(0)
    rows = jnp.where(
        step < 2 * half,
        jnp.where(step < half, own_ref[...], sib_ref[...]),
        jnp.where(step < 3 * half, hal_ref[...], has_ref[...]),
    )
    normed, unused = norm_rows(rows.astype(F32))
    here = step < 2 * half
    ga = dot_nt(gk_ref[...], wk_ref[...]) + dot_nt(gv_ref[...], wv_ref[...])
    gq = jnp.where(here, gq_ref[...], jnp.zeros_like(gq_ref))
    ga = ga + dot_nt(gq, wq_ref[...])

    @pl.when(step == 0)
    def _():
        gain_ref[...] = jnp.zeros_like(gain_ref)
        bias_ref[...] = jnp.zeros_like(bias_ref)

    gain_ref[...] += jnp.sum(ga * normed, axis=0, keepdims=True)
    bias_ref[...] += jnp.sum(ga, axis=0, keepdims=True)

    @pl.when(step < half)
    def _():
        keep_ref[...] = ga

    @pl.when((step // half) % 2 == 1)
    def _():
        send_ref[...] = ga.astype(BF16)

    @pl.when(step // half == 2)
    def _():
        halo_ref[...] = ga


def project_back(core, own, sib, hal, has, gq, gk, gv, w_qkv):
    count, width = own.shape
    mine = gq.shape[1]
    half = count // TILE

    def at(t):
        return lambda i, c: (jnp.clip(i - t * half, 0, half - 1), 0)

    def place(i, c):
        return jnp.where(i < 2 * half, 2 * half, 0) + (((i // half) % 2) ^ c[0]) * half + i % half

    def sent(i, c):
        late = half + jnp.clip(i - 3 * half, 0, half - 1)
        return (jnp.where(i < 2 * half, jnp.clip(i - half, 0, half - 1), late), 0)

    row = pl.BlockSpec((1, width), lambda i, c: (0, 0))
    in_specs = [pl.BlockSpec((TILE, width), at(t)) for t in range(4)] + [
        pl.BlockSpec((TILE, mine), lambda i, c: (jnp.maximum(place(i, c) - 2 * half, 0), 0)),
        pl.BlockSpec((TILE, mine), lambda i, c: (place(i, c), 0)),
        pl.BlockSpec((TILE, mine), lambda i, c: (place(i, c), 0)),
    ] + [
        pl.BlockSpec((width, mine), functools.partial(lambda t, i, c: (0, 2 * t + c[0]), t))
        for t in range(3)
    ]
    return call(
        functools.partial(project_back_body, half), "project_back",
        [shape((count, width), F32), shape((2 * count, width), BF16), shape((count, width), F32),
         shape((1, width), F32), shape((1, width), F32)],
        (core, own, sib, hal, has, gq, gk, gv, w_qkv, w_qkv, w_qkv),
        grid=(4 * half,), in_specs=in_specs, scalars=1,
        out_specs=[pl.BlockSpec((TILE, width), at(0)), pl.BlockSpec((TILE, width), sent),
                   pl.BlockSpec((TILE, width), at(2)), row, row],
        flops=20 * count * width * mine,
    )


def close_body(x_ref, gr_ref, keep_ref, near_ref, far_ref, norm_ref, out_ref):
    ga = keep_ref[...] + near_ref[...].astype(F32) + far_ref[...].astype(F32)
    normed, scale = norm_rows(x_ref[...].astype(F32))
    out_ref[...] = gr_ref[...] + norm_back(ga * vector(norm_ref, 0), normed, scale)


def close(x, gr, keep, near, far, norms):
    count, width = x.shape
    block = pl.BlockSpec((TILE, width), lambda i: (i, 0))
    return call(
        close_body, "close", shape((count, width), F32), (x, gr, keep, near, far, norms),
        grid=(count // TILE,),
        in_specs=[block] * 5 + [pl.BlockSpec(norms.shape, lambda i: (0, 0))], out_specs=block,
    )


def swap(block, axis, distance):
    return lax.ppermute(block, axis, [(i, i ^ distance) for i in range(lax.axis_size(axis))])


def trade(block, axis):
    return lax.all_to_all(block, axis, split_axis=0, concat_axis=0, tiled=True)


def shift(block, axis, distance):
    size = lax.axis_size(axis)
    route = [(i, i + distance) for i in range(size) if 0 <= i + distance < size]
    return lax.ppermute(block, axis, route)


def total(terms):
    return sum(t.astype(F32) for t in terms).astype(BF16)


def add(a, b):
    return total([a, b])


def at_index(block, index):
    return lax.dynamic_index_in_dim(block, index, 0, keepdims=False)


def scatter_steps(pieces, orders):
    pairs = list(pieces)
    for s in range(len(orders[0])):
        arrived = yield [(goes, "seq", bits[s]) for (stays, goes), bits in zip(pairs, orders)]
        terms = [stays + [got] for (stays, goes), got in zip(pairs, arrived)]
        if s + 1 < len(orders[0]):
            half = terms[0][0].shape[0] // 2
            pairs = [
                ([total([t[half:] for t in terms_p])], total([t[:half] for t in terms_p]))
                for terms_p in terms
            ]
    return [total(terms_p) for terms_p in terms]


def gather_steps(parts, orders):
    parts = list(parts)
    for s in reversed(range(1, len(orders[0]))):
        arrived = yield [(part, "seq", bits[s]) for part, bits in zip(parts, orders)]
        parts = [jnp.concatenate([got, part], axis=0) for got, part in zip(arrived, parts)]
    return parts


def dense_steps(pieces, orders):
    sources = lax.axis_size("exp")
    parts = yield from scatter_steps(pieces, orders)
    joined = jnp.stack([p.reshape(sources, -1, LANES) for p in parts], axis=1)
    (got,) = yield [(joined, "exp", 0)]
    own = jnp.sum(got.astype(F32), axis=0).astype(BF16)
    (got,) = yield [(jnp.broadcast_to(own, (sources, *own.shape)), "exp", 0)]
    parts = [got[:, p].reshape(-1, LANES) for p in range(len(orders))]
    return (yield from gather_steps(parts, orders))


def expert_steps(pieces, orders):
    parts = yield from scatter_steps(pieces, orders)
    return (yield from gather_steps(parts, orders))


def one_step(sends):
    return (yield sends)


def across(parts, orders):
    return Stream(one_step([(part, "seq", bits[0]) for part, bits in zip(parts, orders)]))


def beside(parts):
    return Stream(one_step([(part, "seq", 1) for part in parts]))


def small_steps(value, hops):
    for hop in hops:
        (got,) = yield [(value, *hop)]
        value = value + got
    return value


class Stream:
    def __init__(self, steps):
        self.steps = steps
        self.result = None
        self.sent = []
        self.go(None)

    def go(self, arrived):
        try:
            sends = self.steps.send(arrived)
        except StopIteration as stop:
            self.sent, self.raw, self.result = [], [], stop.value
        else:
            self.raw = [send[0] for send in sends]
            self.sent = [swap(*send) if send[2] else trade(*send[:2]) for send in sends]


def meet(streams, others=()):
    streams = [stream for stream in streams if stream.sent]
    arrived, others = lax.optimization_barrier(([stream.sent for stream in streams], others))
    before = []
    for stream, got in zip(streams, arrived):
        stream.go(after(got, before) if before else got)
        before = before + stream.raw
    return others


def spread_columns_body(cols, chip_ref, *refs):
    out_ref = refs[-1]
    first = chip_ref[0] == 0
    own, sib = refs[:4], refs[4:8]
    picks = [
        (0, chip_ref[1] == 0, 0, 1),
        (1, chip_ref[1] == 1, 0, 1),
        (2, chip_ref[2] == 0, 2, 3),
    ]
    for kind, mine, here, there in picks:
        for j in range(cols):
            a, b = (jnp.where(mine, t[here][0, j], t[there][0, j]).astype(F32) for t in (own, sib))
            left = 2 * kind * cols + j
            out_ref[:, lanes_of(left)] = jnp.where(first, a, b)
            out_ref[:, lanes_of(left + cols)] = jnp.where(first, b, a)


def spread_rows_body(chip_ref, *refs):
    out_ref = refs[-1]
    own = pl.program_id(0) == chip_ref[0]
    mine = chip_ref[2] == 1
    subs, cols, lines, unused = refs[0].shape
    for at in range(subs):
        from_at = at ^ chip_ref[4]
        for j in range(cols):
            a, b = (
                jnp.where(mine, refs[t][from_at, j], refs[t + 1][from_at, j]) for t in (0, 2)
            )
            out_ref[lanes_of(j), at * lines : (at + 1) * lines] = (
                jnp.where(own, a, b).astype(F32).T
            )


def spread(chip, own, sib, width, mine, subs):
    cols = mine // LANES
    lines = width // subs
    block = math.gcd(lines, 192)

    def view(t):
        return t.reshape(subs, -1, LANES)[:, : cols * lines].reshape(subs, cols, lines, LANES)

    def part(p):
        def index(i, m):
            return ((i * block // lines) ^ m[3 + p], 0, i % (lines // block), 0)

        return pl.BlockSpec((1, cols, block, LANES), index)

    parts = [[view(t) for pair in side for t in pair] for side in (own, sib)]
    grad_qkv = call(
        functools.partial(spread_columns_body, cols), "spread_columns",
        shape((width, 3 * width), F32), (chip, *parts[0], *parts[1]), grid=(width // block,),
        scalars=1, in_specs=[part(0), part(0), part(1), part(1)] * 2,
        out_specs=pl.BlockSpec((block, 3 * width), lambda i, m: (i, 0)),
    )
    whole = pl.BlockSpec((subs, cols, lines, LANES), lambda i, m: (0, 0, 0, 0))
    grad_out = call(
        spread_rows_body, "spread_rows", shape((width, width), F32),
        (chip, *parts[0][2:], *parts[1][2:]), grid=(2,), scalars=1, in_specs=[whole] * 4,
        out_specs=pl.BlockSpec((mine, width), lambda i, m: (i, 0)),
    )
    return grad_qkv, grad_out


def on_device(
    layer_input,
    token_ids,
    segment_ids,
    hash_table,
    first_gain,
    first_bias,
    second_gain,
    second_bias,
    w_qkv,
    w_out,
    w_up,
    w_down,
    cotangent,
):
    x = layer_input[0]
    cot = cotangent[0]
    local_len, width = x.shape
    mine = width // 2
    sources = lax.axis_size("exp")
    ring = lax.axis_size("seq")
    capacity = 2 * local_len // sources
    seq_at = lax.axis_index("seq")
    exp_at = lax.axis_index("exp")
    core = (seq_at % 2).astype(jnp.int32)
    core_arg = core.reshape(1)
    norms = jnp.concatenate([first_gain, first_bias, second_gain, second_bias])
    norms = norms.reshape(-1, LANES)
    up, down = w_up[0], w_down[0]

    hal = shift(x, "seq", 2)
    sib = swap(x, "seq", 1)

    place = exp_at.astype(jnp.int32).reshape(1)
    at = jnp.stack([exp_at, core, seq_at // 2]).astype(jnp.int32)
    lines = -(-hash_table.shape[0] // (8 * LANES)) * 8
    table = jnp.pad(hash_table, (0, lines * LANES - hash_table.shape[0])).reshape(lines, LANES)
    docs = 2 * ring * local_len // DOC_MOST
    slot, low, low_tall, meta, *grad_out = route(
        at, token_ids, table, cot, segment_ids, sources, capacity, docs
    )
    grad_in = [grad_out[0]] + [swap(grad_out[k], "exp", k) for k in range(1, sources)]

    *made, q = project(core_arg, x, after(sib, slot), norms, w_qkv, None)
    hal = after(hal, q)
    has = swap(hal, "seq", 1)
    a, k, v = project(core_arg, hal, has, norms, w_qkv, made)
    attn_own, attn_give, attn_all, attn_tall, logs = attend(meta, q, k, v, low_tall)
    attn_other = swap(attn_give, "seq", 1)
    resid, *rows_out = lift(
        core_arg, attn_own, after(attn_other, grad_in), w_out, x, norms, slot, sources, capacity
    )
    rows_in = [rows_out[0]] + [swap(rows_out[k], "exp", k) for k in range(1, sources)]
    talls, pres, backs, outs, turned = [], [], [], [], []
    for k_at in range(sources):
        tall, pre, back, out, turn = expert(rows_in[k_at], grad_in[k_at], up, down)
        talls.append(tall)
        pres.append(pre)
        outs.append(out)
        turned.append(turn)
        backs.append(back if k_at == 0 else swap(back, "exp", k_at))
        if k_at + 1 < sources:
            rows_in[k_at + 1] = after(rows_in[k_at + 1], back)
    bits = [1 << b for b in range(1, ring.bit_length() - 1)]
    orders = [bits, bits[::-1]]
    sides = [(seq_at // o[0]) % 2 for o in orders]
    subs = ring // 4
    masks = [
        sum((1 - (seq_at // bit) % 2) << (len(o) - 2 - at) for at, bit in enumerate(o[1:]))
        for o in orders
    ]
    chip = jnp.stack([core, *sides, *masks]).astype(jnp.int32)

    turned, backs[:-2] = lax.optimization_barrier((turned, backs[:-2]))
    blocks = expert_grad(chip, turned, grad_in, talls, pres, subs)
    given, kept = blocks[:2], blocks[2:]
    given, backs[-2] = lax.optimization_barrier((given, backs[-2]))
    given, backs[-1] = lax.optimization_barrier((given, backs[-1]))
    got = [swap(t, "seq", 1) for t in given]
    gr, gattn, gain_two_grad, bias_two_grad = lower(slot, resid, cot, norms, backs)
    got = after(got, gattn)
    goes = [add(kept[p][:width], got[p][:width]) for p in range(2)]
    stays = [[kept[p][width:], got[p][width:]] for p in range(2)]
    experts = Stream(expert_steps(list(zip(stays, goes)), orders))
    outs = after(outs, goes)
    returned = [outs[0]] + [swap(outs[k], "exp", k) for k in range(1, sources)]
    gattn_sib = swap(gattn, "seq", 1)
    unit = sources * 16
    sub = -(-(mine // LANES * width // subs) // unit) * unit
    gq, gk, gv = attend_back(
        meta, q, k, v, gattn, after(gattn_sib, goes), w_out, attn_tall, logs, low
    )
    pieces = dense_pieces(chip, a, gq, gk, gv, attn_all, gattn, gattn_sib, subs, sub)
    pieces, returned = lax.optimization_barrier((pieces, returned))
    dense = Stream(
        dense_steps([([pieces[0]], pieces[1]), ([pieces[2]], pieces[3])], orders)
    )
    (gq,) = meet([experts], (after(gq, pieces),))
    keep, give, halo, gain_one_grad, bias_one_grad = project_back(
        core_arg, x, sib, hal, has, gq, gk, gv, w_qkv
    )
    small = jnp.concatenate([gain_one_grad, bias_one_grad, gain_two_grad, bias_two_grad], axis=0)
    (give,) = meet([dense, experts], (give,))
    near = swap(give, "seq", 1)
    (near,) = meet([dense], (near,))
    for rest in range(len(bits) - 2):
        meet([dense, experts])
    far = shift(add(halo, near[local_len:]), "seq", -2)
    hops = [("seq", bit) for bit in bits + [1]]
    hops += [("exp", 1 << b) for b in range(sources.bit_length() - 1)]
    small = Stream(small_steps(small, hops))
    layer_output = finish(slot, resid, returned)
    (layer_output,) = meet([dense, experts, small], (layer_output,))
    for rest in range(len(bits) - 2):
        meet([experts])
    own_parts = experts.result
    other_chip = across(own_parts, orders)
    other_core = beside(after(own_parts, layer_output))
    meet([dense, other_chip, other_core, small])
    other_both = beside(other_chip.result)
    hidden = down.shape[0]
    made = widen(core, sides, masks, own_parts, other_chip.result, (), hidden, subs)
    while dense.result is None:
        made = meet([dense, other_both, small], made)
    own_dense = dense.result
    dense_chip, dense_core = across(own_dense, orders), beside(own_dense)
    made = widen(
        1 - core, sides, masks, other_core.result, other_both.result, made, hidden, subs
    )
    grad_w_up, grad_w_down = meet([dense_chip, dense_core, small], made)
    dense_both = beside(dense_chip.result)
    meet([dense_both, small])
    while small.sent:
        small.go(small.sent)
    grad_w_qkv, grad_w_out = spread(
        chip, list(zip(own_dense, dense_chip.result)),
        list(zip(dense_core.result, dense_both.result)), width, mine, subs,
    )
    grad_input = close(x, gr, keep, near, after(far, grad_w_qkv), norms)
    small = small.result
    return (
        layer_output[None],
        grad_input[None],
        grad_w_qkv,
        grad_w_out,
        small[0],
        small[1],
        small[2],
        small[3],
        grad_w_up[None],
        grad_w_down[None],
    )


def solution(mesh):
    in_specs = (
        P("exp", "seq", None),
        P("exp", "seq"),
        P("exp", None),
        P(),
        P(),
        P(),
        P(),
        P(),
        P(),
        P(),
        P("exp", None, None),
        P("exp", None, None),
        P("exp", "seq", None),
    )
    out_specs = (
        P("exp", "seq", None),
        P("exp", "seq", None),
        P(),
        P(),
        P(),
        P(),
        P(),
        P(),
        P("exp", None, None),
        P("exp", None, None),
    )
    return jax.shard_map(
        on_device, mesh=mesh, in_specs=in_specs, out_specs=out_specs, check_vma=False
    )
```

```python
import functools
import math

import jax
import jax.numpy as jnp
from jax import lax
from jax.experimental import pallas as pl
from jax.experimental.pallas import tpu as pltpu
from jax.sharding import PartitionSpec as P

HEADS = 12
HEAD_DIM = 64
DOC_MOST = 1024
EPSILON = 1e-05
LOW = -1e30
LOWER = -2e30
LANES = 128
TILE = 256
F32 = jnp.float32
BF16 = jnp.bfloat16
MIB = 1 << 20
COST = 1


def dot(a, b):
    return lax.dot_general(a, b, (((1,), (0,)), ((), ())), preferred_element_type=F32)


def dot_nt(a, b):
    return lax.dot_general(a, b, (((1,), (1,)), ((), ())), preferred_element_type=F32)


def dot_tn(a, b):
    return lax.dot_general(a, b, (((0,), (0,)), ((), ())), preferred_element_type=F32)


def iota(shape, axis):
    return lax.broadcasted_iota(jnp.int32, shape, axis)


def one_hot(ids, width):
    return jnp.where(iota((ids.shape[0], width), 1) == ids, 1.0, 0.0).astype(BF16)


def norm_rows(values):
    center = values - jnp.mean(values, axis=-1, keepdims=True)
    scale = lax.rsqrt(jnp.mean(center * center, axis=-1, keepdims=True) + EPSILON)
    return center * scale, scale


def norm_back(grad, normed, scale):
    inner = jnp.mean(grad * normed, axis=-1, keepdims=True)
    return scale * (grad - jnp.mean(grad, axis=-1, keepdims=True) - normed * inner)


def after(value, *others):
    return lax.optimization_barrier((value, others))[0]


def shape(dims, dtype):
    return jax.ShapeDtypeStruct(dims, dtype)


def call(body, name, out_shape, args, *, grid=(), in_specs=None, out_specs=None, scratch=(),
         scalars=0, aliases=None, flops=0, nbytes=0, special=0, vmem=56):
    outs = out_shape if isinstance(out_shape, (tuple, list)) else [out_shape]
    whole = pl.BlockSpec(memory_space=pltpu.VMEM)
    if in_specs is None:
        in_specs = [whole] * (len(args) - scalars)
    if out_specs is None:
        out_specs = [whole] * len(outs)
        if not isinstance(out_shape, (tuple, list)):
            out_specs = out_specs[0]
    return pl.pallas_call(
        body,
        name=name,
        out_shape=out_shape,
        grid_spec=pltpu.PrefetchScalarGridSpec(
            num_scalar_prefetch=scalars,
            grid=grid,
            in_specs=in_specs,
            out_specs=out_specs,
            scratch_shapes=scratch,
        ),
        input_output_aliases=aliases or {},
        cost_estimate=pl.CostEstimate(flops=COST, bytes_accessed=COST, transcendentals=0),
        compiler_params=pltpu.CompilerParams(vmem_limit_bytes=vmem * MIB),
    )(*args)


def column(row):
    return jnp.broadcast_to(row.astype(F32), (8, row.shape[1])).T[:, :1].astype(jnp.int32)


def route_body(parts, capacity, docs, at_ref, ids_ref, table_ref, rows_ref, segment_ref, slot_ref,
               low_ref, tall_ref, meta_ref, *out_refs):
    ids = column(ids_ref[...])
    count = ids.shape[0]
    lines = table_ref.shape[0]
    picked = dot(one_hot(ids >> 7, lines), table_ref[...].astype(F32).astype(BF16))
    lane = iota((count, LANES), 1)
    choice = jnp.sum(
        jnp.where(lane == (ids & (LANES - 1)), picked, 0.0), axis=1, keepdims=True
    ).astype(jnp.int32)
    mine = lane == choice
    below = jnp.where(iota((count, count), 0) > iota((count, count), 1), 1.0, 0.0).astype(BF16)
    ranks = dot(below, jnp.where(mine, 1.0, 0.0).astype(BF16))
    rank = jnp.sum(jnp.where(mine, ranks, 0.0), axis=1, keepdims=True).astype(jnp.int32)
    slot = (choice ^ at_ref[0]) * capacity + rank
    slot_ref[...] = slot
    rows = rows_ref[...]
    for k in range(parts):
        chosen = one_hot(slot - k * capacity, capacity)
        out_refs[k][...] = dot_tn(chosen, rows).astype(BF16)

    pair_len = low_ref.shape[1]
    pair_at = pl.multiple_of(at_ref[2] * pair_len, pair_len)
    segments = segment_ref[...]
    here = segment_ref[:, pl.ds(pair_at, pair_len)]
    low = jnp.zeros((1, pair_len), F32)
    for d in range(docs):
        start = jnp.sum(jnp.where(segments < d, 1.0, 0.0), axis=1, keepdims=True)
        low = low + jnp.where(here == d, start, 0.0)
    low = low.astype(jnp.int32) - (pair_at - pair_len)
    low_ref[...] = low
    tall_ref[...] = column(low)
    place = iota((1, LANES), 1)
    meta = jnp.where(place == 0, at_ref[1], 0)
    for t in range(pair_len // TILE):
        meta = jnp.where(place == 1 + t, low[:, t * TILE : t * TILE + 1] >> 8, meta)
    meta_ref[...] = meta


def route(at, ids, table, rows, segments, parts, capacity, docs):
    count, width = rows.shape
    pair_len = 2 * count
    outs = [shape((count, 1), jnp.int32), shape((1, pair_len), jnp.int32),
            shape((pair_len, 1), jnp.int32), shape((1, LANES), jnp.int32)]
    outs += [shape((capacity, width), BF16)] * parts
    return call(
        functools.partial(route_body, parts, capacity, docs), "route", outs,
        (at, ids, table, rows, segments), scalars=1,
    )


def vector(ref, at):
    lines = ref.shape[0] // 4
    return jnp.concatenate([ref[at * lines + j : at * lines + j + 1, :] for j in range(lines)], axis=1)


def project_body(skip, core_ref, own_ref, sib_ref, norm_ref, wq_ref, wk_ref, wv_ref, *refs):
    outs = refs[skip:-1]
    held_ref = refs[-1]
    step = pl.program_id(0)
    half = (pl.num_programs(0) - 1) // 2
    before = held_ref[(step + 1) % 2]
    outs[1][...] = dot(before, wk_ref[...]).astype(BF16)
    outs[2][...] = dot(before, wv_ref[...]).astype(BF16)
    if not skip:
        outs[3][...] = dot(before, wq_ref[...]).astype(BF16)
    rows = jnp.where(step < half, own_ref[...], sib_ref[...])
    normed, unused = norm_rows(rows.astype(F32))
    a = (normed * vector(norm_ref, 0) + vector(norm_ref, 1)).astype(BF16)
    held_ref[step % 2] = a
    outs[0][...] = a


def project(core, own, sib, norms, w_qkv, made):
    count, width = own.shape
    mine = width // 2
    half = count // TILE
    base = 0 if made else 2 * half

    def place(i, c):
        return ((i // half) ^ c[0]) * half + i % half

    def now(i, c):
        return (base + place(jnp.minimum(i, 2 * half - 1), c), 0)

    def then(i, c):
        return (base + place(jnp.maximum(i - 1, 0), c), 0)

    in_specs = [
        pl.BlockSpec((TILE, width), lambda i, c: (jnp.minimum(i, half - 1), 0)),
        pl.BlockSpec((TILE, width), lambda i, c: (jnp.clip(i - half, 0, half - 1), 0)),
        pl.BlockSpec(norms.shape, lambda i, c: (0, 0)),
    ] + [
        pl.BlockSpec((width, mine), functools.partial(lambda t, i, c: (0, 2 * t + c[0]), t))
        for t in range(3)
    ]
    args = [core, own, sib, norms, w_qkv, w_qkv, w_qkv]
    outs = [shape((4 * count, width), BF16)] + [shape((4 * count, mine), BF16)] * 2
    out_specs = [
        pl.BlockSpec((TILE, width), now),
        pl.BlockSpec((TILE, mine), then),
        pl.BlockSpec((TILE, mine), then),
    ]
    aliases = {}
    if made:
        in_specs += [pl.BlockSpec(memory_space=pl.ANY)] * 3
        aliases = {7: 0, 8: 1, 9: 2}
        args += list(made)
    else:
        outs.append(shape((2 * count, mine), BF16))
        out_specs.append(
            pl.BlockSpec((TILE, mine), lambda i, c: (place(jnp.maximum(i - 1, 0), c), 0))
        )
    return call(
        functools.partial(project_body, 3 if made else 0), "project", outs, args,
        grid=(2 * half + 1,), in_specs=in_specs, out_specs=out_specs, scalars=1, aliases=aliases,
        scratch=[pltpu.VMEM((2, TILE, width), BF16)],
    )


def masked_heads(block):
    lane = iota(block.shape, 1)
    zero = jnp.zeros((), block.dtype)
    return [
        jnp.where(lane < HEAD_DIM, block, zero),
        jnp.where(lane < HEAD_DIM, zero, block),
    ]


def flip(block):
    return block.astype(F32).T.astype(block.dtype)


def lanes_of(group):
    return slice(group * LANES, (group + 1) * LANES)


def put_heads(heads_ref, q_ref):
    def some(t, unused):
        here = pl.ds(pl.multiple_of(t * TILE, TILE), TILE)
        block = q_ref[here, :] * jnp.asarray(HEAD_DIM**-0.5, BF16)
        for g in range(q_ref.shape[1] // LANES):
            for h, part in enumerate(masked_heads(block[:, lanes_of(g)])):
                heads_ref[2 * g + h, here, :] = part
        return unused

    lax.fori_loop(0, q_ref.shape[0] // TILE, some, 0)


def tile_mask(begin, low, high):
    place = begin + iota((TILE, TILE), 0)
    return (place >= low) & (place <= high)


def attend_body(meta_ref, q_ref, k_ref, v_ref, lo_ref, own_ref, sib_ref, all_ref, tall_ref,
                log_ref, heads_ref, acc_ref, rows_ref):
    total, mine = q_ref.shape
    half = total // 2
    heads = range(mine // HEAD_DIM)
    put_heads(heads_ref, q_ref)
    core = meta_ref[0, 0]

    def tile(t, unused):
        at = pl.multiple_of(t * TILE, TILE)
        here = pl.ds(at, TILE)
        low = lo_ref[here, :]
        high = total + at + iota((TILE, 1), 0)
        acc_ref[...] = jnp.zeros_like(acc_ref)

        def step(j, state):
            begin = pl.multiple_of(j * TILE, TILE)
            there = pl.ds(begin, TILE)
            place = begin + iota((TILE, TILE), 1)
            allowed = (place >= low) & (place <= high)
            scores = [
                jnp.where(
                    allowed, dot_nt(heads_ref[h, here, :], k_ref[there, lanes_of(h // 2)]), LOWER
                )
                for h in heads
            ]
            tops = [
                jnp.maximum(state[2 * h], jnp.max(scores[h], axis=1, keepdims=True)) for h in heads
            ]
            shares = [jnp.exp(scores[h] - tops[h]) for h in heads]
            factors = [jnp.exp(state[2 * h] - tops[h]) for h in heads]
            sums = [
                state[2 * h + 1] * factors[h] + jnp.sum(shares[h], axis=1, keepdims=True)
                for h in heads
            ]
            more = [dot(shares[h].astype(BF16), v_ref[there, lanes_of(h // 2)]) for h in heads]
            for h in heads:
                acc_ref[h] = acc_ref[h] * factors[h] + more[h]
            return tuple(x for h in heads for x in (tops[h], sums[h]))

        first = (jnp.full((TILE, 1), LOW, F32), jnp.zeros((TILE, 1), F32))
        state = lax.fori_loop(
            meta_ref[0, 1 + t], total // TILE + t + 1, step, first * len(heads)
        )
        lane = iota((TILE, LANES), 1)
        logs = jnp.zeros((TILE, LANES), F32)
        for h in heads:
            logs = jnp.where(lane == h, state[2 * h] + jnp.log(state[2 * h + 1]), logs)
        log_ref[:, here] = logs.T[: log_ref.shape[0], :]
        for g in range(mine // LANES):
            left = acc_ref[2 * g] / state[4 * g + 1]
            right = acc_ref[2 * g + 1] / state[4 * g + 3]
            out = jnp.where(lane < HEAD_DIM, left, right)
            rows_ref[here, lanes_of(g)] = out
            tall_ref[lanes_of(g), here] = out.T
        return unused

    lax.fori_loop(0, total // TILE, tile, 0)

    def some(t, unused):
        at = pl.multiple_of(t * TILE, TILE)
        here = pl.ds(at, TILE)
        own_at = pl.ds(pl.multiple_of(core * half + at, TILE), TILE)
        sib_at = pl.ds(pl.multiple_of((1 - core) * half + at, TILE), TILE)
        all_ref[own_at, :] = rows_ref[own_at, :].astype(BF16)
        all_ref[sib_at, :] = rows_ref[sib_at, :].astype(BF16)
        own_ref[here, :] = rows_ref[own_at, :].astype(BF16)
        sib_ref[here, :] = rows_ref[sib_at, :].astype(BF16)
        return unused

    lax.fori_loop(0, half // TILE, some, 0)


def attend(meta, q, k, v, low):
    total, mine = q.shape
    heads = mine // HEAD_DIM
    outs = [
        shape((total // 2, mine), BF16),
        shape((total // 2, mine), BF16),
        shape((total, mine), BF16),
        shape((mine, total), F32),
        shape((-(-heads // 8) * 8, total), F32),
    ]
    return call(
        attend_body, "attend", outs, (meta, q, k, v, low), scalars=1,
        scratch=[pltpu.VMEM((heads, total, LANES), BF16), pltpu.VMEM((heads, TILE, LANES), F32),
                 pltpu.VMEM((total, mine), F32)],
    )


def fetch(pairs, sems):
    copies = [pltpu.make_async_copy(a, b, sems.at[i]) for i, (a, b) in enumerate(pairs)]
    for copy in copies:
        copy.start()
    return [copy.wait for copy in copies]


def both_rows(core, own, sib, rows_ref):
    half = own.shape[0]
    return [
        (own, rows_ref.at[pl.ds(pl.multiple_of(core * half, half), half), :]),
        (sib, rows_ref.at[pl.ds(pl.multiple_of((1 - core) * half, half), half), :]),
    ]


def attend_back_body(meta_ref, q_hbm, k_hbm, v_hbm, own_hbm, sib_hbm, wo_hbm, tall_hbm, log_ref,
                     lo_ref, gq_ref, gk_ref, gv_ref, rows_ref, heads_ref, grads_ref, delta_ref,
                     kt_ref, gqt_ref, gks_ref, gvs_ref, q_ref, k_ref, v_ref, wo_ref, tall_ref,
                     sems):
    total, mine = q_ref.shape
    heads = mine // HEAD_DIM
    core = meta_ref[0, 0]
    mine_at = pl.ds(pl.multiple_of(core * mine, mine), mine)
    waits = fetch(
        both_rows(core, own_hbm, sib_hbm, rows_ref)
        + [(wo_hbm.at[mine_at, :], wo_ref), (tall_hbm, tall_ref), (q_hbm, q_ref), (k_hbm, k_ref),
           (v_hbm, v_ref)],
        sems,
    )

    def clear(t, unused):
        here = pl.ds(pl.multiple_of(t * TILE, TILE), TILE)
        gks_ref[here, :] = jnp.zeros((TILE, mine), F32)
        gvs_ref[here, :] = jnp.zeros((TILE, mine), F32)
        return unused

    lax.fori_loop(0, 2 * total // TILE, clear, 0)
    gqt_ref[...] = jnp.zeros_like(gqt_ref)
    for wait in waits[:4]:
        wait()
    weights = wo_ref[...]

    def begin(t, unused):
        here = pl.ds(pl.multiple_of(t * TILE, TILE), TILE)
        grads = dot_nt(rows_ref[here, :], weights).astype(BF16)
        turned = grads.astype(F32).T * tall_ref[:, here]
        for h in range(heads):
            span = slice(h * HEAD_DIM, (h + 1) * HEAD_DIM)
            delta_ref[h : h + 1, here] = jnp.sum(turned[span, :], axis=0, keepdims=True)
        for g in range(mine // LANES):
            for h, part in enumerate(masked_heads(grads[:, lanes_of(g)])):
                grads_ref[2 * g + h, here, :] = part
        return unused

    lax.fori_loop(0, total // TILE, begin, 0, unroll=2)
    waits[4]()
    put_heads(heads_ref, q_ref)
    waits[5]()

    def turn(t, unused):
        here = pl.ds(pl.multiple_of(t * TILE, TILE), TILE)
        kt_ref[:, here] = flip(k_ref[here, :])
        return unused

    lax.fori_loop(0, 2 * total // TILE, turn, 0, unroll=2)
    waits[6]()

    def tile(t, unused):
        at = pl.multiple_of(t * TILE, TILE)
        here = pl.ds(at, TILE)
        low = lo_ref[:, here]
        high = total + at + iota((1, TILE), 1)

        logs = [log_ref[h : h + 1, here] for h in range(heads)]
        deltas = [delta_ref[h : h + 1, here] for h in range(heads)]

        def step(j, carry):
            begin = pl.multiple_of(j * TILE, TILE)
            there = pl.ds(begin, TILE)
            allowed = tile_mask(begin, low, high)
            every = range(heads)
            queries = [heads_ref[h, here, :] for h in every]
            grads = [grads_ref[h, here, :] for h in every]
            scores = [dot_nt(k_ref[there, lanes_of(h // 2)], queries[h]) for h in every]
            grad_soft = [dot_nt(v_ref[there, lanes_of(h // 2)], grads[h]) for h in every]
            soft = [jnp.exp(jnp.where(allowed, scores[h], LOWER) - logs[h]) for h in every]
            grad_scores = [(soft[h] * (grad_soft[h] - deltas[h])).astype(BF16) for h in every]
            soft = [s.astype(BF16) for s in soft]
            gv = [dot(soft[h], grads[h]) for h in every]
            gk = [dot(grad_scores[h], queries[h]) for h in every]
            gq = [
                dot(kt_ref[h * HEAD_DIM : (h + 1) * HEAD_DIM, there], grad_scores[h])
                for h in every
            ]
            for g in range(heads // 2):
                gvs_ref[there, lanes_of(g)] += gv[2 * g] + gv[2 * g + 1]
                gks_ref[there, lanes_of(g)] += gk[2 * g] + gk[2 * g + 1]
            for h in every:
                gqt_ref[h * HEAD_DIM : (h + 1) * HEAD_DIM, here] += gq[h]
            return carry

        return lax.fori_loop(meta_ref[0, 1 + t], total // TILE + t + 1, step, unused)

    lax.fori_loop(0, total // TILE, tile, 0)

    def finish_queries(t, unused):
        here = pl.ds(pl.multiple_of(t * TILE, TILE), TILE)
        gq_ref[here, :] = (gqt_ref[:, here].T * (HEAD_DIM**-0.5)).astype(BF16)
        return unused

    def finish_keys(t, unused):
        here = pl.ds(pl.multiple_of(t * TILE, TILE), TILE)
        gk_ref[here, :] = gks_ref[here, :].astype(BF16)
        gv_ref[here, :] = gvs_ref[here, :].astype(BF16)
        return unused

    lax.fori_loop(0, total // TILE, finish_queries, 0)
    lax.fori_loop(0, 2 * total // TILE, finish_keys, 0)


def attend_back(meta, q, k, v, own, sib, w_out, tall, logs, low):
    total, mine = q.shape
    width = own.shape[1]
    heads = mine // HEAD_DIM
    outs = [
        shape((total, mine), BF16),
        shape((2 * total, mine), BF16),
        shape((2 * total, mine), BF16),
    ]
    return call(
        attend_back_body, "attend_back", outs,
        (meta, q, k, v, own, sib, w_out, tall, logs, low), scalars=1,
        in_specs=[pl.BlockSpec(memory_space=pl.ANY)] * 7 + [pl.BlockSpec(memory_space=pltpu.VMEM)] * 2,
        scratch=[pltpu.VMEM((total, width), BF16), pltpu.VMEM((heads, total, LANES), BF16),
                 pltpu.VMEM((heads, total, LANES), BF16), pltpu.VMEM(logs.shape, F32),
                 pltpu.VMEM((mine, 2 * total), BF16), pltpu.VMEM((mine, total), F32),
                 pltpu.VMEM((2 * total, mine), F32), pltpu.VMEM((2 * total, mine), F32),
                 pltpu.VMEM(q.shape, BF16), pltpu.VMEM(k.shape, BF16), pltpu.VMEM(v.shape, BF16),
                 pltpu.VMEM((mine, width), BF16), pltpu.VMEM(tall.shape, F32),
                 pltpu.SemaphoreType.DMA((7,))],
    )


def dense_body(subs, sub, chip_ref, a_hbm, gq_hbm, gk_hbm, gv_hbm, all_hbm, own_hbm, sib_hbm,
               *refs):
    piece_refs = refs[:4]
    dense_ref, rows_ref, short_ref, long_ref, sems = refs[4:]
    unused, total, mine = short_ref.shape
    half = total // 2
    width = rows_ref.shape[1]
    lines = width // subs
    quarter = subs * sub
    core = chip_ref[0]
    own_at = pl.multiple_of(2 * total + core * half, half)
    sib_at = pl.multiple_of(2 * total + (1 - core) * half, half)
    waits = fetch(
        [(own_hbm, rows_ref.at[pl.ds(own_at, half), :]),
         (sib_hbm, rows_ref.at[pl.ds(sib_at, half), :]),
         (a_hbm, rows_ref.at[pl.ds(0, 2 * total), :]),
         (gq_hbm, short_ref.at[0]), (all_hbm, short_ref.at[1]),
         (gk_hbm, long_ref.at[0]), (gv_hbm, long_ref.at[1])],
        sems,
    )

    def put(kind, turned):
        for j in range(mine // LANES):
            block = turned[lanes_of(j), :].T.astype(BF16)
            for at in range(subs):
                first = pl.multiple_of(kind * quarter + at * sub + j * lines, 16)
                dense_ref[pl.ds(first, lines), :] = block[at * lines : (at + 1) * lines, :]

    def short(i, unused):
        rows = rows_ref[pl.ds(pl.multiple_of((1 + i) * total, total), total), :]
        put(3 * i, dot_tn(short_ref[i], rows))
        return unused

    def long(i, unused):
        put(1 + i, dot_tn(long_ref[i], rows_ref[: 2 * total, :]))
        return unused

    for wait in waits[:5]:
        wait()
    lax.fori_loop(0, 2, short, 0)
    waits[5]()
    waits[6]()
    lax.fori_loop(0, 2, long, 0)
    spare = sub - mine // LANES * lines
    if spare:
        for at in range(4 * subs):
            dense_ref[(at + 1) * sub - spare : (at + 1) * sub, :] = jnp.zeros((spare, LANES), BF16)
    for p in range(2):
        side = chip_ref[1 + p]
        for r, which in enumerate((side, 1 - side)):
            for at in range(subs):
                from_at = pl.multiple_of((2 * p + which) * quarter + at * sub, 16)
                to_at = pl.multiple_of((at ^ chip_ref[3 + p]) * sub, 16)
                piece_refs[2 * p + r][pl.ds(to_at, sub), :] = dense_ref[pl.ds(from_at, sub), :]


def dense_pieces(chip, a, gq, gk, gv, attn_all, own, sib, subs, sub):
    return call(
        functools.partial(dense_body, subs, sub), "dense",
        [shape((subs * sub, LANES), BF16)] * 4,
        (chip, a, gq, gk, gv, attn_all, own, sib), scalars=1,
        in_specs=[pl.BlockSpec(memory_space=pl.ANY)] * 7,
        scratch=[pltpu.VMEM((4 * subs * sub, LANES), BF16),
                 pltpu.VMEM((3 * gq.shape[0], a.shape[1]), BF16),
                 pltpu.VMEM((2, *gq.shape), BF16), pltpu.VMEM((2, *gk.shape), BF16),
                 pltpu.SemaphoreType.DMA((7,))],
    )


def lift_body(parts, capacity, core_ref, own_ref, other_ref, w_ref, x_ref, norm_ref, slot_ref,
              resid_ref, *out_refs):
    mine = own_ref.shape[1]
    core = core_ref[0]
    own_at = pl.ds(pl.multiple_of(core * mine, mine), mine)
    other_at = pl.ds(pl.multiple_of((1 - core) * mine, mine), mine)
    *out_refs, rows_ref = out_refs

    def some(t, unused):
        here = pl.ds(pl.multiple_of(t * TILE, TILE), TILE)
        more = dot(own_ref[here, :], w_ref[own_at, :]) + dot(other_ref[here, :], w_ref[other_at, :])
        resid = x_ref[here, :].astype(F32) + more
        resid_ref[here, :] = resid
        normed, scale = norm_rows(resid)
        rows_ref[here, :] = (normed * vector(norm_ref, 2) + vector(norm_ref, 3)).astype(BF16)
        return unused

    lax.fori_loop(0, own_ref.shape[0] // TILE, some, 0)
    slot = slot_ref[...]
    for k in range(parts):
        chosen = one_hot(slot - k * capacity, capacity)
        out_refs[k][...] = dot_tn(chosen, rows_ref[...]).astype(BF16)


def lift(core, own, other, w_out, x, norms, slot, parts, capacity):
    count, width = x.shape
    outs = [shape((count, width), F32)] + [shape((capacity, width), BF16)] * parts
    return call(
        functools.partial(lift_body, parts, capacity), "lift", outs,
        (core, own, other, w_out, x, norms, slot), scratch=[pltpu.VMEM((count, width), BF16)],
        scalars=1, flops=2 * count * width * (width + parts * capacity),
    )


GATE_A = math.sqrt(2.0 / math.pi)
GATE_B = 0.044715


def expert_body(sub, rows_ref, grad_ref, up_ref, down_ref, tall_ref, pre_ref, back_ref, out_ref,
                turned_ref, back_acc, out_acc):
    step = pl.program_id(0)

    @pl.when(step == 0)
    def _():
        back_acc[...] = jnp.zeros_like(back_acc)
        out_acc[...] = jnp.zeros_like(out_acc)
        turned_ref[...] = flip(rows_ref[...])

    parts = [slice(s * sub, (s + 1) * sub) for s in range(down_ref.shape[0] // sub)]
    pres = [dot(rows_ref[...], up_ref[:, part]) for part in parts]
    grads = [dot_nt(grad_ref[...], down_ref[part, :]) for part in parts]
    hids, slopes = [], []
    for pre in pres:
        square = pre * pre
        bend = jnp.tanh(GATE_A * (pre + GATE_B * (square * pre)))
        half = 0.5 + 0.5 * bend
        hids.append(pre * half)
        slopes.append(
            half + (pre * (1.0 - bend * bend)) * (0.5 * GATE_A + (1.5 * GATE_A * GATE_B) * square)
        )
    low = jnp.concatenate([(g * s).astype(BF16) for g, s in zip(grads, slopes)], axis=1)
    back_acc[...] += dot_nt(low, up_ref[...])
    out_acc[...] += dot(jnp.concatenate([h.astype(BF16) for h in hids], axis=1), down_ref[...])
    pre_ref[...] = low
    for part, hid in zip(parts, hids):
        tall_ref[part, :] = hid.T.astype(BF16)

    @pl.when(step == pl.num_programs(0) - 1)
    def _():
        back_ref[...] = back_acc[...].astype(BF16)
        out_ref[...] = out_acc[...].astype(BF16)


def expert(rows, grads, w_up, w_down, sub=256):
    count, width = rows.shape
    hidden = w_up.shape[1]
    block = width
    const = pl.BlockSpec((count, width), lambda j: (0, 0))
    return call(
        functools.partial(expert_body, sub), "expert",
        [shape((hidden, count), BF16), shape((count, hidden), BF16), shape((count, width), BF16),
         shape((count, width), BF16), shape((width, count), BF16)],
        (rows, grads, w_up, w_down), grid=(hidden // block,),
        in_specs=[const, const, pl.BlockSpec((width, block), lambda j: (0, j)),
                  pl.BlockSpec((block, width), lambda j: (j, 0))],
        out_specs=[pl.BlockSpec((block, count), lambda j: (j, 0)),
                   pl.BlockSpec((count, block), lambda j: (0, j)), const, const,
                   pl.BlockSpec((width, count), lambda j: (0, 0))],
        scratch=[pltpu.VMEM((count, width), F32)] * 2,
    )


def expert_grad_body(parts, subs, chip_ref, *refs):
    turned, grads, talls, pres = (refs[parts * t : parts * (t + 1)] for t in range(4))
    *outs, held_ref, sems = refs[4 * parts :]
    width = held_ref.shape[2]
    lines = width // subs
    step = pl.program_id(0)
    steps = len(outs)
    slot = step % 2

    def copy(t, at):
        return pltpu.make_async_copy(held_ref.at[at], outs[t], sems.at[at])

    @pl.when(step >= 2)
    def _():
        copy(0, slot).wait()

    def product(left, right):
        out = None
        for a, b in zip(left, right):
            more = dot(a[...], b[...])
            out = more if out is None else out + more
        return out.astype(BF16)

    half = steps // 2
    side, mask = chip_ref[1 + step % half], chip_ref[3 + step % half]
    pairs = ((product(turned, pres), side == 0), (product(talls, grads), side == 1))
    for value, stays in pairs:
        base = jnp.where(stays, width, 0)
        for at in range(subs):
            first = pl.multiple_of(base + (at ^ mask) * lines, 16)
            held_ref[slot, pl.ds(first, lines), :] = value[at * lines : (at + 1) * lines, :]

    for t in range(steps):

        @pl.when(step == t)
        def _(t=t):
            copy(t, t % 2).start()

    @pl.when(step == steps - 1)
    def _():
        copy(0, 0).wait()
        copy(0, 1).wait()


def expert_grad(chip, turned, grads, talls, pres, subs):
    parts = len(grads)
    count, width = grads[0].shape
    blocks = talls[0].shape[0] // width
    half = blocks // 2

    def column(i, m):
        return jnp.where(i < half, (1 - m[0]) * half, m[0] * half - half) + i

    const = lambda dims: pl.BlockSpec(dims, lambda i, m: (0, 0))
    return call(
        functools.partial(expert_grad_body, parts, subs), "expert_grad",
        [shape((2 * width, width), BF16)] * blocks,
        (chip, *turned, *grads, *talls, *pres), grid=(blocks,), scalars=1,
        in_specs=[const((width, count))] * parts + [const((count, width))] * parts
        + [pl.BlockSpec((width, count), lambda i, m: (column(i, m), 0))] * parts
        + [pl.BlockSpec((count, width), lambda i, m: (0, column(i, m)))] * parts,
        out_specs=[pl.BlockSpec(memory_space=pl.ANY)] * blocks,
        scratch=[pltpu.VMEM((2, 2 * width, width), BF16), pltpu.SemaphoreType.DMA((2,))],
    )


def widen_body(skip, meta_ref, *refs):
    pairs, (up_out, down_out) = refs[:4], refs[4 + skip :]
    second = pl.program_id(0) >= pl.num_programs(0) // 2
    first = meta_ref[1 + pl.program_id(0) // (pl.num_programs(0) // 2)] == 0
    mine = jnp.where(second, pairs[2][...], pairs[0][...])
    theirs = jnp.where(second, pairs[3][...], pairs[1][...])
    up_out[...] = jnp.where(first, mine, theirs).astype(F32)
    down_out[...] = jnp.where(first, theirs, mine).astype(F32)


def widen(core, sides, masks, mine, theirs, made, hidden, subs):
    width = mine[0].shape[1]
    rows = width // subs
    meta = jnp.stack([core, *sides, *masks]).astype(jnp.int32)

    def index(p):
        def at(i, m):
            here = jnp.clip(i - p * subs, 0, subs - 1)
            return (here ^ m[3 + p], 0)

        return at

    blocks = [pl.BlockSpec((rows, width), index(p)) for p in (0, 0, 1, 1)]
    column = lambda i, m: 2 * m[0] + i // subs
    return call(
        functools.partial(widen_body, len(made)), "widen",
        [shape((width, hidden), F32), shape((hidden, width), F32)],
        (meta, mine[0], theirs[0], mine[1], theirs[1], *made), grid=(2 * subs,), scalars=1,
        in_specs=blocks + [pl.BlockSpec(memory_space=pl.ANY)] * len(made),
        out_specs=[pl.BlockSpec((rows, width), lambda i, m: (i % subs, column(i, m))),
                   pl.BlockSpec((rows, width), lambda i, m: (column(i, m) * subs + i % subs, 0))],
        aliases={5: 0, 6: 1} if made else None,
    )


def collect(slot, part_refs):
    total = None
    for k, ref in enumerate(part_refs):
        capacity = ref.shape[0]
        more = dot(one_hot(slot - k * capacity, capacity), ref[...])
        total = more if total is None else total + more
    return total


def lower_body(parts, slot_ref, resid_ref, cot_ref, norm_ref, *refs):
    grads = collect(slot_ref[...], refs[:parts])
    gr_ref, low_ref, gain_out, bias_out = refs[parts:]
    normed, scale = norm_rows(resid_ref[...])

    @pl.when(pl.program_id(0) == 0)
    def _():
        gain_out[...] = jnp.zeros_like(gain_out)
        bias_out[...] = jnp.zeros_like(bias_out)

    gain_out[...] += jnp.sum(grads * normed, axis=0, keepdims=True)
    bias_out[...] += jnp.sum(grads, axis=0, keepdims=True)
    gr = cot_ref[...].astype(F32) + norm_back(grads * vector(norm_ref, 2), normed, scale)
    gr_ref[...] = gr
    low_ref[...] = gr.astype(BF16)


def row_specs(dims, *whole):
    return [pl.BlockSpec((TILE, d), lambda i: (i, 0)) for d in dims] + [
        pl.BlockSpec(w.shape, lambda i: (0, 0)) for w in whole
    ]


def lower(slot, resid, cot, norms, back):
    parts = len(back)
    count, width = resid.shape
    outs = [shape((count, width), F32), shape((count, width), BF16),
            shape((1, width), F32), shape((1, width), F32)]
    return call(
        functools.partial(lower_body, parts), "lower", outs, (slot, resid, cot, norms, *back),
        grid=(count // TILE,), in_specs=row_specs((1, width, width), norms, *back),
        out_specs=row_specs((width, width), outs[2], outs[3]),
    )


def finish_body(slot_ref, resid_ref, *refs):
    refs[-1][...] = (resid_ref[...] + collect(slot_ref[...], refs[:-1])).astype(BF16)


def finish(slot, resid, parts):
    count, width = resid.shape
    return call(
        finish_body, "finish", shape(resid.shape, BF16), (slot, resid, *parts),
        grid=(count // TILE,), in_specs=row_specs((1, width), *parts),
        out_specs=row_specs((width,))[0],
    )


def project_back_body(half, core_ref, own_ref, sib_ref, hal_ref, has_ref, gq_ref, gk_ref, gv_ref,
                      wq_ref, wk_ref, wv_ref, keep_ref, send_ref, halo_ref, gain_ref, bias_ref):
    step = pl.program_id(0)
    rows = jnp.where(
        step < 2 * half,
        jnp.where(step < half, own_ref[...], sib_ref[...]),
        jnp.where(step < 3 * half, hal_ref[...], has_ref[...]),
    )
    normed, unused = norm_rows(rows.astype(F32))
    here = step < 2 * half
    ga = dot_nt(gk_ref[...], wk_ref[...]) + dot_nt(gv_ref[...], wv_ref[...])
    gq = jnp.where(here, gq_ref[...], jnp.zeros_like(gq_ref))
    ga = ga + dot_nt(gq, wq_ref[...])

    @pl.when(step == 0)
    def _():
        gain_ref[...] = jnp.zeros_like(gain_ref)
        bias_ref[...] = jnp.zeros_like(bias_ref)

    gain_ref[...] += jnp.sum(ga * normed, axis=0, keepdims=True)
    bias_ref[...] += jnp.sum(ga, axis=0, keepdims=True)

    @pl.when(step < half)
    def _():
        keep_ref[...] = ga

    @pl.when((step // half) % 2 == 1)
    def _():
        send_ref[...] = ga.astype(BF16)

    @pl.when(step // half == 2)
    def _():
        halo_ref[...] = ga


def project_back(core, own, sib, hal, has, gq, gk, gv, w_qkv):
    count, width = own.shape
    mine = gq.shape[1]
    half = count // TILE

    def at(t):
        return lambda i, c: (jnp.clip(i - t * half, 0, half - 1), 0)

    def place(i, c):
        return jnp.where(i < 2 * half, 2 * half, 0) + (((i // half) % 2) ^ c[0]) * half + i % half

    def sent(i, c):
        late = half + jnp.clip(i - 3 * half, 0, half - 1)
        return (jnp.where(i < 2 * half, jnp.clip(i - half, 0, half - 1), late), 0)

    row = pl.BlockSpec((1, width), lambda i, c: (0, 0))
    in_specs = [pl.BlockSpec((TILE, width), at(t)) for t in range(4)] + [
        pl.BlockSpec((TILE, mine), lambda i, c: (jnp.maximum(place(i, c) - 2 * half, 0), 0)),
        pl.BlockSpec((TILE, mine), lambda i, c: (place(i, c), 0)),
        pl.BlockSpec((TILE, mine), lambda i, c: (place(i, c), 0)),
    ] + [
        pl.BlockSpec((width, mine), functools.partial(lambda t, i, c: (0, 2 * t + c[0]), t))
        for t in range(3)
    ]
    return call(
        functools.partial(project_back_body, half), "project_back",
        [shape((count, width), F32), shape((2 * count, width), BF16), shape((count, width), F32),
         shape((1, width), F32), shape((1, width), F32)],
        (core, own, sib, hal, has, gq, gk, gv, w_qkv, w_qkv, w_qkv),
        grid=(4 * half,), in_specs=in_specs, scalars=1,
        out_specs=[pl.BlockSpec((TILE, width), at(0)), pl.BlockSpec((TILE, width), sent),
                   pl.BlockSpec((TILE, width), at(2)), row, row],
        flops=20 * count * width * mine,
    )


def close_body(x_ref, gr_ref, keep_ref, near_ref, far_ref, norm_ref, out_ref):
    ga = keep_ref[...] + near_ref[...].astype(F32) + far_ref[...].astype(F32)
    normed, scale = norm_rows(x_ref[...].astype(F32))
    out_ref[...] = gr_ref[...] + norm_back(ga * vector(norm_ref, 0), normed, scale)


def close(x, gr, keep, near, far, norms):
    count, width = x.shape
    block = pl.BlockSpec((TILE, width), lambda i: (i, 0))
    return call(
        close_body, "close", shape((count, width), F32), (x, gr, keep, near, far, norms),
        grid=(count // TILE,),
        in_specs=[block] * 5 + [pl.BlockSpec(norms.shape, lambda i: (0, 0))], out_specs=block,
    )


def swap(block, axis, distance):
    return lax.ppermute(block, axis, [(i, i ^ distance) for i in range(lax.axis_size(axis))])


def trade(block, axis):
    return lax.all_to_all(block, axis, split_axis=0, concat_axis=0, tiled=True)


def shift(block, axis, distance):
    size = lax.axis_size(axis)
    route = [(i, i + distance) for i in range(size) if 0 <= i + distance < size]
    return lax.ppermute(block, axis, route)


def total(terms):
    return sum(t.astype(F32) for t in terms).astype(BF16)


def add(a, b):
    return total([a, b])


def at_index(block, index):
    return lax.dynamic_index_in_dim(block, index, 0, keepdims=False)


def scatter_steps(pieces, orders):
    pairs = list(pieces)
    for s in range(len(orders[0])):
        arrived = yield [(goes, "seq", bits[s]) for (stays, goes), bits in zip(pairs, orders)]
        terms = [stays + [got] for (stays, goes), got in zip(pairs, arrived)]
        if s + 1 < len(orders[0]):
            half = terms[0][0].shape[0] // 2
            pairs = [
                ([total([t[half:] for t in terms_p])], total([t[:half] for t in terms_p]))
                for terms_p in terms
            ]
    return [total(terms_p) for terms_p in terms]


def gather_steps(parts, orders):
    parts = list(parts)
    for s in reversed(range(1, len(orders[0]))):
        arrived = yield [(part, "seq", bits[s]) for part, bits in zip(parts, orders)]
        parts = [jnp.concatenate([got, part], axis=0) for got, part in zip(arrived, parts)]
    return parts


def dense_steps(pieces, orders):
    sources = lax.axis_size("exp")
    parts = yield from scatter_steps(pieces, orders)
    joined = jnp.stack([p.reshape(sources, -1, LANES) for p in parts], axis=1)
    (got,) = yield [(joined, "exp", 0)]
    own = jnp.sum(got.astype(F32), axis=0).astype(BF16)
    (got,) = yield [(jnp.broadcast_to(own, (sources, *own.shape)), "exp", 0)]
    parts = [got[:, p].reshape(-1, LANES) for p in range(len(orders))]
    return (yield from gather_steps(parts, orders))


def expert_steps(pieces, orders):
    parts = yield from scatter_steps(pieces, orders)
    return (yield from gather_steps(parts, orders))


def one_step(sends):
    return (yield sends)


def across(parts, orders):
    return Stream(one_step([(part, "seq", bits[0]) for part, bits in zip(parts, orders)]))


def beside(parts):
    return Stream(one_step([(part, "seq", 1) for part in parts]))


def small_steps(value, hops):
    for hop in hops:
        (got,) = yield [(value, *hop)]
        value = value + got
    return value


class Stream:
    def __init__(self, steps):
        self.steps = steps
        self.result = None
        self.sent = []
        self.go(None)

    def go(self, arrived):
        try:
            sends = self.steps.send(arrived)
        except StopIteration as stop:
            self.sent, self.raw, self.result = [], [], stop.value
        else:
            self.raw = [send[0] for send in sends]
            self.sent = [swap(*send) if send[2] else trade(*send[:2]) for send in sends]


def meet(streams, others=()):
    streams = [stream for stream in streams if stream.sent]
    arrived, others = lax.optimization_barrier(([stream.sent for stream in streams], others))
    before = []
    for stream, got in zip(streams, arrived):
        stream.go(after(got, before) if before else got)
        before = before + stream.raw
    return others


def spread_columns_body(cols, chip_ref, *refs):
    out_ref = refs[-1]
    first = chip_ref[0] == 0
    own, sib = refs[:4], refs[4:8]
    picks = [
        (0, chip_ref[1] == 0, 0, 1),
        (1, chip_ref[1] == 1, 0, 1),
        (2, chip_ref[2] == 0, 2, 3),
    ]
    for kind, mine, here, there in picks:
        for j in range(cols):
            a, b = (jnp.where(mine, t[here][0, j], t[there][0, j]).astype(F32) for t in (own, sib))
            left = 2 * kind * cols + j
            out_ref[:, lanes_of(left)] = jnp.where(first, a, b)
            out_ref[:, lanes_of(left + cols)] = jnp.where(first, b, a)


def spread_rows_body(chip_ref, *refs):
    out_ref = refs[-1]
    own = pl.program_id(0) == chip_ref[0]
    mine = chip_ref[2] == 1
    subs, cols, lines, unused = refs[0].shape
    for at in range(subs):
        from_at = at ^ chip_ref[4]
        for j in range(cols):
            a, b = (
                jnp.where(mine, refs[t][from_at, j], refs[t + 1][from_at, j]) for t in (0, 2)
            )
            out_ref[lanes_of(j), at * lines : (at + 1) * lines] = (
                jnp.where(own, a, b).astype(F32).T
            )


def spread(chip, own, sib, width, mine, subs):
    cols = mine // LANES
    lines = width // subs
    block = math.gcd(lines, 192)

    def view(t):
        return t.reshape(subs, -1, LANES)[:, : cols * lines].reshape(subs, cols, lines, LANES)

    def part(p):
        def index(i, m):
            return ((i * block // lines) ^ m[3 + p], 0, i % (lines // block), 0)

        return pl.BlockSpec((1, cols, block, LANES), index)

    parts = [[view(t) for pair in side for t in pair] for side in (own, sib)]
    grad_qkv = call(
        functools.partial(spread_columns_body, cols), "spread_columns",
        shape((width, 3 * width), F32), (chip, *parts[0], *parts[1]), grid=(width // block,),
        scalars=1, in_specs=[part(0), part(0), part(1), part(1)] * 2,
        out_specs=pl.BlockSpec((block, 3 * width), lambda i, m: (i, 0)),
    )
    whole = pl.BlockSpec((subs, cols, lines, LANES), lambda i, m: (0, 0, 0, 0))
    grad_out = call(
        spread_rows_body, "spread_rows", shape((width, width), F32),
        (chip, *parts[0][2:], *parts[1][2:]), grid=(2,), scalars=1, in_specs=[whole] * 4,
        out_specs=pl.BlockSpec((mine, width), lambda i, m: (i, 0)),
    )
    return grad_qkv, grad_out


def on_device(
    layer_input,
    token_ids,
    segment_ids,
    hash_table,
    first_gain,
    first_bias,
    second_gain,
    second_bias,
    w_qkv,
    w_out,
    w_up,
    w_down,
    cotangent,
):
    x = layer_input[0]
    cot = cotangent[0]
    local_len, width = x.shape
    mine = width // 2
    sources = lax.axis_size("exp")
    ring = lax.axis_size("seq")
    capacity = 2 * local_len // sources
    seq_at = lax.axis_index("seq")
    exp_at = lax.axis_index("exp")
    core = (seq_at % 2).astype(jnp.int32)
    core_arg = core.reshape(1)
    norms = jnp.concatenate([first_gain, first_bias, second_gain, second_bias])
    norms = norms.reshape(-1, LANES)
    up, down = w_up[0], w_down[0]

    hal = shift(x, "seq", 2)
    sib = swap(x, "seq", 1)

    place = exp_at.astype(jnp.int32).reshape(1)
    at = jnp.stack([exp_at, core, seq_at // 2]).astype(jnp.int32)
    lines = -(-hash_table.shape[0] // (8 * LANES)) * 8
    table = jnp.pad(hash_table, (0, lines * LANES - hash_table.shape[0])).reshape(lines, LANES)
    docs = 2 * ring * local_len // DOC_MOST
    slot, low, low_tall, meta, *grad_out = route(
        at, token_ids, table, cot, segment_ids, sources, capacity, docs
    )
    grad_in = [grad_out[0]] + [swap(grad_out[k], "exp", k) for k in range(1, sources)]

    *made, q = project(core_arg, x, after(sib, slot), norms, w_qkv, None)
    hal = after(hal, q)
    has = swap(hal, "seq", 1)
    a, k, v = project(core_arg, hal, has, norms, w_qkv, made)
    attn_own, attn_give, attn_all, attn_tall, logs = attend(meta, q, k, v, low_tall)
    attn_other = swap(attn_give, "seq", 1)
    resid, *rows_out = lift(
        core_arg, attn_own, after(attn_other, grad_in), w_out, x, norms, slot, sources, capacity
    )
    rows_in = [rows_out[0]] + [swap(rows_out[k], "exp", k) for k in range(1, sources)]
    talls, pres, backs, outs, turned = [], [], [], [], []
    for k_at in range(sources):
        tall, pre, back, out, turn = expert(rows_in[k_at], grad_in[k_at], up, down)
        talls.append(tall)
        pres.append(pre)
        outs.append(out)
        turned.append(turn)
        backs.append(back if k_at == 0 else swap(back, "exp", k_at))
        if k_at + 1 < sources:
            rows_in[k_at + 1] = after(rows_in[k_at + 1], back)
    bits = [1 << b for b in range(1, ring.bit_length() - 1)]
    orders = [bits, bits[::-1]]
    sides = [(seq_at // o[0]) % 2 for o in orders]
    subs = ring // 4
    masks = [
        sum((1 - (seq_at // bit) % 2) << (len(o) - 2 - at) for at, bit in enumerate(o[1:]))
        for o in orders
    ]
    chip = jnp.stack([core, *sides, *masks]).astype(jnp.int32)

    turned, backs[:-2] = lax.optimization_barrier((turned, backs[:-2]))
    blocks = expert_grad(chip, turned, grad_in, talls, pres, subs)
    given, kept = blocks[:2], blocks[2:]
    given, backs[-2] = lax.optimization_barrier((given, backs[-2]))
    given, backs[-1] = lax.optimization_barrier((given, backs[-1]))
    got = [swap(t, "seq", 1) for t in given]
    gr, gattn, gain_two_grad, bias_two_grad = lower(slot, resid, cot, norms, backs)
    got = after(got, gattn)
    goes = [add(kept[p][:width], got[p][:width]) for p in range(2)]
    stays = [[kept[p][width:], got[p][width:]] for p in range(2)]
    experts = Stream(expert_steps(list(zip(stays, goes)), orders))
    outs = after(outs, goes)
    returned = [outs[0]] + [swap(outs[k], "exp", k) for k in range(1, sources)]
    gattn_sib = swap(gattn, "seq", 1)
    unit = sources * 16
    sub = -(-(mine // LANES * width // subs) // unit) * unit
    gq, gk, gv = attend_back(
        meta, q, k, v, gattn, after(gattn_sib, goes), w_out, attn_tall, logs, low
    )
    pieces = dense_pieces(chip, a, gq, gk, gv, attn_all, gattn, gattn_sib, subs, sub)
    pieces, returned = lax.optimization_barrier((pieces, returned))
    dense = Stream(
        dense_steps([([pieces[0]], pieces[1]), ([pieces[2]], pieces[3])], orders)
    )
    (gq,) = meet([experts], (after(gq, pieces),))
    keep, give, halo, gain_one_grad, bias_one_grad = project_back(
        core_arg, x, sib, hal, has, gq, gk, gv, w_qkv
    )
    small = jnp.concatenate([gain_one_grad, bias_one_grad, gain_two_grad, bias_two_grad], axis=0)
    (give,) = meet([dense, experts], (give,))
    near = swap(give, "seq", 1)
    (near,) = meet([dense], (near,))
    for rest in range(len(bits) - 2):
        meet([dense, experts])
    far = add(halo, near[local_len:])
    hops = [("seq", bit) for bit in bits + [1]]
    hops += [("exp", 1 << b) for b in range(sources.bit_length() - 1)]
    small = Stream(small_steps(small, hops))
    layer_output = finish(slot, resid, returned)
    layer_output, far = meet([dense, experts, small], (layer_output, far))
    far = shift(far, "seq", -2)
    for rest in range(len(bits) - 2):
        meet([experts])
    own_parts = experts.result
    other_chip = across(own_parts, orders)
    other_core = beside(after(own_parts, layer_output))
    meet([dense, other_chip, other_core, small])
    other_both = beside(other_chip.result)
    hidden = down.shape[0]
    made = widen(core, sides, masks, own_parts, other_chip.result, (), hidden, subs)
    while dense.result is None:
        made = meet([dense, other_both, small], made)
    own_dense = dense.result
    dense_chip, dense_core = across(own_dense, orders), beside(own_dense)
    made = widen(
        1 - core, sides, masks, other_core.result, other_both.result, made, hidden, subs
    )
    grad_w_up, grad_w_down = meet([dense_chip, dense_core, small], made)
    dense_both = beside(dense_chip.result)
    meet([dense_both, small])
    while small.sent:
        small.go(small.sent)
    grad_w_qkv, grad_w_out = spread(
        chip, list(zip(own_dense, dense_chip.result)),
        list(zip(dense_core.result, dense_both.result)), width, mine, subs,
    )
    grad_input = close(x, gr, keep, near, after(far, grad_w_qkv), norms)
    small = small.result
    return (
        layer_output[None],
        grad_input[None],
        grad_w_qkv,
        grad_w_out,
        small[0],
        small[1],
        small[2],
        small[3],
        grad_w_up[None],
        grad_w_down[None],
    )


def solution(mesh):
    in_specs = (
        P("exp", "seq", None),
        P("exp", "seq"),
        P("exp", None),
        P(),
        P(),
        P(),
        P(),
        P(),
        P(),
        P(),
        P("exp", None, None),
        P("exp", None, None),
        P("exp", "seq", None),
    )
    out_specs = (
        P("exp", "seq", None),
        P("exp", "seq", None),
        P(),
        P(),
        P(),
        P(),
        P(),
        P(),
        P("exp", None, None),
        P("exp", None, None),
    )
    return jax.shard_map(
        on_device, mesh=mesh, in_specs=in_specs, out_specs=out_specs, check_vma=False
    )
```

```python
import functools
import math

import jax
import jax.numpy as jnp
from jax import lax
from jax.experimental import pallas as pl
from jax.experimental.pallas import tpu as pltpu
from jax.sharding import PartitionSpec as P

HEADS = 12
HEAD_DIM = 64
DOC_MOST = 1024
EPSILON = 1e-05
LOW = -1e30
LOWER = -2e30
LANES = 128
TILE = 256
F32 = jnp.float32
BF16 = jnp.bfloat16
MIB = 1 << 20
COST = 1


def dot(a, b):
    return lax.dot_general(a, b, (((1,), (0,)), ((), ())), preferred_element_type=F32)


def dot_nt(a, b):
    return lax.dot_general(a, b, (((1,), (1,)), ((), ())), preferred_element_type=F32)


def dot_tn(a, b):
    return lax.dot_general(a, b, (((0,), (0,)), ((), ())), preferred_element_type=F32)


def iota(shape, axis):
    return lax.broadcasted_iota(jnp.int32, shape, axis)


def one_hot(ids, width):
    return jnp.where(iota((ids.shape[0], width), 1) == ids, 1.0, 0.0).astype(BF16)


def norm_rows(values):
    center = values - jnp.mean(values, axis=-1, keepdims=True)
    scale = lax.rsqrt(jnp.mean(center * center, axis=-1, keepdims=True) + EPSILON)
    return center * scale, scale


def norm_back(grad, normed, scale):
    inner = jnp.mean(grad * normed, axis=-1, keepdims=True)
    return scale * (grad - jnp.mean(grad, axis=-1, keepdims=True) - normed * inner)


def after(value, *others):
    return lax.optimization_barrier((value, others))[0]


def shape(dims, dtype):
    return jax.ShapeDtypeStruct(dims, dtype)


def call(body, name, out_shape, args, *, grid=(), in_specs=None, out_specs=None, scratch=(),
         scalars=0, aliases=None, flops=0, nbytes=0, special=0, vmem=56):
    outs = out_shape if isinstance(out_shape, (tuple, list)) else [out_shape]
    whole = pl.BlockSpec(memory_space=pltpu.VMEM)
    if in_specs is None:
        in_specs = [whole] * (len(args) - scalars)
    if out_specs is None:
        out_specs = [whole] * len(outs)
        if not isinstance(out_shape, (tuple, list)):
            out_specs = out_specs[0]
    return pl.pallas_call(
        body,
        name=name,
        out_shape=out_shape,
        grid_spec=pltpu.PrefetchScalarGridSpec(
            num_scalar_prefetch=scalars,
            grid=grid,
            in_specs=in_specs,
            out_specs=out_specs,
            scratch_shapes=scratch,
        ),
        input_output_aliases=aliases or {},
        cost_estimate=pl.CostEstimate(flops=COST, bytes_accessed=COST, transcendentals=0),
        compiler_params=pltpu.CompilerParams(vmem_limit_bytes=vmem * MIB),
    )(*args)


def column(row):
    return jnp.broadcast_to(row.astype(F32), (8, row.shape[1])).T[:, :1].astype(jnp.int32)


def route_body(parts, capacity, docs, at_ref, ids_ref, table_ref, rows_ref, segment_ref, slot_ref,
               low_ref, tall_ref, meta_ref, *out_refs):
    ids = column(ids_ref[...])
    count = ids.shape[0]
    lines = table_ref.shape[0]
    picked = dot(one_hot(ids >> 7, lines), table_ref[...].astype(F32).astype(BF16))
    lane = iota((count, LANES), 1)
    choice = jnp.sum(
        jnp.where(lane == (ids & (LANES - 1)), picked, 0.0), axis=1, keepdims=True
    ).astype(jnp.int32)
    mine = lane == choice
    below = jnp.where(iota((count, count), 0) > iota((count, count), 1), 1.0, 0.0).astype(BF16)
    ranks = dot(below, jnp.where(mine, 1.0, 0.0).astype(BF16))
    rank = jnp.sum(jnp.where(mine, ranks, 0.0), axis=1, keepdims=True).astype(jnp.int32)
    slot = (choice ^ at_ref[0]) * capacity + rank
    slot_ref[...] = slot
    rows = rows_ref[...]
    for k in range(parts):
        chosen = one_hot(slot - k * capacity, capacity)
        out_refs[k][...] = dot_tn(chosen, rows).astype(BF16)

    pair_len = low_ref.shape[1]
    pair_at = pl.multiple_of(at_ref[2] * pair_len, pair_len)
    segments = segment_ref[...]
    here = segment_ref[:, pl.ds(pair_at, pair_len)]
    low = jnp.zeros((1, pair_len), F32)
    for d in range(docs):
        start = jnp.sum(jnp.where(segments < d, 1.0, 0.0), axis=1, keepdims=True)
        low = low + jnp.where(here == d, start, 0.0)
    low = low.astype(jnp.int32) - (pair_at - pair_len)
    low_ref[...] = low
    tall_ref[...] = column(low)
    place = iota((1, LANES), 1)
    meta = jnp.where(place == 0, at_ref[1], 0)
    for t in range(pair_len // TILE):
        meta = jnp.where(place == 1 + t, low[:, t * TILE : t * TILE + 1] >> 8, meta)
    meta_ref[...] = meta


def route(at, ids, table, rows, segments, parts, capacity, docs):
    count, width = rows.shape
    pair_len = 2 * count
    outs = [shape((count, 1), jnp.int32), shape((1, pair_len), jnp.int32),
            shape((pair_len, 1), jnp.int32), shape((1, LANES), jnp.int32)]
    outs += [shape((capacity, width), BF16)] * parts
    return call(
        functools.partial(route_body, parts, capacity, docs), "route", outs,
        (at, ids, table, rows, segments), scalars=1,
    )


def vector(ref, at):
    lines = ref.shape[0] // 4
    return jnp.concatenate([ref[at * lines + j : at * lines + j + 1, :] for j in range(lines)], axis=1)


def project_body(skip, core_ref, own_ref, sib_ref, norm_ref, wq_ref, wk_ref, wv_ref, *refs):
    outs = refs[skip:-1]
    held_ref = refs[-1]
    step = pl.program_id(0)
    half = (pl.num_programs(0) - 1) // 2
    before = held_ref[(step + 1) % 2]
    outs[1][...] = dot(before, wk_ref[...]).astype(BF16)
    outs[2][...] = dot(before, wv_ref[...]).astype(BF16)
    if not skip:
        outs[3][...] = dot(before, wq_ref[...]).astype(BF16)
    rows = jnp.where(step < half, own_ref[...], sib_ref[...])
    normed, unused = norm_rows(rows.astype(F32))
    a = (normed * vector(norm_ref, 0) + vector(norm_ref, 1)).astype(BF16)
    held_ref[step % 2] = a
    outs[0][...] = a


def project(core, own, sib, norms, w_qkv, made):
    count, width = own.shape
    mine = width // 2
    half = count // TILE
    base = 0 if made else 2 * half

    def place(i, c):
        return ((i // half) ^ c[0]) * half + i % half

    def now(i, c):
        return (base + place(jnp.minimum(i, 2 * half - 1), c), 0)

    def then(i, c):
        return (base + place(jnp.maximum(i - 1, 0), c), 0)

    in_specs = [
        pl.BlockSpec((TILE, width), lambda i, c: (jnp.minimum(i, half - 1), 0)),
        pl.BlockSpec((TILE, width), lambda i, c: (jnp.clip(i - half, 0, half - 1), 0)),
        pl.BlockSpec(norms.shape, lambda i, c: (0, 0)),
    ] + [
        pl.BlockSpec((width, mine), functools.partial(lambda t, i, c: (0, 2 * t + c[0]), t))
        for t in range(3)
    ]
    args = [core, own, sib, norms, w_qkv, w_qkv, w_qkv]
    outs = [shape((4 * count, width), BF16)] + [shape((4 * count, mine), BF16)] * 2
    out_specs = [
        pl.BlockSpec((TILE, width), now),
        pl.BlockSpec((TILE, mine), then),
        pl.BlockSpec((TILE, mine), then),
    ]
    aliases = {}
    if made:
        in_specs += [pl.BlockSpec(memory_space=pl.ANY)] * 3
        aliases = {7: 0, 8: 1, 9: 2}
        args += list(made)
    else:
        outs.append(shape((2 * count, mine), BF16))
        out_specs.append(
            pl.BlockSpec((TILE, mine), lambda i, c: (place(jnp.maximum(i - 1, 0), c), 0))
        )
    return call(
        functools.partial(project_body, 3 if made else 0), "project", outs, args,
        grid=(2 * half + 1,), in_specs=in_specs, out_specs=out_specs, scalars=1, aliases=aliases,
        scratch=[pltpu.VMEM((2, TILE, width), BF16)],
    )


def masked_heads(block):
    lane = iota(block.shape, 1)
    zero = jnp.zeros((), block.dtype)
    return [
        jnp.where(lane < HEAD_DIM, block, zero),
        jnp.where(lane < HEAD_DIM, zero, block),
    ]


def flip(block):
    return block.astype(F32).T.astype(block.dtype)


def lanes_of(group):
    return slice(group * LANES, (group + 1) * LANES)


def put_heads(heads_ref, q_ref):
    def some(t, unused):
        here = pl.ds(pl.multiple_of(t * TILE, TILE), TILE)
        block = q_ref[here, :] * jnp.asarray(HEAD_DIM**-0.5, BF16)
        for g in range(q_ref.shape[1] // LANES):
            for h, part in enumerate(masked_heads(block[:, lanes_of(g)])):
                heads_ref[2 * g + h, here, :] = part
        return unused

    lax.fori_loop(0, q_ref.shape[0] // TILE, some, 0)


def tile_mask(begin, low, high):
    place = begin + iota((TILE, TILE), 0)
    return (place >= low) & (place <= high)


def attend_body(meta_ref, q_ref, k_ref, v_ref, lo_ref, own_ref, sib_ref, all_ref, tall_ref,
                log_ref, heads_ref, acc_ref, rows_ref):
    total, mine = q_ref.shape
    half = total // 2
    heads = range(mine // HEAD_DIM)
    put_heads(heads_ref, q_ref)
    core = meta_ref[0, 0]

    def tile(t, unused):
        at = pl.multiple_of(t * TILE, TILE)
        here = pl.ds(at, TILE)
        low = lo_ref[here, :]
        high = total + at + iota((TILE, 1), 0)
        acc_ref[...] = jnp.zeros_like(acc_ref)

        def step(j, state):
            begin = pl.multiple_of(j * TILE, TILE)
            there = pl.ds(begin, TILE)
            place = begin + iota((TILE, TILE), 1)
            allowed = (place >= low) & (place <= high)
            scores = [
                jnp.where(
                    allowed, dot_nt(heads_ref[h, here, :], k_ref[there, lanes_of(h // 2)]), LOWER
                )
                for h in heads
            ]
            tops = [
                jnp.maximum(state[2 * h], jnp.max(scores[h], axis=1, keepdims=True)) for h in heads
            ]
            shares = [jnp.exp(scores[h] - tops[h]) for h in heads]
            factors = [jnp.exp(state[2 * h] - tops[h]) for h in heads]
            sums = [
                state[2 * h + 1] * factors[h] + jnp.sum(shares[h], axis=1, keepdims=True)
                for h in heads
            ]
            more = [dot(shares[h].astype(BF16), v_ref[there, lanes_of(h // 2)]) for h in heads]
            for h in heads:
                acc_ref[h] = acc_ref[h] * factors[h] + more[h]
            return tuple(x for h in heads for x in (tops[h], sums[h]))

        first = (jnp.full((TILE, 1), LOW, F32), jnp.zeros((TILE, 1), F32))
        state = lax.fori_loop(
            meta_ref[0, 1 + t], total // TILE + t + 1, step, first * len(heads)
        )
        lane = iota((TILE, LANES), 1)
        logs = jnp.zeros((TILE, LANES), F32)
        for h in heads:
            logs = jnp.where(lane == h, state[2 * h] + jnp.log(state[2 * h + 1]), logs)
        log_ref[:, here] = logs.T[: log_ref.shape[0], :]
        for g in range(mine // LANES):
            left = acc_ref[2 * g] / state[4 * g + 1]
            right = acc_ref[2 * g + 1] / state[4 * g + 3]
            out = jnp.where(lane < HEAD_DIM, left, right)
            rows_ref[here, lanes_of(g)] = out
            tall_ref[lanes_of(g), here] = out.T
        return unused

    lax.fori_loop(0, total // TILE, tile, 0)

    def some(t, unused):
        at = pl.multiple_of(t * TILE, TILE)
        here = pl.ds(at, TILE)
        own_at = pl.ds(pl.multiple_of(core * half + at, TILE), TILE)
        sib_at = pl.ds(pl.multiple_of((1 - core) * half + at, TILE), TILE)
        all_ref[own_at, :] = rows_ref[own_at, :].astype(BF16)
        all_ref[sib_at, :] = rows_ref[sib_at, :].astype(BF16)
        own_ref[here, :] = rows_ref[own_at, :].astype(BF16)
        sib_ref[here, :] = rows_ref[sib_at, :].astype(BF16)
        return unused

    lax.fori_loop(0, half // TILE, some, 0)


def attend(meta, q, k, v, low):
    total, mine = q.shape
    heads = mine // HEAD_DIM
    outs = [
        shape((total // 2, mine), BF16),
        shape((total // 2, mine), BF16),
        shape((total, mine), BF16),
        shape((mine, total), F32),
        shape((-(-heads // 8) * 8, total), F32),
    ]
    return call(
        attend_body, "attend", outs, (meta, q, k, v, low), scalars=1,
        scratch=[pltpu.VMEM((heads, total, LANES), BF16), pltpu.VMEM((heads, TILE, LANES), F32),
                 pltpu.VMEM((total, mine), F32)],
    )


def fetch(pairs, sems):
    copies = [pltpu.make_async_copy(a, b, sems.at[i]) for i, (a, b) in enumerate(pairs)]
    for copy in copies:
        copy.start()
    return [copy.wait for copy in copies]


def both_rows(core, own, sib, rows_ref):
    half = own.shape[0]
    return [
        (own, rows_ref.at[pl.ds(pl.multiple_of(core * half, half), half), :]),
        (sib, rows_ref.at[pl.ds(pl.multiple_of((1 - core) * half, half), half), :]),
    ]


def attend_back_body(meta_ref, q_hbm, k_hbm, v_hbm, own_hbm, sib_hbm, wo_hbm, tall_hbm, log_ref,
                     lo_ref, gq_ref, gk_ref, gv_ref, rows_ref, heads_ref, grads_ref, delta_ref,
                     kt_ref, gqt_ref, gks_ref, gvs_ref, q_ref, k_ref, v_ref, wo_ref, tall_ref,
                     sems):
    total, mine = q_ref.shape
    heads = mine // HEAD_DIM
    core = meta_ref[0, 0]
    mine_at = pl.ds(pl.multiple_of(core * mine, mine), mine)
    waits = fetch(
        both_rows(core, own_hbm, sib_hbm, rows_ref)
        + [(wo_hbm.at[mine_at, :], wo_ref), (tall_hbm, tall_ref), (q_hbm, q_ref), (k_hbm, k_ref),
           (v_hbm, v_ref)],
        sems,
    )

    def clear(t, unused):
        here = pl.ds(pl.multiple_of(t * TILE, TILE), TILE)
        gks_ref[here, :] = jnp.zeros((TILE, mine), F32)
        gvs_ref[here, :] = jnp.zeros((TILE, mine), F32)
        return unused

    lax.fori_loop(0, 2 * total // TILE, clear, 0)
    gqt_ref[...] = jnp.zeros_like(gqt_ref)
    for wait in waits[:4]:
        wait()
    weights = wo_ref[...]

    def begin(t, unused):
        here = pl.ds(pl.multiple_of(t * TILE, TILE), TILE)
        grads = dot_nt(rows_ref[here, :], weights).astype(BF16)
        turned = grads.astype(F32).T * tall_ref[:, here]
        for h in range(heads):
            span = slice(h * HEAD_DIM, (h + 1) * HEAD_DIM)
            delta_ref[h : h + 1, here] = jnp.sum(turned[span, :], axis=0, keepdims=True)
        for g in range(mine // LANES):
            for h, part in enumerate(masked_heads(grads[:, lanes_of(g)])):
                grads_ref[2 * g + h, here, :] = part
        return unused

    lax.fori_loop(0, total // TILE, begin, 0, unroll=2)
    waits[4]()
    put_heads(heads_ref, q_ref)
    waits[5]()

    def turn(t, unused):
        here = pl.ds(pl.multiple_of(t * TILE, TILE), TILE)
        kt_ref[:, here] = flip(k_ref[here, :])
        return unused

    lax.fori_loop(0, 2 * total // TILE, turn, 0, unroll=2)
    waits[6]()

    def tile(t, unused):
        at = pl.multiple_of(t * TILE, TILE)
        here = pl.ds(at, TILE)
        low = lo_ref[:, here]
        high = total + at + iota((1, TILE), 1)

        logs = [log_ref[h : h + 1, here] for h in range(heads)]
        deltas = [delta_ref[h : h + 1, here] for h in range(heads)]

        def step(j, carry):
            begin = pl.multiple_of(j * TILE, TILE)
            there = pl.ds(begin, TILE)
            allowed = tile_mask(begin, low, high)
            every = range(heads)
            queries = [heads_ref[h, here, :] for h in every]
            grads = [grads_ref[h, here, :] for h in every]
            scores = [dot_nt(k_ref[there, lanes_of(h // 2)], queries[h]) for h in every]
            grad_soft = [dot_nt(v_ref[there, lanes_of(h // 2)], grads[h]) for h in every]
            soft = [jnp.exp(jnp.where(allowed, scores[h], LOWER) - logs[h]) for h in every]
            grad_scores = [(soft[h] * (grad_soft[h] - deltas[h])).astype(BF16) for h in every]
            soft = [s.astype(BF16) for s in soft]
            gv = [dot(soft[h], grads[h]) for h in every]
            gk = [dot(grad_scores[h], queries[h]) for h in every]
            gq = [
                dot(kt_ref[h * HEAD_DIM : (h + 1) * HEAD_DIM, there], grad_scores[h])
                for h in every
            ]
            for g in range(heads // 2):
                gvs_ref[there, lanes_of(g)] += gv[2 * g] + gv[2 * g + 1]
                gks_ref[there, lanes_of(g)] += gk[2 * g] + gk[2 * g + 1]
            for h in every:
                gqt_ref[h * HEAD_DIM : (h + 1) * HEAD_DIM, here] += gq[h]
            return carry

        return lax.fori_loop(meta_ref[0, 1 + t], total // TILE + t + 1, step, unused)

    lax.fori_loop(0, total // TILE, tile, 0)

    def finish_queries(t, unused):
        here = pl.ds(pl.multiple_of(t * TILE, TILE), TILE)
        gq_ref[here, :] = (gqt_ref[:, here].T * (HEAD_DIM**-0.5)).astype(BF16)
        return unused

    def finish_keys(t, unused):
        here = pl.ds(pl.multiple_of(t * TILE, TILE), TILE)
        gk_ref[here, :] = gks_ref[here, :].astype(BF16)
        gv_ref[here, :] = gvs_ref[here, :].astype(BF16)
        return unused

    lax.fori_loop(0, total // TILE, finish_queries, 0)
    lax.fori_loop(0, 2 * total // TILE, finish_keys, 0)


def attend_back(meta, q, k, v, own, sib, w_out, tall, logs, low):
    total, mine = q.shape
    width = own.shape[1]
    heads = mine // HEAD_DIM
    outs = [
        shape((total, mine), BF16),
        shape((2 * total, mine), BF16),
        shape((2 * total, mine), BF16),
    ]
    return call(
        attend_back_body, "attend_back", outs,
        (meta, q, k, v, own, sib, w_out, tall, logs, low), scalars=1,
        in_specs=[pl.BlockSpec(memory_space=pl.ANY)] * 7 + [pl.BlockSpec(memory_space=pltpu.VMEM)] * 2,
        scratch=[pltpu.VMEM((total, width), BF16), pltpu.VMEM((heads, total, LANES), BF16),
                 pltpu.VMEM((heads, total, LANES), BF16), pltpu.VMEM(logs.shape, F32),
                 pltpu.VMEM((mine, 2 * total), BF16), pltpu.VMEM((mine, total), F32),
                 pltpu.VMEM((2 * total, mine), F32), pltpu.VMEM((2 * total, mine), F32),
                 pltpu.VMEM(q.shape, BF16), pltpu.VMEM(k.shape, BF16), pltpu.VMEM(v.shape, BF16),
                 pltpu.VMEM((mine, width), BF16), pltpu.VMEM(tall.shape, F32),
                 pltpu.SemaphoreType.DMA((7,))],
    )


def dense_body(subs, sub, chip_ref, a_hbm, gq_hbm, gk_hbm, gv_hbm, all_hbm, own_hbm, sib_hbm,
               *refs):
    piece_refs = refs[:4]
    dense_ref, rows_ref, short_ref, long_ref, sems = refs[4:]
    unused, total, mine = short_ref.shape
    half = total // 2
    width = rows_ref.shape[1]
    lines = width // subs
    quarter = subs * sub
    core = chip_ref[0]
    own_at = pl.multiple_of(2 * total + core * half, half)
    sib_at = pl.multiple_of(2 * total + (1 - core) * half, half)
    waits = fetch(
        [(own_hbm, rows_ref.at[pl.ds(own_at, half), :]),
         (sib_hbm, rows_ref.at[pl.ds(sib_at, half), :]),
         (a_hbm, rows_ref.at[pl.ds(0, 2 * total), :]),
         (gq_hbm, short_ref.at[0]), (all_hbm, short_ref.at[1]),
         (gk_hbm, long_ref.at[0]), (gv_hbm, long_ref.at[1])],
        sems,
    )

    def put(kind, turned):
        for j in range(mine // LANES):
            block = turned[lanes_of(j), :].T.astype(BF16)
            for at in range(subs):
                first = pl.multiple_of(kind * quarter + at * sub + j * lines, 16)
                dense_ref[pl.ds(first, lines), :] = block[at * lines : (at + 1) * lines, :]

    def short(i, unused):
        rows = rows_ref[pl.ds(pl.multiple_of((1 + i) * total, total), total), :]
        put(3 * i, dot_tn(short_ref[i], rows))
        return unused

    def long(i, unused):
        put(1 + i, dot_tn(long_ref[i], rows_ref[: 2 * total, :]))
        return unused

    for wait in waits[:5]:
        wait()
    lax.fori_loop(0, 2, short, 0)
    waits[5]()
    waits[6]()
    lax.fori_loop(0, 2, long, 0)
    spare = sub - mine // LANES * lines
    if spare:
        for at in range(4 * subs):
            dense_ref[(at + 1) * sub - spare : (at + 1) * sub, :] = jnp.zeros((spare, LANES), BF16)
    for p in range(2):
        side = chip_ref[1 + p]
        for r, which in enumerate((side, 1 - side)):
            for at in range(subs):
                from_at = pl.multiple_of((2 * p + which) * quarter + at * sub, 16)
                to_at = pl.multiple_of((at ^ chip_ref[3 + p]) * sub, 16)
                piece_refs[2 * p + r][pl.ds(to_at, sub), :] = dense_ref[pl.ds(from_at, sub), :]


def dense_pieces(chip, a, gq, gk, gv, attn_all, own, sib, subs, sub):
    return call(
        functools.partial(dense_body, subs, sub), "dense",
        [shape((subs * sub, LANES), BF16)] * 4,
        (chip, a, gq, gk, gv, attn_all, own, sib), scalars=1,
        in_specs=[pl.BlockSpec(memory_space=pl.ANY)] * 7,
        scratch=[pltpu.VMEM((4 * subs * sub, LANES), BF16),
                 pltpu.VMEM((3 * gq.shape[0], a.shape[1]), BF16),
                 pltpu.VMEM((2, *gq.shape), BF16), pltpu.VMEM((2, *gk.shape), BF16),
                 pltpu.SemaphoreType.DMA((7,))],
    )


def lift_body(parts, capacity, core_ref, own_ref, other_ref, w_ref, x_ref, norm_ref, slot_ref,
              resid_ref, *out_refs):
    mine = own_ref.shape[1]
    core = core_ref[0]
    own_at = pl.ds(pl.multiple_of(core * mine, mine), mine)
    other_at = pl.ds(pl.multiple_of((1 - core) * mine, mine), mine)
    *out_refs, rows_ref = out_refs

    def some(t, unused):
        here = pl.ds(pl.multiple_of(t * TILE, TILE), TILE)
        more = dot(own_ref[here, :], w_ref[own_at, :]) + dot(other_ref[here, :], w_ref[other_at, :])
        resid = x_ref[here, :].astype(F32) + more
        resid_ref[here, :] = resid
        normed, scale = norm_rows(resid)
        rows_ref[here, :] = (normed * vector(norm_ref, 2) + vector(norm_ref, 3)).astype(BF16)
        return unused

    lax.fori_loop(0, own_ref.shape[0] // TILE, some, 0)
    slot = slot_ref[...]
    for k in range(parts):
        chosen = one_hot(slot - k * capacity, capacity)
        out_refs[k][...] = dot_tn(chosen, rows_ref[...]).astype(BF16)


def lift(core, own, other, w_out, x, norms, slot, parts, capacity):
    count, width = x.shape
    outs = [shape((count, width), F32)] + [shape((capacity, width), BF16)] * parts
    return call(
        functools.partial(lift_body, parts, capacity), "lift", outs,
        (core, own, other, w_out, x, norms, slot), scratch=[pltpu.VMEM((count, width), BF16)],
        scalars=1, flops=2 * count * width * (width + parts * capacity),
    )


GATE_A = math.sqrt(2.0 / math.pi)
GATE_B = 0.044715


def expert_body(sub, rows_ref, grad_ref, up_ref, down_ref, tall_ref, pre_ref, back_ref, out_ref,
                turned_ref, back_acc, out_acc):
    step = pl.program_id(0)

    @pl.when(step == 0)
    def _():
        back_acc[...] = jnp.zeros_like(back_acc)
        out_acc[...] = jnp.zeros_like(out_acc)
        turned_ref[...] = flip(rows_ref[...])

    parts = [slice(s * sub, (s + 1) * sub) for s in range(down_ref.shape[0] // sub)]
    pres = [dot(rows_ref[...], up_ref[:, part]) for part in parts]
    grads = [dot_nt(grad_ref[...], down_ref[part, :]) for part in parts]
    hids, slopes = [], []
    for pre in pres:
        square = pre * pre
        bend = jnp.tanh(GATE_A * (pre + GATE_B * (square * pre)))
        half = 0.5 + 0.5 * bend
        hids.append(pre * half)
        slopes.append(
            half + (pre * (1.0 - bend * bend)) * (0.5 * GATE_A + (1.5 * GATE_A * GATE_B) * square)
        )
    low = jnp.concatenate([(g * s).astype(BF16) for g, s in zip(grads, slopes)], axis=1)
    back_acc[...] += dot_nt(low, up_ref[...])
    out_acc[...] += dot(jnp.concatenate([h.astype(BF16) for h in hids], axis=1), down_ref[...])
    pre_ref[...] = low
    for part, hid in zip(parts, hids):
        tall_ref[part, :] = hid.T.astype(BF16)

    @pl.when(step == pl.num_programs(0) - 1)
    def _():
        back_ref[...] = back_acc[...].astype(BF16)
        out_ref[...] = out_acc[...].astype(BF16)


def expert(rows, grads, w_up, w_down, sub=256):
    count, width = rows.shape
    hidden = w_up.shape[1]
    block = width
    const = pl.BlockSpec((count, width), lambda j: (0, 0))
    return call(
        functools.partial(expert_body, sub), "expert",
        [shape((hidden, count), BF16), shape((count, hidden), BF16), shape((count, width), BF16),
         shape((count, width), BF16), shape((width, count), BF16)],
        (rows, grads, w_up, w_down), grid=(hidden // block,),
        in_specs=[const, const, pl.BlockSpec((width, block), lambda j: (0, j)),
                  pl.BlockSpec((block, width), lambda j: (j, 0))],
        out_specs=[pl.BlockSpec((block, count), lambda j: (j, 0)),
                   pl.BlockSpec((count, block), lambda j: (0, j)), const, const,
                   pl.BlockSpec((width, count), lambda j: (0, 0))],
        scratch=[pltpu.VMEM((count, width), F32)] * 2,
    )


def expert_grad_body(parts, subs, chip_ref, *refs):
    turned, grads, talls, pres = (refs[parts * t : parts * (t + 1)] for t in range(4))
    *outs, held_ref, sems = refs[4 * parts :]
    width = held_ref.shape[2]
    lines = width // subs
    step = pl.program_id(0)
    steps = len(outs)
    slot = step % 2

    def copy(t, at):
        return pltpu.make_async_copy(held_ref.at[at], outs[t], sems.at[at])

    @pl.when(step >= 2)
    def _():
        copy(0, slot).wait()

    def product(left, right):
        out = None
        for a, b in zip(left, right):
            more = dot(a[...], b[...])
            out = more if out is None else out + more
        return out.astype(BF16)

    half = steps // 2
    side, mask = chip_ref[1 + step % half], chip_ref[3 + step % half]
    pairs = ((product(turned, pres), side == 0), (product(talls, grads), side == 1))
    for value, stays in pairs:
        base = jnp.where(stays, width, 0)
        for at in range(subs):
            first = pl.multiple_of(base + (at ^ mask) * lines, 16)
            held_ref[slot, pl.ds(first, lines), :] = value[at * lines : (at + 1) * lines, :]

    for t in range(steps):

        @pl.when(step == t)
        def _(t=t):
            copy(t, t % 2).start()

    @pl.when(step == steps - 1)
    def _():
        copy(0, 0).wait()
        copy(0, 1).wait()


def expert_grad(chip, turned, grads, talls, pres, subs):
    parts = len(grads)
    count, width = grads[0].shape
    blocks = talls[0].shape[0] // width
    half = blocks // 2

    def column(i, m):
        return jnp.where(i < half, (1 - m[0]) * half, m[0] * half - half) + i

    const = lambda dims: pl.BlockSpec(dims, lambda i, m: (0, 0))
    return call(
        functools.partial(expert_grad_body, parts, subs), "expert_grad",
        [shape((2 * width, width), BF16)] * blocks,
        (chip, *turned, *grads, *talls, *pres), grid=(blocks,), scalars=1,
        in_specs=[const((width, count))] * parts + [const((count, width))] * parts
        + [pl.BlockSpec((width, count), lambda i, m: (column(i, m), 0))] * parts
        + [pl.BlockSpec((count, width), lambda i, m: (0, column(i, m)))] * parts,
        out_specs=[pl.BlockSpec(memory_space=pl.ANY)] * blocks,
        scratch=[pltpu.VMEM((2, 2 * width, width), BF16), pltpu.SemaphoreType.DMA((2,))],
    )


def widen_body(skip, meta_ref, *refs):
    pairs, (up_out, down_out) = refs[:4], refs[4 + skip :]
    second = pl.program_id(0) >= pl.num_programs(0) // 2
    first = meta_ref[1 + pl.program_id(0) // (pl.num_programs(0) // 2)] == 0
    mine = jnp.where(second, pairs[2][...], pairs[0][...])
    theirs = jnp.where(second, pairs[3][...], pairs[1][...])
    up_out[...] = jnp.where(first, mine, theirs).astype(F32)
    down_out[...] = jnp.where(first, theirs, mine).astype(F32)


def widen(core, sides, masks, mine, theirs, made, hidden, subs):
    width = mine[0].shape[1]
    rows = width // subs
    meta = jnp.stack([core, *sides, *masks]).astype(jnp.int32)

    def index(p):
        def at(i, m):
            here = jnp.clip(i - p * subs, 0, subs - 1)
            return (here ^ m[3 + p], 0)

        return at

    blocks = [pl.BlockSpec((rows, width), index(p)) for p in (0, 0, 1, 1)]
    column = lambda i, m: 2 * m[0] + i // subs
    return call(
        functools.partial(widen_body, len(made)), "widen",
        [shape((width, hidden), F32), shape((hidden, width), F32)],
        (meta, mine[0], theirs[0], mine[1], theirs[1], *made), grid=(2 * subs,), scalars=1,
        in_specs=blocks + [pl.BlockSpec(memory_space=pl.ANY)] * len(made),
        out_specs=[pl.BlockSpec((rows, width), lambda i, m: (i % subs, column(i, m))),
                   pl.BlockSpec((rows, width), lambda i, m: (column(i, m) * subs + i % subs, 0))],
        aliases={5: 0, 6: 1} if made else None,
    )


def collect(slot, part_refs):
    total = None
    for k, ref in enumerate(part_refs):
        capacity = ref.shape[0]
        more = dot(one_hot(slot - k * capacity, capacity), ref[...])
        total = more if total is None else total + more
    return total


def lower_body(parts, slot_ref, resid_ref, cot_ref, norm_ref, *refs):
    grads = collect(slot_ref[...], refs[:parts])
    gr_ref, low_ref, gain_out, bias_out = refs[parts:]
    normed, scale = norm_rows(resid_ref[...])

    @pl.when(pl.program_id(0) == 0)
    def _():
        gain_out[...] = jnp.zeros_like(gain_out)
        bias_out[...] = jnp.zeros_like(bias_out)

    gain_out[...] += jnp.sum(grads * normed, axis=0, keepdims=True)
    bias_out[...] += jnp.sum(grads, axis=0, keepdims=True)
    gr = cot_ref[...].astype(F32) + norm_back(grads * vector(norm_ref, 2), normed, scale)
    gr_ref[...] = gr
    low_ref[...] = gr.astype(BF16)


def row_specs(dims, *whole):
    return [pl.BlockSpec((TILE, d), lambda i: (i, 0)) for d in dims] + [
        pl.BlockSpec(w.shape, lambda i: (0, 0)) for w in whole
    ]


def lower(slot, resid, cot, norms, back):
    parts = len(back)
    count, width = resid.shape
    outs = [shape((count, width), F32), shape((count, width), BF16),
            shape((1, width), F32), shape((1, width), F32)]
    return call(
        functools.partial(lower_body, parts), "lower", outs, (slot, resid, cot, norms, *back),
        grid=(count // TILE,), in_specs=row_specs((1, width, width), norms, *back),
        out_specs=row_specs((width, width), outs[2], outs[3]),
    )


def finish_body(slot_ref, resid_ref, *refs):
    refs[-1][...] = (resid_ref[...] + collect(slot_ref[...], refs[:-1])).astype(BF16)


def finish(slot, resid, parts):
    count, width = resid.shape
    return call(
        finish_body, "finish", shape(resid.shape, BF16), (slot, resid, *parts),
        grid=(count // TILE,), in_specs=row_specs((1, width), *parts),
        out_specs=row_specs((width,))[0],
    )


def project_back_body(half, core_ref, own_ref, sib_ref, hal_ref, has_ref, gq_ref, gk_ref, gv_ref,
                      wq_ref, wk_ref, wv_ref, keep_ref, send_ref, halo_ref, gain_ref, bias_ref):
    step = pl.program_id(0)
    rows = jnp.where(
        step < 2 * half,
        jnp.where(step < half, own_ref[...], sib_ref[...]),
        jnp.where(step < 3 * half, hal_ref[...], has_ref[...]),
    )
    normed, unused = norm_rows(rows.astype(F32))
    here = step < 2 * half
    ga = dot_nt(gk_ref[...], wk_ref[...]) + dot_nt(gv_ref[...], wv_ref[...])
    gq = jnp.where(here, gq_ref[...], jnp.zeros_like(gq_ref))
    ga = ga + dot_nt(gq, wq_ref[...])

    @pl.when(step == 0)
    def _():
        gain_ref[...] = jnp.zeros_like(gain_ref)
        bias_ref[...] = jnp.zeros_like(bias_ref)

    gain_ref[...] += jnp.sum(ga * normed, axis=0, keepdims=True)
    bias_ref[...] += jnp.sum(ga, axis=0, keepdims=True)

    @pl.when(step < half)
    def _():
        keep_ref[...] = ga

    @pl.when((step // half) % 2 == 1)
    def _():
        send_ref[...] = ga.astype(BF16)

    @pl.when(step // half == 2)
    def _():
        halo_ref[...] = ga


def project_back(core, own, sib, hal, has, gq, gk, gv, w_qkv):
    count, width = own.shape
    mine = gq.shape[1]
    half = count // TILE

    def at(t):
        return lambda i, c: (jnp.clip(i - t * half, 0, half - 1), 0)

    def place(i, c):
        return jnp.where(i < 2 * half, 2 * half, 0) + (((i // half) % 2) ^ c[0]) * half + i % half

    def sent(i, c):
        late = half + jnp.clip(i - 3 * half, 0, half - 1)
        return (jnp.where(i < 2 * half, jnp.clip(i - half, 0, half - 1), late), 0)

    row = pl.BlockSpec((1, width), lambda i, c: (0, 0))
    in_specs = [pl.BlockSpec((TILE, width), at(t)) for t in range(4)] + [
        pl.BlockSpec((TILE, mine), lambda i, c: (jnp.maximum(place(i, c) - 2 * half, 0), 0)),
        pl.BlockSpec((TILE, mine), lambda i, c: (place(i, c), 0)),
        pl.BlockSpec((TILE, mine), lambda i, c: (place(i, c), 0)),
    ] + [
        pl.BlockSpec((width, mine), functools.partial(lambda t, i, c: (0, 2 * t + c[0]), t))
        for t in range(3)
    ]
    return call(
        functools.partial(project_back_body, half), "project_back",
        [shape((count, width), F32), shape((2 * count, width), BF16), shape((count, width), F32),
         shape((1, width), F32), shape((1, width), F32)],
        (core, own, sib, hal, has, gq, gk, gv, w_qkv, w_qkv, w_qkv),
        grid=(4 * half,), in_specs=in_specs, scalars=1,
        out_specs=[pl.BlockSpec((TILE, width), at(0)), pl.BlockSpec((TILE, width), sent),
                   pl.BlockSpec((TILE, width), at(2)), row, row],
        flops=20 * count * width * mine,
    )


def close_body(x_ref, gr_ref, keep_ref, near_ref, far_ref, norm_ref, out_ref):
    ga = keep_ref[...] + near_ref[...].astype(F32) + far_ref[...].astype(F32)
    normed, scale = norm_rows(x_ref[...].astype(F32))
    out_ref[...] = gr_ref[...] + norm_back(ga * vector(norm_ref, 0), normed, scale)


def close(x, gr, keep, near, far, norms):
    count, width = x.shape
    block = pl.BlockSpec((TILE, width), lambda i: (i, 0))
    return call(
        close_body, "close", shape((count, width), F32), (x, gr, keep, near, far, norms),
        grid=(count // TILE,),
        in_specs=[block] * 5 + [pl.BlockSpec(norms.shape, lambda i: (0, 0))], out_specs=block,
    )


def swap(block, axis, distance):
    return lax.ppermute(block, axis, [(i, i ^ distance) for i in range(lax.axis_size(axis))])


def trade(block, axis):
    return lax.all_to_all(block, axis, split_axis=0, concat_axis=0, tiled=True)


def shift(block, axis, distance):
    size = lax.axis_size(axis)
    route = [(i, i + distance) for i in range(size) if 0 <= i + distance < size]
    return lax.ppermute(block, axis, route)


def total(terms):
    return sum(t.astype(F32) for t in terms).astype(BF16)


def add(a, b):
    return total([a, b])


def at_index(block, index):
    return lax.dynamic_index_in_dim(block, index, 0, keepdims=False)


def scatter_steps(pieces, orders):
    pairs = list(pieces)
    for s in range(len(orders[0])):
        arrived = yield [(goes, "seq", bits[s]) for (stays, goes), bits in zip(pairs, orders)]
        terms = [stays + [got] for (stays, goes), got in zip(pairs, arrived)]
        if s + 1 < len(orders[0]):
            half = terms[0][0].shape[0] // 2
            pairs = [
                ([total([t[half:] for t in terms_p])], total([t[:half] for t in terms_p]))
                for terms_p in terms
            ]
    return [total(terms_p) for terms_p in terms]


def gather_steps(parts, orders):
    parts = list(parts)
    for s in reversed(range(1, len(orders[0]))):
        arrived = yield [(part, "seq", bits[s]) for part, bits in zip(parts, orders)]
        parts = [jnp.concatenate([got, part], axis=0) for got, part in zip(arrived, parts)]
    return parts


def dense_steps(pieces, orders):
    sources = lax.axis_size("exp")
    parts = yield from scatter_steps(pieces, orders)
    joined = jnp.stack([p.reshape(sources, -1, LANES) for p in parts], axis=1)
    (got,) = yield [(joined, "exp", 0)]
    own = jnp.sum(got.astype(F32), axis=0).astype(BF16)
    (got,) = yield [(jnp.broadcast_to(own, (sources, *own.shape)), "exp", 0)]
    parts = [got[:, p].reshape(-1, LANES) for p in range(len(orders))]
    return (yield from gather_steps(parts, orders))


def expert_steps(pieces, orders):
    parts = yield from scatter_steps(pieces, orders)
    return (yield from gather_steps(parts, orders))


def one_step(sends):
    return (yield sends)


def across(parts, orders):
    return Stream(one_step([(part, "seq", bits[0]) for part, bits in zip(parts, orders)]))


def beside(parts):
    return Stream(one_step([(part, "seq", 1) for part in parts]))


def small_steps(value, hops):
    for hop in hops:
        (got,) = yield [(value, *hop)]
        value = value + got
    return value


class Stream:
    def __init__(self, steps):
        self.steps = steps
        self.result = None
        self.sent = []
        self.go(None)

    def go(self, arrived):
        try:
            sends = self.steps.send(arrived)
        except StopIteration as stop:
            self.sent, self.raw, self.result = [], [], stop.value
        else:
            self.raw = [send[0] for send in sends]
            self.sent = [swap(*send) if send[2] else trade(*send[:2]) for send in sends]


def meet(streams, others=()):
    streams = [stream for stream in streams if stream.sent]
    arrived, others = lax.optimization_barrier(([stream.sent for stream in streams], others))
    before = []
    for stream, got in zip(streams, arrived):
        stream.go(after(got, before) if before else got)
        before = before + stream.raw
    return others


def spread_columns_body(cols, chip_ref, *refs):
    out_ref = refs[-1]
    first = chip_ref[0] == 0
    own, sib = refs[:4], refs[4:8]
    picks = [
        (0, chip_ref[1] == 0, 0, 1),
        (1, chip_ref[1] == 1, 0, 1),
        (2, chip_ref[2] == 0, 2, 3),
    ]
    for kind, mine, here, there in picks:
        for j in range(cols):
            a, b = (jnp.where(mine, t[here][0, j], t[there][0, j]).astype(F32) for t in (own, sib))
            left = 2 * kind * cols + j
            out_ref[:, lanes_of(left)] = jnp.where(first, a, b)
            out_ref[:, lanes_of(left + cols)] = jnp.where(first, b, a)


def spread_rows_body(chip_ref, *refs):
    out_ref = refs[-1]
    own = pl.program_id(0) == chip_ref[0]
    mine = chip_ref[2] == 1
    subs, cols, lines, unused = refs[0].shape
    for at in range(subs):
        from_at = at ^ chip_ref[4]
        for j in range(cols):
            a, b = (
                jnp.where(mine, refs[t][from_at, j], refs[t + 1][from_at, j]) for t in (0, 2)
            )
            out_ref[lanes_of(j), at * lines : (at + 1) * lines] = (
                jnp.where(own, a, b).astype(F32).T
            )


def spread(chip, own, sib, width, mine, subs):
    cols = mine // LANES
    lines = width // subs
    block = math.gcd(lines, 192)

    def view(t):
        return t.reshape(subs, -1, LANES)[:, : cols * lines].reshape(subs, cols, lines, LANES)

    def part(p):
        def index(i, m):
            return ((i * block // lines) ^ m[3 + p], 0, i % (lines // block), 0)

        return pl.BlockSpec((1, cols, block, LANES), index)

    parts = [[view(t) for pair in side for t in pair] for side in (own, sib)]
    grad_qkv = call(
        functools.partial(spread_columns_body, cols), "spread_columns",
        shape((width, 3 * width), F32), (chip, *parts[0], *parts[1]), grid=(width // block,),
        scalars=1, in_specs=[part(0), part(0), part(1), part(1)] * 2,
        out_specs=pl.BlockSpec((block, 3 * width), lambda i, m: (i, 0)),
    )
    whole = pl.BlockSpec((subs, cols, lines, LANES), lambda i, m: (0, 0, 0, 0))
    grad_out = call(
        spread_rows_body, "spread_rows", shape((width, width), F32),
        (chip, *parts[0][2:], *parts[1][2:]), grid=(2,), scalars=1, in_specs=[whole] * 4,
        out_specs=pl.BlockSpec((mine, width), lambda i, m: (i, 0)),
    )
    return grad_qkv, grad_out


def on_device(
    layer_input,
    token_ids,
    segment_ids,
    hash_table,
    first_gain,
    first_bias,
    second_gain,
    second_bias,
    w_qkv,
    w_out,
    w_up,
    w_down,
    cotangent,
):
    x = layer_input[0]
    cot = cotangent[0]
    local_len, width = x.shape
    mine = width // 2
    sources = lax.axis_size("exp")
    ring = lax.axis_size("seq")
    capacity = 2 * local_len // sources
    seq_at = lax.axis_index("seq")
    exp_at = lax.axis_index("exp")
    core = (seq_at % 2).astype(jnp.int32)
    core_arg = core.reshape(1)
    norms = jnp.concatenate([first_gain, first_bias, second_gain, second_bias])
    norms = norms.reshape(-1, LANES)
    up, down = w_up[0], w_down[0]

    hal = shift(x, "seq", 2)
    sib = swap(x, "seq", 1)

    place = exp_at.astype(jnp.int32).reshape(1)
    at = jnp.stack([exp_at, core, seq_at // 2]).astype(jnp.int32)
    lines = -(-hash_table.shape[0] // (8 * LANES)) * 8
    table = jnp.pad(hash_table, (0, lines * LANES - hash_table.shape[0])).reshape(lines, LANES)
    docs = 2 * ring * local_len // DOC_MOST
    slot, low, low_tall, meta, *grad_out = route(
        at, token_ids, table, cot, segment_ids, sources, capacity, docs
    )
    grad_in = [grad_out[0]] + [swap(grad_out[k], "exp", k) for k in range(1, sources)]

    *made, q = project(core_arg, x, after(sib, slot), norms, w_qkv, None)
    hal = after(hal, q)
    has = swap(hal, "seq", 1)
    a, k, v = project(core_arg, hal, has, norms, w_qkv, made)
    attn_own, attn_give, attn_all, attn_tall, logs = attend(meta, q, k, v, low_tall)
    attn_other = swap(attn_give, "seq", 1)
    resid, *rows_out = lift(
        core_arg, attn_own, after(attn_other, grad_in), w_out, x, norms, slot, sources, capacity
    )
    rows_in = [rows_out[0]] + [swap(rows_out[k], "exp", k) for k in range(1, sources)]
    talls, pres, backs, outs, turned = [], [], [], [], []
    for k_at in range(sources):
        tall, pre, back, out, turn = expert(rows_in[k_at], grad_in[k_at], up, down)
        talls.append(tall)
        pres.append(pre)
        outs.append(out)
        turned.append(turn)
        backs.append(back if k_at == 0 else swap(back, "exp", k_at))
        if k_at + 1 < sources:
            rows_in[k_at + 1] = after(rows_in[k_at + 1], back)
    bits = [1 << b for b in range(1, ring.bit_length() - 1)]
    orders = [bits, bits[::-1]]
    sides = [(seq_at // o[0]) % 2 for o in orders]
    subs = ring // 4
    masks = [
        sum((1 - (seq_at // bit) % 2) << (len(o) - 2 - at) for at, bit in enumerate(o[1:]))
        for o in orders
    ]
    chip = jnp.stack([core, *sides, *masks]).astype(jnp.int32)

    turned, backs[:-2] = lax.optimization_barrier((turned, backs[:-2]))
    blocks = expert_grad(chip, turned, grad_in, talls, pres, subs)
    given, kept = blocks[:2], blocks[2:]
    given, backs[-2] = lax.optimization_barrier((given, backs[-2]))
    given, backs[-1] = lax.optimization_barrier((given, backs[-1]))
    got = [swap(t, "seq", 1) for t in given]
    gr, gattn, gain_two_grad, bias_two_grad = lower(slot, resid, cot, norms, backs)
    got = after(got, gattn)
    goes = [add(kept[p][:width], got[p][:width]) for p in range(2)]
    stays = [[kept[p][width:], got[p][width:]] for p in range(2)]
    experts = Stream(expert_steps(list(zip(stays, goes)), orders))
    outs = after(outs, goes)
    returned = [outs[0]] + [swap(outs[k], "exp", k) for k in range(1, sources)]
    gattn_sib = swap(gattn, "seq", 1)
    unit = sources * 16
    sub = -(-(mine // LANES * width // subs) // unit) * unit
    gq, gk, gv = attend_back(
        meta, q, k, v, gattn, after(gattn_sib, goes), w_out, attn_tall, logs, low
    )
    pieces = dense_pieces(chip, a, gq, gk, gv, attn_all, gattn, gattn_sib, subs, sub)
    pieces, returned = lax.optimization_barrier((pieces, returned))
    dense = Stream(
        dense_steps([([pieces[0]], pieces[1]), ([pieces[2]], pieces[3])], orders)
    )
    (gq,) = meet([experts], (after(gq, pieces),))
    keep, give, halo, gain_one_grad, bias_one_grad = project_back(
        core_arg, x, sib, hal, has, gq, gk, gv, w_qkv
    )
    small = jnp.concatenate([gain_one_grad, bias_one_grad, gain_two_grad, bias_two_grad], axis=0)
    (give,) = meet([dense, experts], (give,))
    near = swap(give, "seq", 1)
    hops = [("seq", bit) for bit in [1] + bits]
    hops += [("exp", 1 << b) for b in range(sources.bit_length() - 1)]
    small = Stream(small_steps(small, hops))
    (near,) = meet([dense, small], (near,))
    for rest in range(len(bits) - 2):
        meet([dense, experts])
    far = add(halo, near[local_len:])
    layer_output = finish(slot, resid, returned)
    layer_output, far = meet([dense, experts, small], (layer_output, far))
    far = shift(far, "seq", -2)
    for rest in range(len(bits) - 2):
        meet([experts])
    own_parts = experts.result
    other_chip = across(own_parts, orders)
    other_core = beside(after(own_parts, layer_output))
    meet([dense, other_chip, other_core, small])
    other_both = beside(other_chip.result)
    hidden = down.shape[0]
    made = widen(core, sides, masks, own_parts, other_chip.result, (), hidden, subs)
    while dense.result is None:
        made = meet([dense, other_both, small], made)
    own_dense = dense.result
    dense_chip, dense_core = across(own_dense, orders), beside(own_dense)
    made = widen(
        1 - core, sides, masks, other_core.result, other_both.result, made, hidden, subs
    )
    grad_w_up, grad_w_down = meet([dense_chip, dense_core, small], made)
    dense_both = beside(dense_chip.result)
    meet([dense_both, small])
    while small.sent:
        small.go(small.sent)
    grad_w_qkv, grad_w_out = spread(
        chip, list(zip(own_dense, dense_chip.result)),
        list(zip(dense_core.result, dense_both.result)), width, mine, subs,
    )
    grad_input = close(x, gr, keep, near, after(far, grad_w_qkv), norms)
    small = small.result
    return (
        layer_output[None],
        grad_input[None],
        grad_w_qkv,
        grad_w_out,
        small[0],
        small[1],
        small[2],
        small[3],
        grad_w_up[None],
        grad_w_down[None],
    )


def solution(mesh):
    in_specs = (
        P("exp", "seq", None),
        P("exp", "seq"),
        P("exp", None),
        P(),
        P(),
        P(),
        P(),
        P(),
        P(),
        P(),
        P("exp", None, None),
        P("exp", None, None),
        P("exp", "seq", None),
    )
    out_specs = (
        P("exp", "seq", None),
        P("exp", "seq", None),
        P(),
        P(),
        P(),
        P(),
        P(),
        P(),
        P("exp", None, None),
        P("exp", None, None),
    )
    return jax.shard_map(
        on_device, mesh=mesh, in_specs=in_specs, out_specs=out_specs, check_vma=False
    )
```

```python
import functools
import math

import jax
import jax.numpy as jnp
from jax import lax
from jax.experimental import pallas as pl
from jax.experimental.pallas import tpu as pltpu
from jax.sharding import PartitionSpec as P

HEADS = 12
HEAD_DIM = 64
DOC_MOST = 1024
EPSILON = 1e-05
LOW = -1e30
LOWER = -2e30
LANES = 128
TILE = 256
F32 = jnp.float32
BF16 = jnp.bfloat16
MIB = 1 << 20
COST = 1


def dot(a, b):
    return lax.dot_general(a, b, (((1,), (0,)), ((), ())), preferred_element_type=F32)


def dot_nt(a, b):
    return lax.dot_general(a, b, (((1,), (1,)), ((), ())), preferred_element_type=F32)


def dot_tn(a, b):
    return lax.dot_general(a, b, (((0,), (0,)), ((), ())), preferred_element_type=F32)


def iota(shape, axis):
    return lax.broadcasted_iota(jnp.int32, shape, axis)


def one_hot(ids, width):
    return jnp.where(iota((ids.shape[0], width), 1) == ids, 1.0, 0.0).astype(BF16)


def norm_rows(values):
    center = values - jnp.mean(values, axis=-1, keepdims=True)
    scale = lax.rsqrt(jnp.mean(center * center, axis=-1, keepdims=True) + EPSILON)
    return center * scale, scale


def norm_back(grad, normed, scale):
    inner = jnp.mean(grad * normed, axis=-1, keepdims=True)
    return scale * (grad - jnp.mean(grad, axis=-1, keepdims=True) - normed * inner)


def after(value, *others):
    return lax.optimization_barrier((value, others))[0]


def shape(dims, dtype):
    return jax.ShapeDtypeStruct(dims, dtype)


def call(body, name, out_shape, args, *, grid=(), in_specs=None, out_specs=None, scratch=(),
         scalars=0, aliases=None, flops=0, nbytes=0, special=0, vmem=56):
    outs = out_shape if isinstance(out_shape, (tuple, list)) else [out_shape]
    whole = pl.BlockSpec(memory_space=pltpu.VMEM)
    if in_specs is None:
        in_specs = [whole] * (len(args) - scalars)
    if out_specs is None:
        out_specs = [whole] * len(outs)
        if not isinstance(out_shape, (tuple, list)):
            out_specs = out_specs[0]
    return pl.pallas_call(
        body,
        name=name,
        out_shape=out_shape,
        grid_spec=pltpu.PrefetchScalarGridSpec(
            num_scalar_prefetch=scalars,
            grid=grid,
            in_specs=in_specs,
            out_specs=out_specs,
            scratch_shapes=scratch,
        ),
        input_output_aliases=aliases or {},
        cost_estimate=pl.CostEstimate(flops=COST, bytes_accessed=COST, transcendentals=0),
        compiler_params=pltpu.CompilerParams(vmem_limit_bytes=vmem * MIB),
    )(*args)


def column(row):
    return jnp.broadcast_to(row.astype(F32), (8, row.shape[1])).T[:, :1].astype(jnp.int32)


def route_body(parts, capacity, docs, at_ref, ids_ref, table_ref, rows_ref, segment_ref, slot_ref,
               low_ref, tall_ref, meta_ref, *out_refs):
    ids = column(ids_ref[...])
    count = ids.shape[0]
    lines = table_ref.shape[0]
    picked = dot(one_hot(ids >> 7, lines), table_ref[...].astype(F32).astype(BF16))
    lane = iota((count, LANES), 1)
    choice = jnp.sum(
        jnp.where(lane == (ids & (LANES - 1)), picked, 0.0), axis=1, keepdims=True
    ).astype(jnp.int32)
    mine = lane == choice
    below = jnp.where(iota((count, count), 0) > iota((count, count), 1), 1.0, 0.0).astype(BF16)
    ranks = dot(below, jnp.where(mine, 1.0, 0.0).astype(BF16))
    rank = jnp.sum(jnp.where(mine, ranks, 0.0), axis=1, keepdims=True).astype(jnp.int32)
    slot = (choice ^ at_ref[0]) * capacity + rank
    slot_ref[...] = slot
    rows = rows_ref[...]
    for k in range(parts):
        chosen = one_hot(slot - k * capacity, capacity)
        out_refs[k][...] = dot_tn(chosen, rows).astype(BF16)

    pair_len = low_ref.shape[1]
    pair_at = pl.multiple_of(at_ref[2] * pair_len, pair_len)
    segments = segment_ref[...]
    here = segment_ref[:, pl.ds(pair_at, pair_len)]
    low = jnp.zeros((1, pair_len), F32)
    for d in range(docs):
        start = jnp.sum(jnp.where(segments < d, 1.0, 0.0), axis=1, keepdims=True)
        low = low + jnp.where(here == d, start, 0.0)
    low = low.astype(jnp.int32) - (pair_at - pair_len)
    low_ref[...] = low
    tall_ref[...] = column(low)
    place = iota((1, LANES), 1)
    meta = jnp.where(place == 0, at_ref[1], 0)
    for t in range(pair_len // TILE):
        meta = jnp.where(place == 1 + t, low[:, t * TILE : t * TILE + 1] >> 8, meta)
    meta_ref[...] = meta


def route(at, ids, table, rows, segments, parts, capacity, docs):
    count, width = rows.shape
    pair_len = 2 * count
    outs = [shape((count, 1), jnp.int32), shape((1, pair_len), jnp.int32),
            shape((pair_len, 1), jnp.int32), shape((1, LANES), jnp.int32)]
    outs += [shape((capacity, width), BF16)] * parts
    return call(
        functools.partial(route_body, parts, capacity, docs), "route", outs,
        (at, ids, table, rows, segments), scalars=1,
    )


def vector(ref, at):
    lines = ref.shape[0] // 4
    return jnp.concatenate([ref[at * lines + j : at * lines + j + 1, :] for j in range(lines)], axis=1)


def project_body(skip, core_ref, own_ref, sib_ref, norm_ref, wq_ref, wk_ref, wv_ref, *refs):
    outs = refs[skip:-1]
    held_ref = refs[-1]
    step = pl.program_id(0)
    half = (pl.num_programs(0) - 1) // 2
    before = held_ref[(step + 1) % 2]
    outs[1][...] = dot(before, wk_ref[...]).astype(BF16)
    outs[2][...] = dot(before, wv_ref[...]).astype(BF16)
    if not skip:
        outs[3][...] = dot(before, wq_ref[...]).astype(BF16)
    rows = jnp.where(step < half, own_ref[...], sib_ref[...])
    normed, unused = norm_rows(rows.astype(F32))
    a = (normed * vector(norm_ref, 0) + vector(norm_ref, 1)).astype(BF16)
    held_ref[step % 2] = a
    outs[0][...] = a


def project(core, own, sib, norms, w_qkv, made):
    count, width = own.shape
    mine = width // 2
    half = count // TILE
    base = 0 if made else 2 * half

    def place(i, c):
        return ((i // half) ^ c[0]) * half + i % half

    def now(i, c):
        return (base + place(jnp.minimum(i, 2 * half - 1), c), 0)

    def then(i, c):
        return (base + place(jnp.maximum(i - 1, 0), c), 0)

    in_specs = [
        pl.BlockSpec((TILE, width), lambda i, c: (jnp.minimum(i, half - 1), 0)),
        pl.BlockSpec((TILE, width), lambda i, c: (jnp.clip(i - half, 0, half - 1), 0)),
        pl.BlockSpec(norms.shape, lambda i, c: (0, 0)),
    ] + [
        pl.BlockSpec((width, mine), functools.partial(lambda t, i, c: (0, 2 * t + c[0]), t))
        for t in range(3)
    ]
    args = [core, own, sib, norms, w_qkv, w_qkv, w_qkv]
    outs = [shape((4 * count, width), BF16)] + [shape((4 * count, mine), BF16)] * 2
    out_specs = [
        pl.BlockSpec((TILE, width), now),
        pl.BlockSpec((TILE, mine), then),
        pl.BlockSpec((TILE, mine), then),
    ]
    aliases = {}
    if made:
        in_specs += [pl.BlockSpec(memory_space=pl.ANY)] * 3
        aliases = {7: 0, 8: 1, 9: 2}
        args += list(made)
    else:
        outs.append(shape((2 * count, mine), BF16))
        out_specs.append(
            pl.BlockSpec((TILE, mine), lambda i, c: (place(jnp.maximum(i - 1, 0), c), 0))
        )
    return call(
        functools.partial(project_body, 3 if made else 0), "project", outs, args,
        grid=(2 * half + 1,), in_specs=in_specs, out_specs=out_specs, scalars=1, aliases=aliases,
        scratch=[pltpu.VMEM((2, TILE, width), BF16)],
    )


def masked_heads(block):
    lane = iota(block.shape, 1)
    zero = jnp.zeros((), block.dtype)
    return [
        jnp.where(lane < HEAD_DIM, block, zero),
        jnp.where(lane < HEAD_DIM, zero, block),
    ]


def flip(block):
    return block.astype(F32).T.astype(block.dtype)


def lanes_of(group):
    return slice(group * LANES, (group + 1) * LANES)


def put_heads(heads_ref, q_ref):
    def some(t, unused):
        here = pl.ds(pl.multiple_of(t * TILE, TILE), TILE)
        block = q_ref[here, :] * jnp.asarray(HEAD_DIM**-0.5, BF16)
        for g in range(q_ref.shape[1] // LANES):
            for h, part in enumerate(masked_heads(block[:, lanes_of(g)])):
                heads_ref[2 * g + h, here, :] = part
        return unused

    lax.fori_loop(0, q_ref.shape[0] // TILE, some, 0, unroll=2)


def tile_mask(begin, low, high):
    place = begin + iota((TILE, TILE), 0)
    return (place >= low) & (place <= high)


def attend_body(meta_ref, q_ref, k_ref, v_ref, lo_ref, own_ref, sib_ref, all_ref, tall_ref,
                log_ref, heads_ref, acc_ref, rows_ref):
    total, mine = q_ref.shape
    half = total // 2
    heads = range(mine // HEAD_DIM)
    put_heads(heads_ref, q_ref)
    core = meta_ref[0, 0]

    def tile(t, unused):
        at = pl.multiple_of(t * TILE, TILE)
        here = pl.ds(at, TILE)
        low = lo_ref[here, :]
        high = total + at + iota((TILE, 1), 0)
        acc_ref[...] = jnp.zeros_like(acc_ref)

        def step(j, state):
            begin = pl.multiple_of(j * TILE, TILE)
            there = pl.ds(begin, TILE)
            place = begin + iota((TILE, TILE), 1)
            allowed = (place >= low) & (place <= high)
            scores = [
                jnp.where(
                    allowed, dot_nt(heads_ref[h, here, :], k_ref[there, lanes_of(h // 2)]), LOWER
                )
                for h in heads
            ]
            tops = [
                jnp.maximum(state[2 * h], jnp.max(scores[h], axis=1, keepdims=True)) for h in heads
            ]
            shares = [jnp.exp(scores[h] - tops[h]) for h in heads]
            factors = [jnp.exp(state[2 * h] - tops[h]) for h in heads]
            sums = [
                state[2 * h + 1] * factors[h] + jnp.sum(shares[h], axis=1, keepdims=True)
                for h in heads
            ]
            more = [dot(shares[h].astype(BF16), v_ref[there, lanes_of(h // 2)]) for h in heads]
            for h in heads:
                acc_ref[h] = acc_ref[h] * factors[h] + more[h]
            return tuple(x for h in heads for x in (tops[h], sums[h]))

        first = (jnp.full((TILE, 1), LOW, F32), jnp.zeros((TILE, 1), F32))
        state = lax.fori_loop(
            meta_ref[0, 1 + t], total // TILE + t + 1, step, first * len(heads)
        )
        lane = iota((TILE, LANES), 1)
        logs = jnp.zeros((TILE, LANES), F32)
        for h in heads:
            logs = jnp.where(lane == h, state[2 * h] + jnp.log(state[2 * h + 1]), logs)
        log_ref[:, here] = logs.T[: log_ref.shape[0], :]
        for g in range(mine // LANES):
            left = acc_ref[2 * g] / state[4 * g + 1]
            right = acc_ref[2 * g + 1] / state[4 * g + 3]
            out = jnp.where(lane < HEAD_DIM, left, right)
            rows_ref[here, lanes_of(g)] = out
            tall_ref[lanes_of(g), here] = out.T
        return unused

    lax.fori_loop(0, total // TILE, tile, 0)

    def some(t, unused):
        at = pl.multiple_of(t * TILE, TILE)
        here = pl.ds(at, TILE)
        own_at = pl.ds(pl.multiple_of(core * half + at, TILE), TILE)
        sib_at = pl.ds(pl.multiple_of((1 - core) * half + at, TILE), TILE)
        all_ref[own_at, :] = rows_ref[own_at, :].astype(BF16)
        all_ref[sib_at, :] = rows_ref[sib_at, :].astype(BF16)
        own_ref[here, :] = rows_ref[own_at, :].astype(BF16)
        sib_ref[here, :] = rows_ref[sib_at, :].astype(BF16)
        return unused

    lax.fori_loop(0, half // TILE, some, 0)


def attend(meta, q, k, v, low):
    total, mine = q.shape
    heads = mine // HEAD_DIM
    outs = [
        shape((total // 2, mine), BF16),
        shape((total // 2, mine), BF16),
        shape((total, mine), BF16),
        shape((mine, total), F32),
        shape((-(-heads // 8) * 8, total), F32),
    ]
    return call(
        attend_body, "attend", outs, (meta, q, k, v, low), scalars=1,
        scratch=[pltpu.VMEM((heads, total, LANES), BF16), pltpu.VMEM((heads, TILE, LANES), F32),
                 pltpu.VMEM((total, mine), F32)],
    )


def fetch(pairs, sems):
    copies = [pltpu.make_async_copy(a, b, sems.at[i]) for i, (a, b) in enumerate(pairs)]
    for copy in copies:
        copy.start()
    return [copy.wait for copy in copies]


def both_rows(core, own, sib, rows_ref):
    half = own.shape[0]
    return [
        (own, rows_ref.at[pl.ds(pl.multiple_of(core * half, half), half), :]),
        (sib, rows_ref.at[pl.ds(pl.multiple_of((1 - core) * half, half), half), :]),
    ]


def attend_back_body(meta_ref, q_hbm, k_hbm, v_hbm, own_hbm, sib_hbm, wo_hbm, tall_hbm, log_ref,
                     lo_ref, gq_ref, gk_ref, gv_ref, rows_ref, heads_ref, grads_ref, delta_ref,
                     kt_ref, gqt_ref, gks_ref, gvs_ref, q_ref, k_ref, v_ref, wo_ref, tall_ref,
                     sems):
    total, mine = q_ref.shape
    heads = mine // HEAD_DIM
    core = meta_ref[0, 0]
    mine_at = pl.ds(pl.multiple_of(core * mine, mine), mine)
    waits = fetch(
        both_rows(core, own_hbm, sib_hbm, rows_ref)
        + [(wo_hbm.at[mine_at, :], wo_ref), (tall_hbm, tall_ref), (q_hbm, q_ref), (k_hbm, k_ref),
           (v_hbm, v_ref)],
        sems,
    )

    def clear(t, unused):
        here = pl.ds(pl.multiple_of(t * TILE, TILE), TILE)
        gks_ref[here, :] = jnp.zeros((TILE, mine), F32)
        gvs_ref[here, :] = jnp.zeros((TILE, mine), F32)
        return unused

    lax.fori_loop(0, 2 * total // TILE, clear, 0)
    gqt_ref[...] = jnp.zeros_like(gqt_ref)
    for wait in waits[:4]:
        wait()
    weights = wo_ref[...]

    def begin(t, unused):
        here = pl.ds(pl.multiple_of(t * TILE, TILE), TILE)
        grads = dot_nt(rows_ref[here, :], weights).astype(BF16)
        turned = grads.astype(F32).T * tall_ref[:, here]
        for h in range(heads):
            span = slice(h * HEAD_DIM, (h + 1) * HEAD_DIM)
            delta_ref[h : h + 1, here] = jnp.sum(turned[span, :], axis=0, keepdims=True)
        for g in range(mine // LANES):
            for h, part in enumerate(masked_heads(grads[:, lanes_of(g)])):
                grads_ref[2 * g + h, here, :] = part
        return unused

    lax.fori_loop(0, total // TILE, begin, 0, unroll=4)
    waits[4]()
    put_heads(heads_ref, q_ref)
    waits[5]()

    def turn(t, unused):
        here = pl.ds(pl.multiple_of(t * TILE, TILE), TILE)
        kt_ref[:, here] = flip(k_ref[here, :])
        return unused

    lax.fori_loop(0, 2 * total // TILE, turn, 0, unroll=2)
    waits[6]()

    def tile(t, unused):
        at = pl.multiple_of(t * TILE, TILE)
        here = pl.ds(at, TILE)
        low = lo_ref[:, here]
        high = total + at + iota((1, TILE), 1)

        logs = [log_ref[h : h + 1, here] for h in range(heads)]
        deltas = [delta_ref[h : h + 1, here] for h in range(heads)]

        def step(j, carry):
            begin = pl.multiple_of(j * TILE, TILE)
            there = pl.ds(begin, TILE)
            allowed = tile_mask(begin, low, high)
            every = range(heads)
            queries = [heads_ref[h, here, :] for h in every]
            grads = [grads_ref[h, here, :] for h in every]
            scores = [dot_nt(k_ref[there, lanes_of(h // 2)], queries[h]) for h in every]
            grad_soft = [dot_nt(v_ref[there, lanes_of(h // 2)], grads[h]) for h in every]
            soft = [jnp.exp(jnp.where(allowed, scores[h], LOWER) - logs[h]) for h in every]
            grad_scores = [(soft[h] * (grad_soft[h] - deltas[h])).astype(BF16) for h in every]
            soft = [s.astype(BF16) for s in soft]
            gv = [dot(soft[h], grads[h]) for h in every]
            gk = [dot(grad_scores[h], queries[h]) for h in every]
            gq = [
                dot(kt_ref[h * HEAD_DIM : (h + 1) * HEAD_DIM, there], grad_scores[h])
                for h in every
            ]
            for g in range(heads // 2):
                gvs_ref[there, lanes_of(g)] += gv[2 * g] + gv[2 * g + 1]
                gks_ref[there, lanes_of(g)] += gk[2 * g] + gk[2 * g + 1]
            for h in every:
                gqt_ref[h * HEAD_DIM : (h + 1) * HEAD_DIM, here] += gq[h]
            return carry

        return lax.fori_loop(meta_ref[0, 1 + t], total // TILE + t + 1, step, unused)

    lax.fori_loop(0, total // TILE, tile, 0)

    def finish_queries(t, unused):
        here = pl.ds(pl.multiple_of(t * TILE, TILE), TILE)
        gq_ref[here, :] = (gqt_ref[:, here].T * (HEAD_DIM**-0.5)).astype(BF16)
        return unused

    def finish_keys(t, unused):
        here = pl.ds(pl.multiple_of(t * TILE, TILE), TILE)
        gk_ref[here, :] = gks_ref[here, :].astype(BF16)
        gv_ref[here, :] = gvs_ref[here, :].astype(BF16)
        return unused

    lax.fori_loop(0, total // TILE, finish_queries, 0)
    lax.fori_loop(0, 2 * total // TILE, finish_keys, 0, unroll=2)


def attend_back(meta, q, k, v, own, sib, w_out, tall, logs, low):
    total, mine = q.shape
    width = own.shape[1]
    heads = mine // HEAD_DIM
    outs = [
        shape((total, mine), BF16),
        shape((2 * total, mine), BF16),
        shape((2 * total, mine), BF16),
    ]
    return call(
        attend_back_body, "attend_back", outs,
        (meta, q, k, v, own, sib, w_out, tall, logs, low), scalars=1,
        in_specs=[pl.BlockSpec(memory_space=pl.ANY)] * 7 + [pl.BlockSpec(memory_space=pltpu.VMEM)] * 2,
        scratch=[pltpu.VMEM((total, width), BF16), pltpu.VMEM((heads, total, LANES), BF16),
                 pltpu.VMEM((heads, total, LANES), BF16), pltpu.VMEM(logs.shape, F32),
                 pltpu.VMEM((mine, 2 * total), BF16), pltpu.VMEM((mine, total), F32),
                 pltpu.VMEM((2 * total, mine), F32), pltpu.VMEM((2 * total, mine), F32),
                 pltpu.VMEM(q.shape, BF16), pltpu.VMEM(k.shape, BF16), pltpu.VMEM(v.shape, BF16),
                 pltpu.VMEM((mine, width), BF16), pltpu.VMEM(tall.shape, F32),
                 pltpu.SemaphoreType.DMA((7,))],
    )


def dense_body(subs, sub, chip_ref, a_hbm, gq_hbm, gk_hbm, gv_hbm, all_hbm, own_hbm, sib_hbm,
               *refs):
    piece_refs = refs[:4]
    dense_ref, rows_ref, short_ref, long_ref, sems = refs[4:]
    unused, total, mine = short_ref.shape
    half = total // 2
    width = rows_ref.shape[1]
    lines = width // subs
    quarter = subs * sub
    core = chip_ref[0]
    own_at = pl.multiple_of(2 * total + core * half, half)
    sib_at = pl.multiple_of(2 * total + (1 - core) * half, half)
    waits = fetch(
        [(own_hbm, rows_ref.at[pl.ds(own_at, half), :]),
         (sib_hbm, rows_ref.at[pl.ds(sib_at, half), :]),
         (a_hbm, rows_ref.at[pl.ds(0, 2 * total), :]),
         (gq_hbm, short_ref.at[0]), (all_hbm, short_ref.at[1]),
         (gk_hbm, long_ref.at[0]), (gv_hbm, long_ref.at[1])],
        sems,
    )

    def put(kind, turned):
        for j in range(mine // LANES):
            block = turned[lanes_of(j), :].T.astype(BF16)
            for at in range(subs):
                first = pl.multiple_of(kind * quarter + at * sub + j * lines, 16)
                dense_ref[pl.ds(first, lines), :] = block[at * lines : (at + 1) * lines, :]

    def short(i, unused):
        rows = rows_ref[pl.ds(pl.multiple_of((1 + i) * total, total), total), :]
        put(3 * i, dot_tn(short_ref[i], rows))
        return unused

    def long(i, unused):
        put(1 + i, dot_tn(long_ref[i], rows_ref[: 2 * total, :]))
        return unused

    for wait in waits[:5]:
        wait()
    lax.fori_loop(0, 2, short, 0)
    waits[5]()
    waits[6]()
    lax.fori_loop(0, 2, long, 0)
    spare = sub - mine // LANES * lines
    if spare:
        for at in range(4 * subs):
            dense_ref[(at + 1) * sub - spare : (at + 1) * sub, :] = jnp.zeros((spare, LANES), BF16)
    for p in range(2):
        side = chip_ref[1 + p]
        for r, which in enumerate((side, 1 - side)):
            for at in range(subs):
                from_at = pl.multiple_of((2 * p + which) * quarter + at * sub, 16)
                to_at = pl.multiple_of((at ^ chip_ref[3 + p]) * sub, 16)
                piece_refs[2 * p + r][pl.ds(to_at, sub), :] = dense_ref[pl.ds(from_at, sub), :]


def dense_pieces(chip, a, gq, gk, gv, attn_all, own, sib, subs, sub):
    return call(
        functools.partial(dense_body, subs, sub), "dense",
        [shape((subs * sub, LANES), BF16)] * 4,
        (chip, a, gq, gk, gv, attn_all, own, sib), scalars=1,
        in_specs=[pl.BlockSpec(memory_space=pl.ANY)] * 7,
        scratch=[pltpu.VMEM((4 * subs * sub, LANES), BF16),
                 pltpu.VMEM((3 * gq.shape[0], a.shape[1]), BF16),
                 pltpu.VMEM((2, *gq.shape), BF16), pltpu.VMEM((2, *gk.shape), BF16),
                 pltpu.SemaphoreType.DMA((7,))],
    )


def lift_body(parts, capacity, core_ref, own_ref, other_ref, w_ref, x_ref, norm_ref, slot_ref,
              resid_ref, *out_refs):
    mine = own_ref.shape[1]
    core = core_ref[0]
    own_at = pl.ds(pl.multiple_of(core * mine, mine), mine)
    other_at = pl.ds(pl.multiple_of((1 - core) * mine, mine), mine)
    *out_refs, rows_ref = out_refs

    def some(t, unused):
        here = pl.ds(pl.multiple_of(t * TILE, TILE), TILE)
        more = dot(own_ref[here, :], w_ref[own_at, :]) + dot(other_ref[here, :], w_ref[other_at, :])
        resid = x_ref[here, :].astype(F32) + more
        resid_ref[here, :] = resid
        normed, scale = norm_rows(resid)
        rows_ref[here, :] = (normed * vector(norm_ref, 2) + vector(norm_ref, 3)).astype(BF16)
        return unused

    lax.fori_loop(0, own_ref.shape[0] // TILE, some, 0)
    slot = slot_ref[...]
    for k in range(parts):
        chosen = one_hot(slot - k * capacity, capacity)
        out_refs[k][...] = dot_tn(chosen, rows_ref[...]).astype(BF16)


def lift(core, own, other, w_out, x, norms, slot, parts, capacity):
    count, width = x.shape
    outs = [shape((count, width), F32)] + [shape((capacity, width), BF16)] * parts
    return call(
        functools.partial(lift_body, parts, capacity), "lift", outs,
        (core, own, other, w_out, x, norms, slot), scratch=[pltpu.VMEM((count, width), BF16)],
        scalars=1, flops=2 * count * width * (width + parts * capacity),
    )


GATE_A = math.sqrt(2.0 / math.pi)
GATE_B = 0.044715


def expert_body(sub, rows_ref, grad_ref, up_ref, down_ref, tall_ref, pre_ref, back_ref, out_ref,
                turned_ref, back_acc, out_acc):
    step = pl.program_id(0)

    @pl.when(step == 0)
    def _():
        back_acc[...] = jnp.zeros_like(back_acc)
        out_acc[...] = jnp.zeros_like(out_acc)
        turned_ref[...] = flip(rows_ref[...])

    parts = [slice(s * sub, (s + 1) * sub) for s in range(down_ref.shape[0] // sub)]
    pres = [dot(rows_ref[...], up_ref[:, part]) for part in parts]
    grads = [dot_nt(grad_ref[...], down_ref[part, :]) for part in parts]
    hids, slopes = [], []
    for pre in pres:
        square = pre * pre
        bend = jnp.tanh(GATE_A * (pre + GATE_B * (square * pre)))
        half = 0.5 + 0.5 * bend
        hids.append(pre * half)
        slopes.append(
            half + (pre * (1.0 - bend * bend)) * (0.5 * GATE_A + (1.5 * GATE_A * GATE_B) * square)
        )
    low = jnp.concatenate([(g * s).astype(BF16) for g, s in zip(grads, slopes)], axis=1)
    back_acc[...] += dot_nt(low, up_ref[...])
    out_acc[...] += dot(jnp.concatenate([h.astype(BF16) for h in hids], axis=1), down_ref[...])
    pre_ref[...] = low
    for part, hid in zip(parts, hids):
        tall_ref[part, :] = hid.T.astype(BF16)

    @pl.when(step == pl.num_programs(0) - 1)
    def _():
        back_ref[...] = back_acc[...].astype(BF16)
        out_ref[...] = out_acc[...].astype(BF16)


def expert(rows, grads, w_up, w_down, sub=256):
    count, width = rows.shape
    hidden = w_up.shape[1]
    block = width
    const = pl.BlockSpec((count, width), lambda j: (0, 0))
    return call(
        functools.partial(expert_body, sub), "expert",
        [shape((hidden, count), BF16), shape((count, hidden), BF16), shape((count, width), BF16),
         shape((count, width), BF16), shape((width, count), BF16)],
        (rows, grads, w_up, w_down), grid=(hidden // block,),
        in_specs=[const, const, pl.BlockSpec((width, block), lambda j: (0, j)),
                  pl.BlockSpec((block, width), lambda j: (j, 0))],
        out_specs=[pl.BlockSpec((block, count), lambda j: (j, 0)),
                   pl.BlockSpec((count, block), lambda j: (0, j)), const, const,
                   pl.BlockSpec((width, count), lambda j: (0, 0))],
        scratch=[pltpu.VMEM((count, width), F32)] * 2,
    )


def expert_grad_body(parts, subs, chip_ref, *refs):
    turned, grads, talls, pres = (refs[parts * t : parts * (t + 1)] for t in range(4))
    *outs, held_ref, sems = refs[4 * parts :]
    width = held_ref.shape[2]
    lines = width // subs
    step = pl.program_id(0)
    steps = len(outs)
    slot = step % 2

    def copy(t, at):
        return pltpu.make_async_copy(held_ref.at[at], outs[t], sems.at[at])

    @pl.when(step >= 2)
    def _():
        copy(0, slot).wait()

    def product(left, right):
        out = None
        for a, b in zip(left, right):
            more = dot(a[...], b[...])
            out = more if out is None else out + more
        return out.astype(BF16)

    half = steps // 2
    side, mask = chip_ref[1 + step % half], chip_ref[3 + step % half]
    pairs = ((product(turned, pres), side == 0), (product(talls, grads), side == 1))
    for value, stays in pairs:
        base = jnp.where(stays, width, 0)
        for at in range(subs):
            first = pl.multiple_of(base + (at ^ mask) * lines, 16)
            held_ref[slot, pl.ds(first, lines), :] = value[at * lines : (at + 1) * lines, :]

    for t in range(steps):

        @pl.when(step == t)
        def _(t=t):
            copy(t, t % 2).start()

    @pl.when(step == steps - 1)
    def _():
        copy(0, 0).wait()
        copy(0, 1).wait()


def expert_grad(chip, turned, grads, talls, pres, subs):
    parts = len(grads)
    count, width = grads[0].shape
    blocks = talls[0].shape[0] // width
    half = blocks // 2

    def column(i, m):
        return jnp.where(i < half, (1 - m[0]) * half, m[0] * half - half) + i

    const = lambda dims: pl.BlockSpec(dims, lambda i, m: (0, 0))
    return call(
        functools.partial(expert_grad_body, parts, subs), "expert_grad",
        [shape((2 * width, width), BF16)] * blocks,
        (chip, *turned, *grads, *talls, *pres), grid=(blocks,), scalars=1,
        in_specs=[const((width, count))] * parts + [const((count, width))] * parts
        + [pl.BlockSpec((width, count), lambda i, m: (column(i, m), 0))] * parts
        + [pl.BlockSpec((count, width), lambda i, m: (0, column(i, m)))] * parts,
        out_specs=[pl.BlockSpec(memory_space=pl.ANY)] * blocks,
        scratch=[pltpu.VMEM((2, 2 * width, width), BF16), pltpu.SemaphoreType.DMA((2,))],
    )


def widen_body(skip, meta_ref, *refs):
    pairs, (up_out, down_out) = refs[:4], refs[4 + skip :]
    second = pl.program_id(0) >= pl.num_programs(0) // 2
    first = meta_ref[1 + pl.program_id(0) // (pl.num_programs(0) // 2)] == 0
    mine = jnp.where(second, pairs[2][...], pairs[0][...])
    theirs = jnp.where(second, pairs[3][...], pairs[1][...])
    up_out[...] = jnp.where(first, mine, theirs).astype(F32)
    down_out[...] = jnp.where(first, theirs, mine).astype(F32)


def widen(core, sides, masks, mine, theirs, made, hidden, subs):
    width = mine[0].shape[1]
    rows = width // subs
    meta = jnp.stack([core, *sides, *masks]).astype(jnp.int32)

    def index(p):
        def at(i, m):
            here = jnp.clip(i - p * subs, 0, subs - 1)
            return (here ^ m[3 + p], 0)

        return at

    blocks = [pl.BlockSpec((rows, width), index(p)) for p in (0, 0, 1, 1)]
    column = lambda i, m: 2 * m[0] + i // subs
    return call(
        functools.partial(widen_body, len(made)), "widen",
        [shape((width, hidden), F32), shape((hidden, width), F32)],
        (meta, mine[0], theirs[0], mine[1], theirs[1], *made), grid=(2 * subs,), scalars=1,
        in_specs=blocks + [pl.BlockSpec(memory_space=pl.ANY)] * len(made),
        out_specs=[pl.BlockSpec((rows, width), lambda i, m: (i % subs, column(i, m))),
                   pl.BlockSpec((rows, width), lambda i, m: (column(i, m) * subs + i % subs, 0))],
        aliases={5: 0, 6: 1} if made else None,
    )


def collect(slot, part_refs):
    total = None
    for k, ref in enumerate(part_refs):
        capacity = ref.shape[0]
        more = dot(one_hot(slot - k * capacity, capacity), ref[...])
        total = more if total is None else total + more
    return total


def lower_body(parts, slot_ref, resid_ref, cot_ref, norm_ref, *refs):
    grads = collect(slot_ref[...], refs[:parts])
    gr_ref, low_ref, gain_out, bias_out = refs[parts:]
    normed, scale = norm_rows(resid_ref[...])

    @pl.when(pl.program_id(0) == 0)
    def _():
        gain_out[...] = jnp.zeros_like(gain_out)
        bias_out[...] = jnp.zeros_like(bias_out)

    gain_out[...] += jnp.sum(grads * normed, axis=0, keepdims=True)
    bias_out[...] += jnp.sum(grads, axis=0, keepdims=True)
    gr = cot_ref[...].astype(F32) + norm_back(grads * vector(norm_ref, 2), normed, scale)
    gr_ref[...] = gr
    low_ref[...] = gr.astype(BF16)


def row_specs(dims, *whole):
    return [pl.BlockSpec((TILE, d), lambda i: (i, 0)) for d in dims] + [
        pl.BlockSpec(w.shape, lambda i: (0, 0)) for w in whole
    ]


def lower(slot, resid, cot, norms, back):
    parts = len(back)
    count, width = resid.shape
    outs = [shape((count, width), F32), shape((count, width), BF16),
            shape((1, width), F32), shape((1, width), F32)]
    return call(
        functools.partial(lower_body, parts), "lower", outs, (slot, resid, cot, norms, *back),
        grid=(count // TILE,), in_specs=row_specs((1, width, width), norms, *back),
        out_specs=row_specs((width, width), outs[2], outs[3]),
    )


def finish_body(slot_ref, resid_ref, *refs):
    refs[-1][...] = (resid_ref[...] + collect(slot_ref[...], refs[:-1])).astype(BF16)


def finish(slot, resid, parts):
    count, width = resid.shape
    return call(
        finish_body, "finish", shape(resid.shape, BF16), (slot, resid, *parts),
        grid=(count // TILE,), in_specs=row_specs((1, width), *parts),
        out_specs=row_specs((width,))[0],
    )


def project_back_body(half, core_ref, own_ref, sib_ref, hal_ref, has_ref, gq_ref, gk_ref, gv_ref,
                      wq_ref, wk_ref, wv_ref, keep_ref, send_ref, halo_ref, gain_ref, bias_ref):
    step = pl.program_id(0)
    rows = jnp.where(
        step < 2 * half,
        jnp.where(step < half, own_ref[...], sib_ref[...]),
        jnp.where(step < 3 * half, hal_ref[...], has_ref[...]),
    )
    normed, unused = norm_rows(rows.astype(F32))
    here = step < 2 * half
    ga = dot_nt(gk_ref[...], wk_ref[...]) + dot_nt(gv_ref[...], wv_ref[...])
    gq = jnp.where(here, gq_ref[...], jnp.zeros_like(gq_ref))
    ga = ga + dot_nt(gq, wq_ref[...])

    @pl.when(step == 0)
    def _():
        gain_ref[...] = jnp.zeros_like(gain_ref)
        bias_ref[...] = jnp.zeros_like(bias_ref)

    gain_ref[...] += jnp.sum(ga * normed, axis=0, keepdims=True)
    bias_ref[...] += jnp.sum(ga, axis=0, keepdims=True)

    @pl.when(step < half)
    def _():
        keep_ref[...] = ga

    @pl.when((step // half) % 2 == 1)
    def _():
        send_ref[...] = ga.astype(BF16)

    @pl.when(step // half == 2)
    def _():
        halo_ref[...] = ga


def project_back(core, own, sib, hal, has, gq, gk, gv, w_qkv):
    count, width = own.shape
    mine = gq.shape[1]
    half = count // TILE

    def at(t):
        return lambda i, c: (jnp.clip(i - t * half, 0, half - 1), 0)

    def place(i, c):
        return jnp.where(i < 2 * half, 2 * half, 0) + (((i // half) % 2) ^ c[0]) * half + i % half

    def sent(i, c):
        late = half + jnp.clip(i - 3 * half, 0, half - 1)
        return (jnp.where(i < 2 * half, jnp.clip(i - half, 0, half - 1), late), 0)

    row = pl.BlockSpec((1, width), lambda i, c: (0, 0))
    in_specs = [pl.BlockSpec((TILE, width), at(t)) for t in range(4)] + [
        pl.BlockSpec((TILE, mine), lambda i, c: (jnp.maximum(place(i, c) - 2 * half, 0), 0)),
        pl.BlockSpec((TILE, mine), lambda i, c: (place(i, c), 0)),
        pl.BlockSpec((TILE, mine), lambda i, c: (place(i, c), 0)),
    ] + [
        pl.BlockSpec((width, mine), functools.partial(lambda t, i, c: (0, 2 * t + c[0]), t))
        for t in range(3)
    ]
    return call(
        functools.partial(project_back_body, half), "project_back",
        [shape((count, width), F32), shape((2 * count, width), BF16), shape((count, width), F32),
         shape((1, width), F32), shape((1, width), F32)],
        (core, own, sib, hal, has, gq, gk, gv, w_qkv, w_qkv, w_qkv),
        grid=(4 * half,), in_specs=in_specs, scalars=1,
        out_specs=[pl.BlockSpec((TILE, width), at(0)), pl.BlockSpec((TILE, width), sent),
                   pl.BlockSpec((TILE, width), at(2)), row, row],
        flops=20 * count * width * mine,
    )


def close_body(x_ref, gr_ref, keep_ref, near_ref, far_ref, norm_ref, out_ref):
    ga = keep_ref[...] + near_ref[...].astype(F32) + far_ref[...].astype(F32)
    normed, scale = norm_rows(x_ref[...].astype(F32))
    out_ref[...] = gr_ref[...] + norm_back(ga * vector(norm_ref, 0), normed, scale)


def close(x, gr, keep, near, far, norms):
    count, width = x.shape
    block = pl.BlockSpec((TILE, width), lambda i: (i, 0))
    return call(
        close_body, "close", shape((count, width), F32), (x, gr, keep, near, far, norms),
        grid=(count // TILE,),
        in_specs=[block] * 5 + [pl.BlockSpec(norms.shape, lambda i: (0, 0))], out_specs=block,
    )


def swap(block, axis, distance):
    return lax.ppermute(block, axis, [(i, i ^ distance) for i in range(lax.axis_size(axis))])


def trade(block, axis):
    return lax.all_to_all(block, axis, split_axis=0, concat_axis=0, tiled=True)


def shift(block, axis, distance):
    size = lax.axis_size(axis)
    route = [(i, i + distance) for i in range(size) if 0 <= i + distance < size]
    return lax.ppermute(block, axis, route)


def total(terms):
    return sum(t.astype(F32) for t in terms).astype(BF16)


def add(a, b):
    return total([a, b])


def at_index(block, index):
    return lax.dynamic_index_in_dim(block, index, 0, keepdims=False)


def scatter_steps(pieces, orders):
    pairs = list(pieces)
    for s in range(len(orders[0])):
        arrived = yield [(goes, "seq", bits[s]) for (stays, goes), bits in zip(pairs, orders)]
        terms = [stays + [got] for (stays, goes), got in zip(pairs, arrived)]
        if s + 1 < len(orders[0]):
            half = terms[0][0].shape[0] // 2
            pairs = [
                ([total([t[half:] for t in terms_p])], total([t[:half] for t in terms_p]))
                for terms_p in terms
            ]
    return [total(terms_p) for terms_p in terms]


def gather_steps(parts, orders):
    parts = list(parts)
    for s in reversed(range(1, len(orders[0]))):
        arrived = yield [(part, "seq", bits[s]) for part, bits in zip(parts, orders)]
        parts = [jnp.concatenate([got, part], axis=0) for got, part in zip(arrived, parts)]
    return parts


def dense_steps(pieces, orders):
    sources = lax.axis_size("exp")
    parts = yield from scatter_steps(pieces, orders)
    joined = jnp.stack([p.reshape(sources, -1, LANES) for p in parts], axis=1)
    (got,) = yield [(joined, "exp", 0)]
    own = jnp.sum(got.astype(F32), axis=0).astype(BF16)
    (got,) = yield [(jnp.broadcast_to(own, (sources, *own.shape)), "exp", 0)]
    parts = [got[:, p].reshape(-1, LANES) for p in range(len(orders))]
    return (yield from gather_steps(parts, orders))


def expert_steps(pieces, orders):
    parts = yield from scatter_steps(pieces, orders)
    return (yield from gather_steps(parts, orders))


def one_step(sends):
    return (yield sends)


def across(parts, orders):
    return Stream(one_step([(part, "seq", bits[0]) for part, bits in zip(parts, orders)]))


def beside(parts):
    return Stream(one_step([(part, "seq", 1) for part in parts]))


def small_steps(value, hops):
    for hop in hops:
        (got,) = yield [(value, *hop)]
        value = value + got
    return value


class Stream:
    def __init__(self, steps):
        self.steps = steps
        self.result = None
        self.sent = []
        self.go(None)

    def go(self, arrived):
        try:
            sends = self.steps.send(arrived)
        except StopIteration as stop:
            self.sent, self.raw, self.result = [], [], stop.value
        else:
            self.raw = [send[0] for send in sends]
            self.sent = [swap(*send) if send[2] else trade(*send[:2]) for send in sends]


def meet(streams, others=()):
    streams = [stream for stream in streams if stream.sent]
    arrived, others = lax.optimization_barrier(([stream.sent for stream in streams], others))
    before = []
    for stream, got in zip(streams, arrived):
        stream.go(after(got, before) if before else got)
        before = before + stream.raw
    return others


def spread_columns_body(cols, chip_ref, *refs):
    out_ref = refs[-1]
    first = chip_ref[0] == 0
    own, sib = refs[:4], refs[4:8]
    picks = [
        (0, chip_ref[1] == 0, 0, 1),
        (1, chip_ref[1] == 1, 0, 1),
        (2, chip_ref[2] == 0, 2, 3),
    ]
    for kind, mine, here, there in picks:
        for j in range(cols):
            a, b = (jnp.where(mine, t[here][0, j], t[there][0, j]).astype(F32) for t in (own, sib))
            left = 2 * kind * cols + j
            out_ref[:, lanes_of(left)] = jnp.where(first, a, b)
            out_ref[:, lanes_of(left + cols)] = jnp.where(first, b, a)


def spread_rows_body(chip_ref, *refs):
    out_ref = refs[-1]
    own = pl.program_id(0) == chip_ref[0]
    mine = chip_ref[2] == 1
    subs, cols, lines, unused = refs[0].shape
    for at in range(subs):
        from_at = at ^ chip_ref[4]
        for j in range(cols):
            a, b = (
                jnp.where(mine, refs[t][from_at, j], refs[t + 1][from_at, j]) for t in (0, 2)
            )
            out_ref[lanes_of(j), at * lines : (at + 1) * lines] = (
                jnp.where(own, a, b).astype(F32).T
            )


def spread(chip, own, sib, width, mine, subs):
    cols = mine // LANES
    lines = width // subs
    block = math.gcd(lines, 192)

    def view(t):
        return t.reshape(subs, -1, LANES)[:, : cols * lines].reshape(subs, cols, lines, LANES)

    def part(p):
        def index(i, m):
            return ((i * block // lines) ^ m[3 + p], 0, i % (lines // block), 0)

        return pl.BlockSpec((1, cols, block, LANES), index)

    parts = [[view(t) for pair in side for t in pair] for side in (own, sib)]
    grad_qkv = call(
        functools.partial(spread_columns_body, cols), "spread_columns",
        shape((width, 3 * width), F32), (chip, *parts[0], *parts[1]), grid=(width // block,),
        scalars=1, in_specs=[part(0), part(0), part(1), part(1)] * 2,
        out_specs=pl.BlockSpec((block, 3 * width), lambda i, m: (i, 0)),
    )
    whole = pl.BlockSpec((subs, cols, lines, LANES), lambda i, m: (0, 0, 0, 0))
    grad_out = call(
        spread_rows_body, "spread_rows", shape((width, width), F32),
        (chip, *parts[0][2:], *parts[1][2:]), grid=(2,), scalars=1, in_specs=[whole] * 4,
        out_specs=pl.BlockSpec((mine, width), lambda i, m: (i, 0)),
    )
    return grad_qkv, grad_out


def on_device(
    layer_input,
    token_ids,
    segment_ids,
    hash_table,
    first_gain,
    first_bias,
    second_gain,
    second_bias,
    w_qkv,
    w_out,
    w_up,
    w_down,
    cotangent,
):
    x = layer_input[0]
    cot = cotangent[0]
    local_len, width = x.shape
    mine = width // 2
    sources = lax.axis_size("exp")
    ring = lax.axis_size("seq")
    capacity = 2 * local_len // sources
    seq_at = lax.axis_index("seq")
    exp_at = lax.axis_index("exp")
    core = (seq_at % 2).astype(jnp.int32)
    core_arg = core.reshape(1)
    norms = jnp.concatenate([first_gain, first_bias, second_gain, second_bias])
    norms = norms.reshape(-1, LANES)
    up, down = w_up[0], w_down[0]

    hal = shift(x, "seq", 2)
    sib = swap(x, "seq", 1)

    place = exp_at.astype(jnp.int32).reshape(1)
    at = jnp.stack([exp_at, core, seq_at // 2]).astype(jnp.int32)
    lines = -(-hash_table.shape[0] // (8 * LANES)) * 8
    table = jnp.pad(hash_table, (0, lines * LANES - hash_table.shape[0])).reshape(lines, LANES)
    docs = 2 * ring * local_len // DOC_MOST
    slot, low, low_tall, meta, *grad_out = route(
        at, token_ids, table, cot, segment_ids, sources, capacity, docs
    )
    grad_in = [grad_out[0]] + [swap(grad_out[k], "exp", k) for k in range(1, sources)]

    *made, q = project(core_arg, x, after(sib, slot), norms, w_qkv, None)
    hal = after(hal, q)
    has = swap(hal, "seq", 1)
    a, k, v = project(core_arg, hal, has, norms, w_qkv, made)
    attn_own, attn_give, attn_all, attn_tall, logs = attend(meta, q, k, v, low_tall)
    attn_other = swap(attn_give, "seq", 1)
    resid, *rows_out = lift(
        core_arg, attn_own, after(attn_other, grad_in), w_out, x, norms, slot, sources, capacity
    )
    rows_in = [rows_out[0]] + [swap(rows_out[k], "exp", k) for k in range(1, sources)]
    talls, pres, backs, outs, turned = [], [], [], [], []
    for k_at in range(sources):
        tall, pre, back, out, turn = expert(rows_in[k_at], grad_in[k_at], up, down)
        talls.append(tall)
        pres.append(pre)
        outs.append(out)
        turned.append(turn)
        backs.append(back if k_at == 0 else swap(back, "exp", k_at))
        if k_at + 1 < sources:
            rows_in[k_at + 1] = after(rows_in[k_at + 1], back)
    bits = [1 << b for b in range(1, ring.bit_length() - 1)]
    orders = [bits, bits[::-1]]
    sides = [(seq_at // o[0]) % 2 for o in orders]
    subs = ring // 4
    masks = [
        sum((1 - (seq_at // bit) % 2) << (len(o) - 2 - at) for at, bit in enumerate(o[1:]))
        for o in orders
    ]
    chip = jnp.stack([core, *sides, *masks]).astype(jnp.int32)

    turned, backs[:-2] = lax.optimization_barrier((turned, backs[:-2]))
    blocks = expert_grad(chip, turned, grad_in, talls, pres, subs)
    given, kept = blocks[:2], blocks[2:]
    given, backs[-2] = lax.optimization_barrier((given, backs[-2]))
    given, backs[-1] = lax.optimization_barrier((given, backs[-1]))
    got = [swap(t, "seq", 1) for t in given]
    gr, gattn, gain_two_grad, bias_two_grad = lower(slot, resid, cot, norms, backs)
    got = after(got, gattn)
    goes = [add(kept[p][:width], got[p][:width]) for p in range(2)]
    stays = [[kept[p][width:], got[p][width:]] for p in range(2)]
    experts = Stream(expert_steps(list(zip(stays, goes)), orders))
    outs = after(outs, goes)
    returned = [outs[0]] + [swap(outs[k], "exp", k) for k in range(1, sources)]
    gattn_sib = swap(gattn, "seq", 1)
    unit = sources * 16
    sub = -(-(mine // LANES * width // subs) // unit) * unit
    gq, gk, gv = attend_back(
        meta, q, k, v, gattn, after(gattn_sib, goes), w_out, attn_tall, logs, low
    )
    pieces = dense_pieces(chip, a, gq, gk, gv, attn_all, gattn, gattn_sib, subs, sub)
    pieces, returned = lax.optimization_barrier((pieces, returned))
    dense = Stream(
        dense_steps([([pieces[0]], pieces[1]), ([pieces[2]], pieces[3])], orders)
    )
    (gq,) = meet([experts], (after(gq, pieces),))
    keep, give, halo, gain_one_grad, bias_one_grad = project_back(
        core_arg, x, sib, hal, has, gq, gk, gv, w_qkv
    )
    small = jnp.concatenate([gain_one_grad, bias_one_grad, gain_two_grad, bias_two_grad], axis=0)
    (give,) = meet([dense, experts], (give,))
    near = swap(give, "seq", 1)
    (near,) = meet([dense], (near,))
    for rest in range(len(bits) - 2):
        meet([dense, experts])
    far = add(halo, near[local_len:])
    hops = [("seq", bit) for bit in bits + [1]]
    hops += [("exp", 1 << b) for b in range(sources.bit_length() - 1)]
    small = Stream(small_steps(small, hops))
    layer_output = finish(slot, resid, returned)
    layer_output, far = meet([dense, experts, small], (layer_output, far))
    far = shift(far, "seq", -2)
    for rest in range(len(bits) - 2):
        meet([experts])
    own_parts = experts.result
    other_chip = across(own_parts, orders)
    other_core = beside(after(own_parts, layer_output))
    meet([dense, other_chip, other_core, small])
    other_both = beside(other_chip.result)
    hidden = down.shape[0]
    made = widen(core, sides, masks, own_parts, other_chip.result, (), hidden, subs)
    while dense.result is None:
        made = meet([dense, other_both, small], made)
    own_dense = dense.result
    dense_chip, dense_core = across(own_dense, orders), beside(own_dense)
    made = widen(
        1 - core, sides, masks, other_core.result, other_both.result, made, hidden, subs
    )
    grad_w_up, grad_w_down = meet([dense_chip, dense_core, small], made)
    dense_both = beside(dense_chip.result)
    meet([dense_both, small])
    while small.sent:
        small.go(small.sent)
    grad_w_qkv, grad_w_out = spread(
        chip, list(zip(own_dense, dense_chip.result)),
        list(zip(dense_core.result, dense_both.result)), width, mine, subs,
    )
    grad_input = close(x, gr, keep, near, after(far, grad_w_qkv), norms)
    small = small.result
    return (
        layer_output[None],
        grad_input[None],
        grad_w_qkv,
        grad_w_out,
        small[0],
        small[1],
        small[2],
        small[3],
        grad_w_up[None],
        grad_w_down[None],
    )


def solution(mesh):
    in_specs = (
        P("exp", "seq", None),
        P("exp", "seq"),
        P("exp", None),
        P(),
        P(),
        P(),
        P(),
        P(),
        P(),
        P(),
        P("exp", None, None),
        P("exp", None, None),
        P("exp", "seq", None),
    )
    out_specs = (
        P("exp", "seq", None),
        P("exp", "seq", None),
        P(),
        P(),
        P(),
        P(),
        P(),
        P(),
        P("exp", None, None),
        P("exp", None, None),
    )
    return jax.shard_map(
        on_device, mesh=mesh, in_specs=in_specs, out_specs=out_specs, check_vma=False
    )
```
